512 devices in a mesh: fine: 128 (over y, z, core), tele: 4 (over x).
Axes of the slice: x: 4, y: 4, z: 16, core: 2. Of those that a mesh axis runs over, the one named last changes fastest.
Arguments:
- right_side: float32 [8192, 320], P(('fine', 'tele')), may hold values from -6 to 6
- fine_inverse: bfloat16 [8192, 320, 320], P(('fine', 'tele')), may hold values from -0.08 to 0.45
- fine_links: int32 [8192, 6], P(('fine', 'tele')), may hold values from -1 to 8191, as said below
- fine_faces: int32 [8192, 6], P(('fine', 'tele')), may hold values from 0 to 23
- coarse_inverse: bfloat16 [1024, 320, 320], P(('fine', 'tele')), may hold values from -0.04 to 0.21
- coarse_links: int32 [1024, 6], P(('fine', 'tele')), may hold values from -1 to 1023, as said below
- coarse_faces: int32 [1024, 6], P(('fine', 'tele')), may hold values from 0 to 23
- face_operators: bfloat16 [24, 80, 80], replicated, may hold values from -1.25 to 1.25
- agglomerate: int32 [8192], P(('fine', 'tele')), may hold values from 0 to 1023, as said below
Outputs:
- solution: float32 [8192, 320], P(('fine', 'tele'))
The draws below stay inside these ranges and needn't reach their ends.
Inputs may be any that keep to these rules, and one draw needn't show every extreme that they name: `fine_links`: any entry other than -1 is an element held by the same device as the element, or by the device just before or after it in the order of fine+tele, cyclically. `coarse_links`: coarse elements form blocks of 8 consecutive ones; any entry other than -1 lies in the element's own block or in the block just before or after it, cyclically. `agglomerate`: fine element i maps into block i // 64 of 8 consecutive coarse elements; every coarse element collects exactly 8 fine elements.
All inputs are finite; a program needn't handle non-finite values.
Results may differ from the reference program's by a relative error of at most 0.02.
Values may be sent and summed in bfloat16 or wider, within the bound.
No kernel may reach another device: no remote copies, remote signals or barrier semaphores. Data moves between devices by JAX's collectives and lax.ppermute only.
A program may use at most 64 MiB of HBM per device.

```python
import math
import jax
import jax.numpy as jnp
from jax import lax

FIELDS = 5
NODES = 4
BLOCK_DOFS = 320
FACE_DOFS = 80
FACE_TYPES = 24
E_DEV = 16
AGGLOMERATE = 8
SWEEPS = 3
CYCLES = 2
COLUMN = 8
FINE_COLUMN = 64
ELEMENTS = 8192
COARSE = 1024


def inverse_blocks(key, row_count, low_diag, high_diag, off_scale):
    key_diag, key_off = jax.random.split(key)
    shape = (row_count, BLOCK_DOFS, BLOCK_DOFS)
    diagonal = jax.random.uniform(key_diag, (row_count, BLOCK_DOFS), jnp.float32, low_diag, high_diag)
    spread = jax.random.truncated_normal(key_off, -4.0, 4.0, shape, jnp.float32)
    identity = jnp.eye(BLOCK_DOFS, dtype=bool)
    scale = off_scale / jnp.sqrt(jnp.float32(BLOCK_DOFS))
    return jnp.where(identity[None], diagonal[:, :, None], spread * scale).astype(jnp.bfloat16)


def draw_fine_inverse(key, part):
    return inverse_blocks(key, ELEMENTS, 0.22, 0.44, 0.11)


def draw_coarse_inverse(key, part):
    return inverse_blocks(key, COARSE, 0.1, 0.2, 0.05)


def neighbour_lists(key, total, per_owner):
    owners = total // per_owner
    key_side, key_slot, key_edge = jax.random.split(key, 3)
    shift_by = jax.random.randint(key_side, (total, 6), -1, 2)
    slot_index = jax.random.randint(key_slot, (total, 6), 0, per_owner)
    boundary = jax.random.randint(key_edge, (total, 6), 0, 8) == 0
    owner = (jnp.arange(total, dtype=jnp.int32) // per_owner)[:, None]
    target = (owner + shift_by) % owners * per_owner + slot_index
    links = jnp.where(boundary, -1, target).astype(jnp.int32)
    return links.at[0, 0].set(total - 1).at[0, 1].set(-1)


def draw_fine_links(key, part):
    return neighbour_lists(key, ELEMENTS, E_DEV)


def draw_coarse_links(key, part):
    return neighbour_lists(key, COARSE, COLUMN)


def draw_agglomerate(key, part):
    columns = ELEMENTS // FINE_COLUMN
    scores = jax.random.randint(key, (columns, FINE_COLUMN), 0, 1048576) * FINE_COLUMN + jnp.arange(FINE_COLUMN, dtype=jnp.int32)[None, :]
    order = jnp.argsort(scores, axis=1)
    base = jnp.arange(FINE_COLUMN, dtype=jnp.int32) // AGGLOMERATE
    local_target = base[order]
    return (local_target + jnp.arange(columns, dtype=jnp.int32)[:, None] * COLUMN).reshape(-1).astype(jnp.int32)


def place_ends(result, key, smallest, largest):
    dims = result.shape
    spot = [jax.random.randint(jax.random.fold_in(key, axis), (), 0, dims[axis]) for axis in range(len(dims))]
    result = result.at[tuple(spot)].set(smallest)
    longest = dims.index(max(dims))
    spot[longest] = (spot[longest] + 1) % dims[longest]
    return result.at[tuple(spot)].set(largest)


def steps_of(stream_key, extent, shards, smallest, high):
    loudness, own = 1.0, jax.random.fold_in(stream_key, 6)
    for position, blocks in shards:
        steps = jnp.exp(jax.random.uniform(jax.random.fold_in(own, position), (blocks,), jnp.float32, smallest / len(shards), high / len(shards)))
        loudness = loudness * jnp.repeat(steps, extent[position] // blocks).reshape([-1 if axis == position else 1 for axis in range(len(extent))])
    return loudness


def centred(rng, dims, scale, bound, cuts=(), kind=jnp.bfloat16):
    drawn = scale * jax.random.normal(rng, dims, jnp.float32)
    if cuts:
        drawn = drawn * steps_of(rng, dims, cuts, -0.22, 0.18)
    return jnp.clip(drawn, -bound, bound).astype(kind)


def setup_inputs(seed: int = 0) -> dict:
    streams_of = jax.random.split(jax.random.key(seed), 10)
    right_side = centred(streams_of[0], (ELEMENTS, BLOCK_DOFS), 1.0, 6.0, ((0, 512),), jnp.float32)
    fine_inverse = draw_fine_inverse(jax.random.fold_in(streams_of[9], 71), 0)
    fine_links = draw_fine_links(jax.random.fold_in(streams_of[9], 71), 0)
    fine_faces = place_ends(jax.random.randint(streams_of[3], (ELEMENTS, 6), 0, FACE_TYPES), jax.random.fold_in(streams_of[3], 1), 0, FACE_TYPES - 1).astype(jnp.int32)
    coarse_inverse = draw_coarse_inverse(jax.random.fold_in(streams_of[9], 71), 0)
    coarse_links = draw_coarse_links(jax.random.fold_in(streams_of[9], 71), 0)
    coarse_faces = place_ends(jax.random.randint(streams_of[6], (COARSE, 6), 0, FACE_TYPES), jax.random.fold_in(streams_of[6], 1), 0, FACE_TYPES - 1).astype(jnp.int32)
    face_operators = centred(streams_of[7], (FACE_TYPES, FACE_DOFS, FACE_DOFS), (FACE_DOFS // 4) ** -0.5, 1.25)
    agglomerate = draw_agglomerate(jax.random.fold_in(streams_of[9], 71), 0)
    return dict(right_side=right_side, fine_inverse=fine_inverse, fine_links=fine_links, fine_faces=fine_faces, coarse_inverse=coarse_inverse, coarse_links=coarse_links, coarse_faces=coarse_faces, face_operators=face_operators, agglomerate=agglomerate)


OPPOSITE = (1, 0, 3, 2, 5, 4)


def take_traces(field_state):
    row_count = field_state.shape[0]
    node_cube = field_state.reshape(row_count, FIELDS, NODES, NODES, NODES)
    far_node = NODES - 1
    faces_list = (node_cube[:, :, 0], node_cube[:, :, far_node], node_cube[:, :, :, 0], node_cube[:, :, :, far_node], node_cube[:, :, :, :, 0], node_cube[:, :, :, :, far_node])
    return jnp.stack([face_slab.reshape(row_count, -1) for face_slab in faces_list], axis=1).astype(jnp.bfloat16)


def lift_faces(coupled):
    row_count = coupled.shape[0]
    pieces = coupled.reshape(row_count, 6, FIELDS, NODES, NODES)
    far_node = NODES - 1
    node_cube = jnp.zeros((row_count, FIELDS, NODES, NODES, NODES), jnp.float32)
    node_cube = node_cube.at[:, :, 0].add(pieces[:, 0])
    node_cube = node_cube.at[:, :, far_node].add(pieces[:, 1])
    node_cube = node_cube.at[:, :, :, 0].add(pieces[:, 2])
    node_cube = node_cube.at[:, :, :, far_node].add(pieces[:, 3])
    node_cube = node_cube.at[:, :, :, :, 0].add(pieces[:, 4])
    node_cube = node_cube.at[:, :, :, :, far_node].add(pieces[:, 5])
    return node_cube.reshape(row_count, -1)


def blockwise(function, arrays):
    row_count = arrays[0].shape[0]
    block_size = math.gcd(row_count, 512)
    shaped = tuple(item.reshape((row_count // block_size, block_size) + item.shape[1:]) for item in arrays)

    def apply_block(pieces):
        return function(*pieces)

    output = lax.map(apply_block, shaped)
    return output.reshape((row_count,) + output.shape[2:])


def inverse_block(inverse, vector):
    return jnp.einsum("nij,nj->ni", inverse.astype(jnp.float32), vector.astype(jnp.float32), precision=lax.Precision.HIGHEST)


def apply_inverse(inverse, vector):
    return blockwise(inverse_block, (inverse, vector))


def coupling(field_state, links, faces, face_operators):
    own_traces = take_traces(field_state)
    flat_rows = own_traces.reshape(-1, own_traces.shape[2])
    opposite = jnp.array(OPPOSITE, jnp.int32)
    row_index = jnp.maximum(links, 0) * 6 + opposite[None, :]
    face_rows = jnp.take(flat_rows, row_index.reshape(-1), axis=0).reshape(links.shape[0], 6, -1)
    face_rows = jnp.where((links >= 0)[:, :, None], face_rows, jnp.zeros_like(face_rows))

    def face_block(rows_block, kinds_block):
        chosen = jnp.take(face_operators, kinds_block.reshape(-1), axis=0).astype(jnp.float32)
        flat_block = rows_block.reshape(-1, rows_block.shape[2]).astype(jnp.float32)
        return jnp.einsum("rjk,rk->rj", chosen, flat_block, precision=lax.Precision.HIGHEST).reshape(rows_block.shape)

    coupled = blockwise(face_block, (face_rows, faces))
    return lift_faces(coupled.astype(jnp.float32))


def reference(right_side, fine_inverse, fine_links, fine_faces, coarse_inverse, coarse_links, coarse_faces, face_operators, agglomerate):
    solution = jnp.zeros(right_side.shape, jnp.float32)
    for cycle_index in range(CYCLES):
        for sweep_index in range(SWEEPS):
            if cycle_index == 0 and sweep_index == 0:
                coupled = jnp.zeros(right_side.shape, jnp.float32)
            else:
                coupled = coupling(solution, fine_links, fine_faces, face_operators)
            lowered = (right_side - coupled).astype(jnp.bfloat16)
            solution = apply_inverse(fine_inverse, lowered)
        residual = lowered.astype(jnp.float32) - coupling(solution, fine_links, fine_faces, face_operators)
        restricted = jax.ops.segment_sum(residual, agglomerate, num_segments=COARSE)
        coarse_state = apply_inverse(coarse_inverse, restricted.astype(jnp.bfloat16))
        for sweep_index in range(SWEEPS - 1):
            coupled_coarse = coupling(coarse_state, coarse_links, coarse_faces, face_operators)
            coarse_state = apply_inverse(coarse_inverse, (restricted - coupled_coarse).astype(jnp.bfloat16))
        solution = solution + jnp.take(coarse_state, agglomerate, axis=0)
    return solution
```

```python
import functools

import jax
import jax.numpy as jnp
import numpy as np
from jax import lax
from jax.experimental import pallas as pl
from jax.experimental.pallas import tpu as pltpu
from jax.sharding import PartitionSpec as P

FIELDS = 5
NODES = 4
SWEEPS = 3
CYCLES = 2
LANES = 128
OPPOSITE = (1, 0, 3, 2, 5, 4)


def passed_along(block, axis, distance):
    devices = range(lax.axis_size(axis))
    route = [((i - distance) % len(devices), i) for i in devices]
    return lax.ppermute(block, axis, route)


def face_tables():
    cube = np.arange(FIELDS * NODES**3).reshape(FIELDS, NODES, NODES, NODES)
    far = NODES - 1
    faces = (cube[:, 0], cube[:, far], cube[:, :, 0], cube[:, :, far], cube[..., 0], cube[..., far])
    table = np.zeros((cube.size, 6 * LANES), np.float32)
    for k, face in enumerate(faces):
        nodes = face.reshape(-1)
        table[nodes, k * LANES + np.arange(nodes.size)] = 1.0
    return table


def halves(value):
    high = value.astype(jnp.bfloat16)
    low = (value - high.astype(jnp.float32)).astype(jnp.bfloat16)
    return high, low


def exact_dot(left, right):
    high, low = halves(right)
    return jnp.dot(left, high, preferred_element_type=jnp.float32) + jnp.dot(
        left, low, preferred_element_type=jnp.float32
    )


def coupling(states, rows, kinds, operators, pick, lift):
    count = states[0].shape[0]
    pool = jnp.concatenate([state.astype(jnp.float32) for state in states], axis=0).astype(jnp.bfloat16)
    traces = jnp.dot(pool, pick, preferred_element_type=jnp.float32).astype(jnp.bfloat16)
    chosen = rows == lax.broadcasted_iota(jnp.int32, (6 * count, pool.shape[0]), 1)
    chosen = jnp.where(chosen, 1.0, 0.0)
    face_rows = jnp.concatenate(
        [
            jnp.dot(
                chosen[k * count : (k + 1) * count].astype(jnp.bfloat16),
                traces[:, OPPOSITE[k] * LANES : (OPPOSITE[k] + 1) * LANES],
                preferred_element_type=jnp.float32,
            )
            for k in range(6)
        ],
        axis=0,
    )
    types = operators.shape[0] // LANES
    kinds = jnp.broadcast_to(kinds, face_rows.shape)
    spread = jnp.concatenate(
        [jnp.where(kinds == q, face_rows, 0.0).astype(jnp.bfloat16) for q in range(types)], axis=1
    )
    coupled = jnp.dot(spread, operators, preferred_element_type=jnp.float32)
    side_by_side = jnp.concatenate([coupled[k * count : (k + 1) * count] for k in range(6)], axis=1)
    high, low = halves(side_by_side)
    return jnp.dot(high, lift, preferred_element_type=jnp.float32) + jnp.dot(
        low, lift, preferred_element_type=jnp.float32
    )


def apply_inverse(inverse_ref, vector):
    count = vector.shape[0]
    row = lax.broadcasted_iota(jnp.int32, vector.shape, 0)
    result = jnp.zeros(vector.shape, jnp.float32)
    for e in range(count):
        product = lax.dot_general(
            vector, inverse_ref[e], (((1,), (1,)), ((), ())), preferred_element_type=jnp.float32
        )
        result = jnp.where(row == e, product, result)
    return result


def first_kernel(right_ref, inverse_ref, state_ref):
    lowered = right_ref[...].astype(jnp.bfloat16)
    state_ref[...] = apply_inverse(inverse_ref, lowered).astype(jnp.bfloat16)


def sweep_kernel(
    prev_ref, own_ref, next_ref, index_ref, operators_ref, pick_ref, lift_ref, right_ref, inverse_ref, *outs
):
    states = [prev_ref[...], own_ref[...], next_ref[...]]
    index = index_ref[...]
    coupled = coupling(
        states, index[:, 0:1], index[:, 1:2], operators_ref[...], pick_ref[...], lift_ref[...]
    )
    lowered = (right_ref[...] - coupled).astype(jnp.bfloat16)
    result = apply_inverse(inverse_ref, lowered)
    outs[0][...] = result.astype(jnp.bfloat16)
    if len(outs) > 1:
        outs[1][...] = result
        outs[2][...] = lowered


def restrict_kernel(
    prev_ref, own_ref, next_ref, index_ref, operators_ref, pick_ref, lift_ref, lowered_ref, target_ref, out_ref
):
    states = [prev_ref[...], own_ref[...], next_ref[...]]
    index = index_ref[...]
    coupled = coupling(
        states, index[:, 0:1], index[:, 1:2], operators_ref[...], pick_ref[...], lift_ref[...]
    )
    residual = lowered_ref[...].astype(jnp.float32) - coupled
    rows = out_ref.shape[1]
    member = target_ref[...] == lax.broadcasted_iota(jnp.int32, (rows, residual.shape[0]), 0)
    partial = exact_dot(jnp.where(member, 1.0, 0.0).astype(jnp.bfloat16), residual)
    for t in range(out_ref.shape[0]):
        out_ref[t] = partial


def coarse_first_kernel(parts_ref, inverse_ref, restricted_ref, state_ref):
    restricted = parts_ref[0]
    for t in range(1, parts_ref.shape[0]):
        restricted = restricted + parts_ref[t]
    restricted_ref[...] = restricted
    state_ref[...] = apply_inverse(inverse_ref, restricted.astype(jnp.bfloat16)).astype(jnp.bfloat16)


def correct_kernel(
    prev_ref,
    own_ref,
    next_ref,
    index_ref,
    operators_ref,
    pick_ref,
    lift_ref,
    right_ref,
    inverse_ref,
    target_ref,
    solution_ref,
    out_ref,
):
    states = [prev_ref[...], own_ref[...], next_ref[...]]
    index = index_ref[...]
    coupled = coupling(
        states, index[:, 0:1], index[:, 1:2], operators_ref[...], pick_ref[...], lift_ref[...]
    )
    coarse = apply_inverse(inverse_ref, (right_ref[...] - coupled).astype(jnp.bfloat16))
    rows, fine = coarse.shape[0], solution_ref.shape[0]
    member = target_ref[...] == lax.broadcasted_iota(jnp.int32, (fine, rows), 1)
    added = exact_dot(jnp.where(member, 1.0, 0.0).astype(jnp.bfloat16), coarse)
    out_ref[...] = (solution_ref[...] + added).astype(out_ref.dtype)


def run(kernel, outs, *operands, flops=1 << 28):
    single = not isinstance(outs, list)
    shapes = [outs] if single else outs
    vmem = pl.BlockSpec(memory_space=pltpu.VMEM)
    moved = sum(o.size * o.dtype.itemsize for o in operands)
    result = pl.pallas_call(
        kernel,
        out_shape=[jax.ShapeDtypeStruct(s, d) for s, d in shapes],
        in_specs=[vmem] * len(operands),
        out_specs=[vmem] * len(shapes),
        compiler_params=pltpu.CompilerParams(vmem_limit_bytes=20 << 20),
        cost_estimate=pl.CostEstimate(flops=flops, bytes_accessed=moved, transcendentals=0),
    )(*operands)
    return result[0] if single else result


def face_index(links, faces, position, devices):
    count = links.shape[0]
    clamped = jnp.maximum(links, 0)
    relative = (clamped // count - position + 1) % devices
    rows = jnp.where(links >= 0, relative * count + clamped % count, -1)
    return jnp.stack([rows.T.reshape(-1), faces.T.reshape(-1)], axis=1)


def shards(
    right_side,
    fine_inverse,
    fine_links,
    fine_faces,
    coarse_inverse,
    coarse_links,
    coarse_faces,
    face_operators,
    agglomerate,
):
    f32, bf16 = jnp.float32, jnp.bfloat16
    fine_rows, dofs = right_side.shape
    tele_size = lax.axis_size("tele")
    tele = lax.axis_index("tele")
    column = lax.axis_index("fine")
    columns = lax.axis_size("fine")
    coarse_rows = coarse_inverse.shape[0] * tele_size

    state = run(first_kernel, ((fine_rows, dofs), bf16), right_side, fine_inverse)

    table = face_tables()
    pick = jnp.asarray(table, bf16)
    lift = jnp.asarray(table.T.copy(), bf16)
    types, face_dofs, _ = face_operators.shape
    pad = LANES - face_dofs
    operators = jnp.pad(face_operators.transpose(0, 2, 1), ((0, 0), (0, pad), (0, pad)))
    operators = operators.reshape(types * LANES, LANES)
    fine_index = face_index(fine_links, fine_faces, column * tele_size + tele, columns * tele_size)
    block_inverse = lax.all_gather(coarse_inverse, "tele", axis=0, tiled=True)
    lists = lax.all_gather(
        jnp.concatenate([coarse_links, coarse_faces], axis=1), "tele", axis=0, tiled=True
    )
    coarse_index = face_index(lists[:, :6], lists[:, 6:], column, columns)
    target = agglomerate % coarse_rows
    target_row, target_column = target[None, :], target[:, None]
    shared = (operators, pick, lift)

    def fine_halo(block):
        axes = ("fine", "tele")
        return passed_along(block, axes, 1), block, passed_along(block, axes, -1)

    def coarse_halo(block):
        return passed_along(block, "fine", 1), block, passed_along(block, "fine", -1)

    for cycle in range(CYCLES):
        for sweep in range(SWEEPS):
            if cycle == 0 and sweep == 0:
                continue
            outs = [((fine_rows, dofs), bf16)]
            if sweep == SWEEPS - 1:
                outs += [((fine_rows, dofs), f32), ((fine_rows, dofs), bf16)]
            result = run(
                sweep_kernel, outs, *fine_halo(state), fine_index, *shared, right_side, fine_inverse
            )
            state = result[0]
        solution, lowered = result[1], result[2]
        parts = run(
            restrict_kernel,
            ((tele_size, coarse_rows, dofs), f32),
            *fine_halo(state),
            fine_index,
            *shared,
            lowered,
            target_row,
        )
        parts = lax.all_to_all(parts, "tele", 0, 0, tiled=True)
        restricted, coarse = run(
            coarse_first_kernel,
            [((coarse_rows, dofs), f32), ((coarse_rows, dofs), bf16)],
            parts,
            block_inverse,
        )
        for sweep in range(SWEEPS - 2):
            coarse = run(
                sweep_kernel,
                [((coarse_rows, dofs), bf16)],
                *coarse_halo(coarse),
                coarse_index,
                *shared,
                restricted,
                block_inverse,
            )[0]
        last = cycle == CYCLES - 1
        state = run(
            correct_kernel,
            ((fine_rows, dofs), f32 if last else bf16),
            *coarse_halo(coarse),
            coarse_index,
            *shared,
            restricted,
            block_inverse,
            target_column,
            solution,
        )
    return state


def solution(mesh):
    both = P(("fine", "tele"))
    return jax.shard_map(
        shards,
        mesh=mesh,
        in_specs=(both, both, both, both, both, both, both, P(), both),
        out_specs=both,
        check_vma=False,
    )
```

```python
import jax
import jax.numpy as jnp
import numpy as np
from jax import lax
from jax.experimental import pallas as pl
from jax.experimental.pallas import tpu as pltpu
from jax.sharding import PartitionSpec as P

FIELDS = 5
NODES = 4
SWEEPS = 3
CYCLES = 2
LANES = 128
OPPOSITE = (1, 0, 3, 2, 5, 4)


def swapped(block, axis):
    count = lax.axis_size(axis)
    outer = lax.ppermute(block, axis, [(i, (i - 1 if i % 2 == 0 else i + 1) % count) for i in range(count)])
    inner = lax.ppermute(block, axis, [(i, i ^ 1) for i in range(count)])
    return inner, outer


def face_table():
    cube = np.arange(FIELDS * NODES**3).reshape(FIELDS, NODES, NODES, NODES)
    far = NODES - 1
    faces = (cube[:, 0], cube[:, far], cube[:, :, 0], cube[:, :, far], cube[..., 0], cube[..., far])
    table = np.zeros((6 * LANES, cube.size), np.float32)
    for k, face in enumerate(faces):
        nodes = face.reshape(-1)
        table[k * LANES + np.arange(nodes.size), nodes] = 1.0
    return table


def halves(value):
    high = value.astype(jnp.bfloat16)
    low = (value - high.astype(jnp.float32)).astype(jnp.bfloat16)
    return high, low


def exact_dot(left, right):
    high, low = halves(right)
    return jnp.dot(left, high, preferred_element_type=jnp.float32) + jnp.dot(
        left, low, preferred_element_type=jnp.float32
    )


def coupling(states, index, operators, lift):
    count = states[0].shape[0]
    pool = jnp.concatenate([state.astype(jnp.float32) for state in states], axis=0).astype(jnp.bfloat16)
    traces = lax.dot_general(pool, lift, (((1,), (1,)), ((), ())), preferred_element_type=jnp.float32)
    traces = traces.astype(jnp.bfloat16)
    column = lax.broadcasted_iota(jnp.int32, (count, pool.shape[0]), 1)
    face_rows, kinds = [], []
    for k in range(6):
        chosen = jnp.where(index[:, k : k + 1] == column, 1.0, 0.0).astype(jnp.bfloat16)
        across = traces[:, OPPOSITE[k] * LANES : (OPPOSITE[k] + 1) * LANES]
        face_rows.append(jnp.dot(chosen, across, preferred_element_type=jnp.float32))
        kinds.append(jnp.broadcast_to(index[:, 6 + k : 7 + k], (count, LANES)))
    face_rows = jnp.concatenate(face_rows, axis=0)
    kinds = jnp.concatenate(kinds, axis=0)
    types = operators.shape[0] // LANES
    spread = jnp.concatenate(
        [jnp.where(kinds == q, face_rows, 0.0).astype(jnp.bfloat16) for q in range(types)], axis=1
    )
    coupled = jnp.dot(spread, operators, preferred_element_type=jnp.float32)
    side_by_side = jnp.concatenate([coupled[k * count : (k + 1) * count] for k in range(6)], axis=1)
    high, low = halves(side_by_side)
    return jnp.dot(high, lift, preferred_element_type=jnp.float32) + jnp.dot(
        low, lift, preferred_element_type=jnp.float32
    )


def apply_inverse(inverse_ref, vector):
    count, dofs = vector.shape
    row = lax.broadcasted_iota(jnp.int32, vector.shape, 0)
    result = jnp.zeros(vector.shape, jnp.float32)
    for e in range(count):
        product = lax.dot_general(
            vector, inverse_ref[e][:, :dofs], (((1,), (1,)), ((), ())), preferred_element_type=jnp.float32
        )
        result = jnp.where(row == e, product, result)
    return result


def first_kernel(right_ref, inverse_ref, state_ref):
    lowered = right_ref[...].astype(jnp.bfloat16)
    state_ref[...] = apply_inverse(inverse_ref, lowered).astype(jnp.bfloat16)


def sweep_kernel(
    prev_ref, own_ref, next_ref, index_ref, operators_ref, lift_ref, right_ref, inverse_ref, *outs
):
    states = [prev_ref[...], own_ref[...], next_ref[...]]
    coupled = coupling(states, index_ref[...], operators_ref[...], lift_ref[...])
    lowered = (right_ref[...] - coupled).astype(jnp.bfloat16)
    result = apply_inverse(inverse_ref, lowered)
    outs[0][...] = result.astype(jnp.bfloat16)
    if len(outs) > 1:
        outs[1][...] = result
        outs[2][...] = lowered


def restrict_kernel(
    prev_ref, own_ref, next_ref, index_ref, operators_ref, lift_ref, lowered_ref, target_ref, *rest
):
    out_ref = rest[-1] if len(rest) == 1 else rest[1]
    states = [prev_ref[...], own_ref[...], next_ref[...]]
    coupled = coupling(states, index_ref[...], operators_ref[...], lift_ref[...])
    residual = lowered_ref[...].astype(jnp.float32) - coupled
    rows = out_ref.shape[1]
    member = target_ref[...] == lax.broadcasted_iota(jnp.int32, (rows, residual.shape[0]), 0)
    partial = exact_dot(jnp.where(member, 1.0, 0.0).astype(jnp.bfloat16), residual)
    for t in range(out_ref.shape[0]):
        out_ref[t] = partial
    if len(rest) > 1:
        packed_ref, _, list_ref = rest
        dofs = residual.shape[1]
        for c in range(rows):
            list_ref[c : c + 1] = packed_ref[c, 0:1, dofs:].astype(jnp.int32)


def coarse_first_kernel(parts_ref, inverse_ref, restricted_ref, state_ref):
    restricted = parts_ref[0]
    for t in range(1, parts_ref.shape[0]):
        restricted = restricted + parts_ref[t]
    restricted_ref[...] = restricted
    state_ref[...] = apply_inverse(inverse_ref, restricted.astype(jnp.bfloat16)).astype(jnp.bfloat16)


def correct_kernel(
    prev_ref,
    own_ref,
    next_ref,
    index_ref,
    operators_ref,
    lift_ref,
    right_ref,
    inverse_ref,
    target_ref,
    solution_ref,
    out_ref,
):
    states = [prev_ref[...], own_ref[...], next_ref[...]]
    coupled = coupling(states, index_ref[...], operators_ref[...], lift_ref[...])
    coarse = apply_inverse(inverse_ref, (right_ref[...] - coupled).astype(jnp.bfloat16))
    rows, fine = coarse.shape[0], solution_ref.shape[0]
    member = target_ref[...] == lax.broadcasted_iota(jnp.int32, (rows, fine), 0)
    added = exact_dot(jnp.where(member, 1.0, 0.0).T.astype(jnp.bfloat16), coarse)
    out_ref[...] = (solution_ref[...] + added).astype(out_ref.dtype)


def run(kernel, outs, *operands, held=(), keep=()):
    count = len(operands)

    def body(*refs):
        kernel(*refs[:count], *refs[count + len(keep) :])

    single = not isinstance(outs, list)
    shapes = [outs] if single else outs
    vmem = pl.BlockSpec(memory_space=pltpu.VMEM)
    moved = sum(o.size * o.dtype.itemsize for o in operands)
    operands = [
        pltpu.with_memory_space_constraint(o, pltpu.VMEM) if i in held else o for i, o in enumerate(operands)
    ]
    operands += [pltpu.with_memory_space_constraint(o, pltpu.VMEM) for o in keep]
    result = pl.pallas_call(
        body,
        out_shape=[jax.ShapeDtypeStruct(s, d) for s, d in shapes],
        in_specs=[vmem] * len(operands),
        out_specs=[vmem] * len(shapes),
        compiler_params=pltpu.CompilerParams(vmem_limit_bytes=20 << 20),
        cost_estimate=pl.CostEstimate(flops=1 << 28, bytes_accessed=moved, transcendentals=0),
    )(*operands)
    return result[0] if single else result


def local_rows(links, count, position):
    owner, within = links // count, links % count
    place = jnp.where(owner == position, 1, jnp.where(owner == position ^ 1, 0, 2))
    return jnp.where(links >= 0, place * count + within, -1)


def shards(
    right_side,
    fine_inverse,
    fine_links,
    fine_faces,
    coarse_inverse,
    coarse_links,
    coarse_faces,
    face_operators,
    agglomerate,
):
    f32, bf16 = jnp.float32, jnp.bfloat16
    fine_rows, dofs = right_side.shape
    tele_size = lax.axis_size("tele")
    tele = lax.axis_index("tele")
    column = lax.axis_index("fine")
    coarse_own = coarse_inverse.shape[0]
    coarse_rows = coarse_own * tele_size

    lift = jnp.asarray(face_table(), bf16)
    types, face_dofs, _ = face_operators.shape
    pad = LANES - face_dofs
    operators = jnp.pad(face_operators.transpose(0, 2, 1), ((0, 0), (0, pad), (0, pad)))
    operators = operators.reshape(types * LANES, LANES)
    fine_index = jnp.concatenate([local_rows(fine_links, fine_rows, column * tele_size + tele), fine_faces], axis=1)
    target = agglomerate % coarse_rows
    target = target[None, :]

    lists = jnp.concatenate([local_rows(coarse_links, coarse_rows, column), coarse_faces], axis=1).astype(bf16)
    lists = jnp.pad(lists[:, None, :], ((0, 0), (0, dofs - 1), (0, -dofs % LANES - lists.shape[1])))
    packed = jnp.concatenate([coarse_inverse, lists], axis=2)
    packed = jnp.broadcast_to(packed[None], (tele_size,) + packed.shape)
    right_side, operators, fine_index, target, packed = lax.optimization_barrier(
        (right_side, operators, fine_index, target, packed)
    )
    packed = lax.all_to_all(packed, "tele", 0, 0, tiled=True)
    block_inverse = packed.reshape((coarse_rows,) + packed.shape[2:])
    shared = (operators, lift)
    inverse = fine_inverse
    state = run(first_kernel, ((fine_rows, dofs), bf16), right_side, inverse, held=(1,))

    def halo(block, axis):
        inner, outer = swapped(block, axis)
        return inner, block, outer

    both = ("fine", "tele")
    for cycle in range(CYCLES):
        keep = (inverse,) if cycle < CYCLES - 1 else ()
        for sweep in range(SWEEPS):
            if cycle == 0 and sweep == 0:
                continue
            outs = [((fine_rows, dofs), bf16)]
            if sweep == SWEEPS - 1:
                outs += [((fine_rows, dofs), f32), ((fine_rows, dofs), bf16)]
            result = run(
                sweep_kernel, outs, *halo(state, both), fine_index, *shared, right_side, inverse, held=(5, 7)
            )
            state = result[0]
        solution, lowered = result[1], result[2]
        operands = (*halo(state, both), fine_index, *shared, lowered, target)
        part_shape = ((tele_size, coarse_rows, dofs), f32)
        if cycle == 0:
            lists_shape = ((coarse_rows, block_inverse.shape[2] - dofs), jnp.int32)
            parts, coarse_index = run(
                restrict_kernel, [part_shape, lists_shape], *operands, block_inverse, held=(5, 8), keep=keep
            )
        else:
            parts = run(restrict_kernel, part_shape, *operands, held=(5,), keep=keep)
        parts = lax.all_to_all(parts, "tele", 0, 0, tiled=True)
        restricted, coarse = run(
            coarse_first_kernel,
            [((coarse_rows, dofs), f32), ((coarse_rows, dofs), bf16)],
            parts,
            block_inverse,
            held=(1,),
            keep=keep,
        )
        for sweep in range(SWEEPS - 2):
            coarse = run(
                sweep_kernel,
                [((coarse_rows, dofs), bf16)],
                *halo(coarse, "fine"),
                coarse_index,
                *shared,
                restricted,
                block_inverse,
                held=(5, 7),
                keep=keep,
            )[0]
        last = cycle == CYCLES - 1
        state = run(
            correct_kernel,
            ((fine_rows, dofs), f32 if last else bf16),
            *halo(coarse, "fine"),
            coarse_index,
            *shared,
            restricted,
            block_inverse,
            target,
            solution,
            held=(5, 7),
            keep=keep,
        )
    return state


def solution(mesh):
    both = P(("fine", "tele"))
    return jax.shard_map(
        shards,
        mesh=mesh,
        in_specs=(both, both, both, both, both, both, both, P(), both),
        out_specs=both,
        check_vma=False,
    )
```

```python
import jax
import jax.numpy as jnp
import numpy as np
from jax import lax
from jax.experimental import pallas as pl
from jax.experimental.pallas import tpu as pltpu
from jax.sharding import PartitionSpec as P

FIELDS = 5
NODES = 4
SWEEPS = 3
CYCLES = 2
LANES = 128
OPPOSITE = (1, 0, 3, 2, 5, 4)


def swapped(block, axis):
    count = lax.axis_size(axis)
    outer = lax.ppermute(block, axis, [(i, (i - 1 if i % 2 == 0 else i + 1) % count) for i in range(count)])
    inner = lax.ppermute(block, axis, [(i, i ^ 1) for i in range(count)])
    return inner, outer


def face_table():
    cube = np.arange(FIELDS * NODES**3).reshape(FIELDS, NODES, NODES, NODES)
    far = NODES - 1
    faces = (cube[:, 0], cube[:, far], cube[:, :, 0], cube[:, :, far], cube[..., 0], cube[..., far])
    table = np.zeros((6 * LANES, cube.size), np.float32)
    for k, face in enumerate(faces):
        nodes = face.reshape(-1)
        table[k * LANES + np.arange(nodes.size), nodes] = 1.0
    return table


def halves(value):
    high = value.astype(jnp.bfloat16)
    low = (value - high.astype(jnp.float32)).astype(jnp.bfloat16)
    return high, low


def exact_dot(left, right):
    high, low = halves(right)
    return jnp.dot(left, high, preferred_element_type=jnp.float32) + jnp.dot(
        left, low, preferred_element_type=jnp.float32
    )


def coupling(states, index, operators, lift):
    count = states[0].shape[0]
    pool = jnp.concatenate([state.astype(jnp.float32) for state in states], axis=0).astype(jnp.bfloat16)
    traces = lax.dot_general(pool, lift, (((1,), (1,)), ((), ())), preferred_element_type=jnp.float32)
    traces = traces.astype(jnp.bfloat16)
    column = lax.broadcasted_iota(jnp.int32, (count, pool.shape[0]), 1)
    face_rows, kinds = [], []
    for k in range(6):
        chosen = jnp.where(index[:, k : k + 1] == column, 1.0, 0.0).astype(jnp.bfloat16)
        across = traces[:, OPPOSITE[k] * LANES : (OPPOSITE[k] + 1) * LANES]
        face_rows.append(jnp.dot(chosen, across, preferred_element_type=jnp.float32))
        kinds.append(jnp.broadcast_to(index[:, 6 + k : 7 + k], (count, LANES)))
    face_rows = jnp.concatenate(face_rows, axis=0)
    kinds = jnp.concatenate(kinds, axis=0)
    types = operators.shape[0] // LANES
    spread = jnp.concatenate(
        [jnp.where(kinds == q, face_rows, 0.0).astype(jnp.bfloat16) for q in range(types)], axis=1
    )
    coupled = jnp.dot(spread, operators, preferred_element_type=jnp.float32)
    side_by_side = jnp.concatenate([coupled[k * count : (k + 1) * count] for k in range(6)], axis=1)
    high, low = halves(side_by_side)
    return jnp.dot(high, lift, preferred_element_type=jnp.float32) + jnp.dot(
        low, lift, preferred_element_type=jnp.float32
    )


def apply_inverse(inverse_ref, vector):
    count = vector.shape[0]
    row = lax.broadcasted_iota(jnp.int32, vector.shape, 0)
    result = jnp.zeros(vector.shape, jnp.float32)
    for e in range(count):
        product = lax.dot_general(
            vector, inverse_ref[e], (((1,), (1,)), ((), ())), preferred_element_type=jnp.float32
        )
        result = jnp.where(row == e, product, result)
    return result


def pool_rows(links, count, position):
    shift = count.bit_length() - 1
    owner, within = links >> shift, links & (count - 1)
    place = jnp.where(owner == position, 1, jnp.where(owner == (position ^ 1), 0, 2))
    return jnp.where(links >= 0, place * count + within, -1)


def first_kernel(
    right_ref,
    inverse_ref,
    faces_ref,
    links_ref,
    coarse_links_ref,
    coarse_faces_ref,
    operators_in_ref,
    state_ref,
    index_ref,
    lists_ref,
    operators_ref,
):
    tele, column = lax.axis_index("tele"), lax.axis_index("fine")
    tele_size = lax.axis_size("tele")
    lowered = right_ref[...].astype(jnp.bfloat16)
    state_ref[...] = apply_inverse(inverse_ref, lowered).astype(jnp.bfloat16)

    fine_rows = right_ref.shape[0]
    rows = pool_rows(links_ref[...], fine_rows, column * tele_size + tele)
    index = jnp.concatenate([rows.astype(jnp.float32), faces_ref[...].astype(jnp.float32)], axis=0)
    index_ref[...] = index.T.astype(jnp.int32)

    own = coarse_links_ref.shape[0]
    count = own * tele_size
    rows = pool_rows(coarse_links_ref[...], count, column).astype(jnp.float32)
    kinds = coarse_faces_ref[...].astype(jnp.float32)
    lists_ref[...] = jnp.zeros(lists_ref.shape, jnp.float32)
    row = lax.broadcasted_iota(jnp.int32, (count, rows.shape[1]), 0)
    for part, values in enumerate((rows, kinds)):
        placed = jnp.zeros(row.shape, jnp.float32)
        for c in range(own):
            placed = jnp.where(row == own * tele + c, values[c : c + 1], placed)
        lists_ref[:, part * 6 : part * 6 + 6] = placed

    types, size, _ = operators_in_ref.shape
    unit = lax.broadcasted_iota(jnp.int32, (LANES, size), 0) == lax.broadcasted_iota(jnp.int32, (LANES, size), 1)
    unit = jnp.where(unit, 1.0, 0.0).astype(jnp.bfloat16)
    operators_ref[...] = jnp.zeros(operators_ref.shape, jnp.bfloat16)
    for q in range(types):
        turned = lax.dot_general(
            unit, operators_in_ref[q], (((1,), (1,)), ((), ())), preferred_element_type=jnp.float32
        )
        operators_ref[q * LANES : (q + 1) * LANES, :size] = turned.astype(jnp.bfloat16)


def sweep_kernel(
    prev_ref, own_ref, next_ref, index_ref, operators_ref, lift_ref, right_ref, inverse_ref, *outs
):
    states = [prev_ref[...], own_ref[...], next_ref[...]]
    coupled = coupling(states, index_ref[...], operators_ref[...], lift_ref[...])
    lowered = (right_ref[...] - coupled).astype(jnp.bfloat16)
    result = apply_inverse(inverse_ref, lowered)
    outs[0][...] = result.astype(jnp.bfloat16)
    if len(outs) > 1:
        outs[1][...] = result
        outs[2][...] = lowered


def restrict_kernel(
    prev_ref, own_ref, next_ref, index_ref, operators_ref, lift_ref, lowered_ref, target_ref, lists_ref, out_ref
):
    states = [prev_ref[...], own_ref[...], next_ref[...]]
    coupled = coupling(states, index_ref[...], operators_ref[...], lift_ref[...])
    residual = lowered_ref[...].astype(jnp.float32) - coupled
    rows, dofs = out_ref.shape[1], residual.shape[1]
    member = target_ref[...] & (rows - 1)
    member = member == lax.broadcasted_iota(jnp.int32, (rows, residual.shape[0]), 0)
    partial = exact_dot(jnp.where(member, 1.0, 0.0).astype(jnp.bfloat16), residual)
    for t in range(out_ref.shape[0]):
        out_ref[t, :, :dofs] = partial
        out_ref[t, :, dofs:] = lists_ref[...]


def coarse_first_kernel(parts_ref, inverse_ref, restricted_ref, state_ref, index_ref):
    total = parts_ref[0]
    for t in range(1, parts_ref.shape[0]):
        total = total + parts_ref[t]
    dofs = restricted_ref.shape[1]
    restricted = total[:, :dofs]
    restricted_ref[...] = restricted
    index_ref[...] = total[:, dofs:].astype(jnp.int32)
    state_ref[...] = apply_inverse(inverse_ref, restricted.astype(jnp.bfloat16)).astype(jnp.bfloat16)


def correct_kernel(
    prev_ref,
    own_ref,
    next_ref,
    index_ref,
    operators_ref,
    lift_ref,
    right_ref,
    inverse_ref,
    target_ref,
    solution_ref,
    out_ref,
):
    states = [prev_ref[...], own_ref[...], next_ref[...]]
    coupled = coupling(states, index_ref[...], operators_ref[...], lift_ref[...])
    coarse = apply_inverse(inverse_ref, (right_ref[...] - coupled).astype(jnp.bfloat16))
    rows, fine = coarse.shape[0], solution_ref.shape[0]
    member = target_ref[...] & (rows - 1)
    member = member == lax.broadcasted_iota(jnp.int32, (rows, fine), 0)
    added = exact_dot(jnp.where(member, 1.0, 0.0).T.astype(jnp.bfloat16), coarse)
    out_ref[...] = (solution_ref[...] + added).astype(out_ref.dtype)


def run(kernel, outs, *operands, held=(), keep=()):
    count = len(operands)

    def body(*refs):
        kernel(*refs[:count], *refs[count + len(keep) :])

    single = not isinstance(outs, list)
    shapes = [outs] if single else outs
    vmem = pl.BlockSpec(memory_space=pltpu.VMEM)
    moved = sum(o.size * o.dtype.itemsize for o in operands)
    operands = [
        pltpu.with_memory_space_constraint(o, pltpu.VMEM) if i in held else o for i, o in enumerate(operands)
    ]
    operands += [pltpu.with_memory_space_constraint(o, pltpu.VMEM) for o in keep]
    result = pl.pallas_call(
        body,
        out_shape=[jax.ShapeDtypeStruct(s, d) for s, d in shapes],
        in_specs=[vmem] * len(operands),
        out_specs=[vmem] * len(shapes),
        compiler_params=pltpu.CompilerParams(vmem_limit_bytes=20 << 20),
        cost_estimate=pl.CostEstimate(flops=1 << 28, bytes_accessed=moved, transcendentals=0),
    )(*operands)
    return result[0] if single else result


def shards(
    right_side,
    fine_inverse,
    fine_links,
    fine_faces,
    coarse_inverse,
    coarse_links,
    coarse_faces,
    face_operators,
    agglomerate,
):
    f32, bf16, i32 = jnp.float32, jnp.bfloat16, jnp.int32
    fine_rows, dofs = right_side.shape
    tele_size = lax.axis_size("tele")
    coarse_rows = coarse_inverse.shape[0] * tele_size
    types = face_operators.shape[0]
    spare = -dofs % LANES

    block_inverse = jnp.broadcast_to(coarse_inverse[None], (tele_size,) + coarse_inverse.shape)
    right_side, block_inverse = lax.optimization_barrier((right_side, block_inverse))
    block_inverse = lax.all_to_all(block_inverse, "tele", 0, 0, tiled=True)
    block_inverse = block_inverse.reshape((coarse_rows,) + coarse_inverse.shape[1:])
    lift = jnp.asarray(face_table(), bf16)
    target = agglomerate[None, :]
    inverse = fine_inverse
    state, fine_index, lists, operators = run(
        first_kernel,
        [
            ((fine_rows, dofs), bf16),
            ((fine_rows, 12), i32),
            ((coarse_rows, spare), f32),
            ((types * LANES, LANES), bf16),
        ],
        right_side,
        inverse,
        fine_faces.T,
        fine_links.T,
        coarse_links,
        coarse_faces,
        face_operators,
        held=(1,),
    )
    shared = (operators, lift)

    def halo(block, axis):
        inner, outer = swapped(block, axis)
        return inner, block, outer

    both = ("fine", "tele")
    for cycle in range(CYCLES):
        for sweep in range(SWEEPS):
            if cycle == 0 and sweep == 0:
                continue
            outs = [((fine_rows, dofs), bf16)]
            if sweep == SWEEPS - 1:
                outs += [((fine_rows, dofs), f32), ((fine_rows, dofs), bf16)]
            result = run(
                sweep_kernel, outs, *halo(state, both), fine_index, *shared, right_side, inverse, held=(5, 7)
            )
            state = result[0]
        solution, lowered = result[1], result[2]
        parts = run(
            restrict_kernel,
            ((tele_size, coarse_rows, dofs + spare), f32),
            *halo(state, both),
            fine_index,
            *shared,
            lowered,
            target,
            lists,
            held=(5,),
            keep=(block_inverse,),
        )
        parts = lax.all_to_all(parts, "tele", 0, 0, tiled=True)
        restricted, coarse, coarse_index = run(
            coarse_first_kernel,
            [((coarse_rows, dofs), f32), ((coarse_rows, dofs), bf16), ((coarse_rows, spare), i32)],
            parts,
            block_inverse,
            held=(1,),
        )
        for sweep in range(SWEEPS - 2):
            coarse = run(
                sweep_kernel,
                [((coarse_rows, dofs), bf16)],
                *halo(coarse, "fine"),
                coarse_index,
                *shared,
                restricted,
                block_inverse,
                held=(5, 7),
            )[0]
        last = cycle == CYCLES - 1
        state = run(
            correct_kernel,
            ((fine_rows, dofs), f32 if last else bf16),
            *halo(coarse, "fine"),
            coarse_index,
            *shared,
            restricted,
            block_inverse,
            target,
            solution,
            held=(5, 7),
        )
    return state


def solution(mesh):
    both = P(("fine", "tele"))
    return jax.shard_map(
        shards,
        mesh=mesh,
        in_specs=(both, both, both, both, both, both, both, P(), both),
        out_specs=both,
        check_vma=False,
    )
```

```python
import functools

import jax
import jax.numpy as jnp
import numpy as np
from jax import lax
from jax.experimental import pallas as pl
from jax.experimental.pallas import tpu as pltpu
from jax.sharding import PartitionSpec as P

FIELDS = 5
NODES = 4
SWEEPS = 3
CYCLES = 2
LANES = 128
OPPOSITE = (1, 0, 3, 2, 5, 4)


def swapped(block, axis):
    count = lax.axis_size(axis)
    outer = lax.ppermute(block, axis, [(i, (i - 1 if i % 2 == 0 else i + 1) % count) for i in range(count)])
    inner = lax.ppermute(block, axis, [(i, i ^ 1) for i in range(count)])
    return inner, outer


def face_table():
    cube = np.arange(FIELDS * NODES**3).reshape(FIELDS, NODES, NODES, NODES)
    far = NODES - 1
    faces = (cube[:, 0], cube[:, far], cube[:, :, 0], cube[:, :, far], cube[..., 0], cube[..., far])
    table = np.zeros((6 * LANES, cube.size), np.float32)
    for k, face in enumerate(faces):
        nodes = face.reshape(-1)
        table[k * LANES + np.arange(nodes.size), nodes] = 1.0
    return table


def halves(value):
    high = value.astype(jnp.bfloat16)
    low = (value - high.astype(jnp.float32)).astype(jnp.bfloat16)
    return high, low


def exact_dot(left, right):
    high, low = halves(right)
    return jnp.dot(left, high, preferred_element_type=jnp.float32) + jnp.dot(
        left, low, preferred_element_type=jnp.float32
    )


def coupling(states, index, operators, lift):
    count = states[0].shape[0]
    pool = jnp.concatenate([state.astype(jnp.float32) for state in states], axis=0).astype(jnp.bfloat16)
    traces = lax.dot_general(pool, lift, (((1,), (1,)), ((), ())), preferred_element_type=jnp.float32)
    traces = traces.astype(jnp.bfloat16)
    column = lax.broadcasted_iota(jnp.int32, (count, pool.shape[0]), 1)
    face_rows, kinds = [], []
    for k in range(6):
        chosen = jnp.where(index[:, k : k + 1] == column, 1.0, 0.0).astype(jnp.bfloat16)
        across = traces[:, OPPOSITE[k] * LANES : (OPPOSITE[k] + 1) * LANES]
        face_rows.append(jnp.dot(chosen, across, preferred_element_type=jnp.float32))
        kinds.append(jnp.broadcast_to(index[:, 6 + k : 7 + k], (count, LANES)))
    face_rows = jnp.concatenate(face_rows, axis=0)
    kinds = jnp.concatenate(kinds, axis=0)
    types = operators.shape[0] // LANES
    spread = jnp.concatenate(
        [jnp.where(kinds == q, face_rows, 0.0).astype(jnp.bfloat16) for q in range(types)], axis=1
    )
    coupled = jnp.dot(spread, operators, preferred_element_type=jnp.float32)
    side_by_side = jnp.concatenate([coupled[k * count : (k + 1) * count] for k in range(6)], axis=1)
    high = side_by_side.astype(jnp.bfloat16).astype(jnp.float32)
    terms = jnp.concatenate([high, side_by_side - high], axis=0).astype(jnp.bfloat16)
    lifted = jnp.dot(terms, lift, preferred_element_type=jnp.float32)
    return lifted[:count] + lifted[count:]


def apply_inverse(blocks, vector):
    row = lax.broadcasted_iota(jnp.int32, vector.shape, 0)
    result = jnp.zeros(vector.shape, jnp.float32)
    first = 0
    for block in blocks:
        for e in range(block.shape[0]):
            product = lax.dot_general(
                vector, block[e], (((1,), (1,)), ((), ())), preferred_element_type=jnp.float32
            )
            result = jnp.where(row == first + e, product, result)
        first += block.shape[0]
    return result


def pool_rows(links, count, position, turn=0):
    shift = count.bit_length() - 1
    owner, within = links >> shift, (links - turn) & (count - 1)
    place = jnp.where(owner == position, 1, jnp.where(owner == (position ^ 1), 0, 2))
    return jnp.where(links >= 0, place * count + within, -1)


def first_kernel(*refs, count):
    sources, (state_ref, index_ref, lists_ref, operators_ref, inverse_ref) = refs[:count], refs[count : count + 5]
    targets, (sems, block_sems) = refs[count + 5 : -2], refs[-2:]
    right_ref, links_ref, faces_ref, coarse_links_ref, coarse_faces_ref, operators_in_ref = targets
    whole = [pltpu.make_async_copy(sources[i], targets[i], sems.at[i]) for i in range(count - 1)]
    blocks = [
        pltpu.make_async_copy(sources[-1].at[e], inverse_ref.at[e], block_sems.at[e])
        for e in range(inverse_ref.shape[0])
    ]
    for copy in [whole[0], *blocks, *whole[1:]]:
        copy.start()

    tele, column = lax.axis_index("tele"), lax.axis_index("fine")
    tele_size = lax.axis_size("tele")
    whole[0].wait()
    lowered = right_ref[...].astype(jnp.bfloat16)
    row = lax.broadcasted_iota(jnp.int32, lowered.shape, 0)
    result = jnp.zeros(lowered.shape, jnp.float32)
    for e, copy in enumerate(blocks):
        copy.wait()
        product = lax.dot_general(
            lowered, inverse_ref[e], (((1,), (1,)), ((), ())), preferred_element_type=jnp.float32
        )
        result = jnp.where(row == e, product, result)
    state_ref[...] = result.astype(jnp.bfloat16)
    for copy in whole[1:]:
        copy.wait()

    fine_rows = right_ref.shape[0]
    rows = pool_rows(links_ref[...], fine_rows, column * tele_size + tele)
    index = jnp.concatenate([rows.astype(jnp.float32), faces_ref[...].astype(jnp.float32)], axis=0)
    index_ref[...] = index.T.astype(jnp.int32)

    own = coarse_links_ref.shape[0]
    count = own * tele_size
    kinds = coarse_faces_ref[...].astype(jnp.float32)
    lists_ref[...] = jnp.zeros(lists_ref.shape, jnp.float32)
    row = lax.broadcasted_iota(jnp.int32, (count, kinds.shape[1]), 0)
    for t in range(tele_size):
        rows = pool_rows(coarse_links_ref[...], count, column, own * t).astype(jnp.float32)
        for part, values in enumerate((rows, kinds)):
            placed = jnp.zeros(row.shape, jnp.float32)
            for c in range(own):
                placed = jnp.where(row == ((own * (tele - t) + c) & (count - 1)), values[c : c + 1], placed)
            lists_ref[t, :, part * 6 : part * 6 + 6] = placed

    types, size, _ = operators_in_ref.shape
    unit = lax.broadcasted_iota(jnp.int32, (LANES, size), 0) == lax.broadcasted_iota(jnp.int32, (LANES, size), 1)
    unit = jnp.where(unit, 1.0, 0.0).astype(jnp.bfloat16)
    operators_ref[...] = jnp.zeros(operators_ref.shape, jnp.bfloat16)
    for q in range(types):
        turned = lax.dot_general(
            unit, operators_in_ref[q], (((1,), (1,)), ((), ())), preferred_element_type=jnp.float32
        )
        operators_ref[q * LANES : (q + 1) * LANES, :size] = turned.astype(jnp.bfloat16)


def take_kernel(before_ref, after_ref, low_ref, high_ref):
    low_ref[...] = before_ref[0:1]
    high_ref[...] = after_ref[1:2]


def sweep(refs, blocks):
    prev_ref, own_ref, next_ref, index_ref, operators_ref, lift_ref, right_ref = refs
    states = [prev_ref[...], own_ref[...], next_ref[...]]
    coupled = coupling(states, index_ref[...], operators_ref[...], lift_ref[...])
    lowered = (right_ref[...] - coupled).astype(jnp.bfloat16)
    return apply_inverse(blocks, lowered), lowered


def sweep_kernel(*refs, blocks):
    result, lowered = sweep(refs[:7], refs[7 : 7 + blocks])
    outs = refs[7 + blocks :]
    outs[0][...] = result.astype(jnp.bfloat16)
    if len(outs) > 1:
        outs[1][...] = result
        outs[2][...] = lowered


def restrict_kernel(
    prev_ref, own_ref, next_ref, index_ref, operators_ref, lift_ref, lowered_ref, target_ref, lists_ref, out_ref
):
    states = [prev_ref[...], own_ref[...], next_ref[...]]
    coupled = coupling(states, index_ref[...], operators_ref[...], lift_ref[...])
    residual = lowered_ref[...].astype(jnp.float32) - coupled
    tele_size, rows, dofs = out_ref.shape[0], out_ref.shape[1], residual.shape[1]
    shape = (tele_size * rows, residual.shape[0])
    row = lax.broadcasted_iota(jnp.int32, shape, 0)
    element = (row + (row >> (rows.bit_length() - 1)) * (rows // tele_size)) & (rows - 1)
    member = jnp.where((target_ref[...] & (rows - 1)) == element, 1.0, 0.0).astype(jnp.bfloat16)
    partial = exact_dot(member, residual)
    for t in range(tele_size):
        out_ref[t, :, :dofs] = partial[t * rows : (t + 1) * rows]
        out_ref[t, :, dofs:] = lists_ref[t]


def coarse_first_kernel(*refs, blocks):
    parts_ref, inverses, (restricted_ref, state_ref, index_ref) = refs[0], refs[1 : 1 + blocks], refs[1 + blocks :]
    total = parts_ref[0]
    for t in range(1, parts_ref.shape[0]):
        total = total + parts_ref[t]
    dofs = restricted_ref.shape[1]
    restricted = total[:, :dofs]
    restricted_ref[...] = restricted
    index_ref[...] = total[:, dofs:].astype(jnp.int32)
    state_ref[...] = apply_inverse(inverses, restricted.astype(jnp.bfloat16)).astype(jnp.bfloat16)


def correct_kernel(*refs, blocks):
    coarse, _ = sweep(refs[:7], refs[7 : 7 + blocks])
    target_ref, solution_ref, out_ref = refs[7 + blocks :]
    rows, fine = coarse.shape[0], solution_ref.shape[0]
    turn = lax.axis_index("tele") * (rows // lax.axis_size("tele"))
    member = ((target_ref[...] - turn) & (rows - 1)) == lax.broadcasted_iota(jnp.int32, (rows, fine), 0)
    added = exact_dot(jnp.where(member, 1.0, 0.0).T.astype(jnp.bfloat16), coarse)
    out_ref[...] = (solution_ref[...] + added).astype(out_ref.dtype)


def run(kernel, outs, *operands, held=(), keep=(), hbm=(), pinned=(), scratch=()):
    count = len(operands)

    def body(*refs):
        kernel(*refs[:count], *refs[count + len(keep) :])

    single = not isinstance(outs, list)
    shapes = [outs] if single else outs
    vmem = pl.BlockSpec(memory_space=pltpu.VMEM)
    moved = sum(o.size * o.dtype.itemsize for o in operands)
    operands = [
        pltpu.with_memory_space_constraint(o, pltpu.HBM if i in hbm else pltpu.VMEM) if i in held or i in hbm else o
        for i, o in enumerate(operands)
    ]
    operands += [pltpu.with_memory_space_constraint(o, pltpu.VMEM) for o in keep]
    result = pl.pallas_call(
        body,
        out_shape=[pltpu.VMEM(s, d) if i in pinned else jax.ShapeDtypeStruct(s, d) for i, (s, d) in enumerate(shapes)],
        in_specs=[pl.BlockSpec(memory_space=pltpu.HBM) if i in hbm else vmem for i in range(len(operands))],
        out_specs=[vmem] * len(shapes),
        scratch_shapes=scratch,
        compiler_params=pltpu.CompilerParams(vmem_limit_bytes=20 << 20),
        cost_estimate=pl.CostEstimate(flops=1 << 28, bytes_accessed=moved, transcendentals=0),
    )(*operands)
    return result[0] if single else result


def shards(
    right_side,
    fine_inverse,
    fine_links,
    fine_faces,
    coarse_inverse,
    coarse_links,
    coarse_faces,
    face_operators,
    agglomerate,
):
    f32, bf16, i32 = jnp.float32, jnp.bfloat16, jnp.int32
    fine_rows, dofs = right_side.shape
    tele_size = lax.axis_size("tele")
    coarse_rows = coarse_inverse.shape[0] * tele_size
    types = face_operators.shape[0]
    spare = -dofs % LANES

    def along(block, distance):
        return lax.ppermute(block, "tele", [(i, (i + distance) % tele_size) for i in range(tele_size)])

    before, after = along(coarse_inverse, 1), along(coarse_inverse, -1)
    lift = jnp.asarray(face_table(), bf16)
    target = agglomerate[None, :]
    operands = (
        right_side,
        fine_links.T,
        fine_faces.T,
        coarse_links,
        coarse_faces,
        face_operators,
        fine_inverse,
    )
    state, fine_index, lists, operators, inverse = run(
        functools.partial(first_kernel, count=len(operands)),
        [
            ((fine_rows, dofs), bf16),
            ((fine_rows, 12), i32),
            ((tele_size, coarse_rows, spare), f32),
            ((types * LANES, LANES), bf16),
            (fine_inverse.shape, bf16),
        ],
        *operands,
        hbm=range(len(operands)),
        pinned=(3, 4),
        scratch=[pltpu.VMEM(o.shape, o.dtype) for o in operands[:-1]]
        + [pltpu.SemaphoreType.DMA((len(operands),)), pltpu.SemaphoreType.DMA((fine_rows,))],
    )
    shared = (operators, lift)

    def halo(block, axis):
        inner, outer = swapped(block, axis)
        return inner, block, outer

    both = ("fine", "tele")
    for cycle in range(CYCLES):
        for sweep in range(SWEEPS):
            if cycle == 0 and sweep == 0:
                continue
            outs = [((fine_rows, dofs), bf16)]
            if sweep == SWEEPS - 1:
                outs += [((fine_rows, dofs), f32), ((fine_rows, dofs), bf16)]
            result = run(
                functools.partial(sweep_kernel, blocks=1),
                outs,
                *halo(state, both),
                fine_index,
                *shared,
                right_side,
                inverse,
                held=(5, 7),
            )
            state = result[0]
            if cycle == 0 and sweep == 1:
                before, after, state = lax.optimization_barrier((before, after, state))
                far_low, far_high = run(take_kernel, [((1,) + before.shape[1:], bf16)] * 2, before, after)
                far_low, far_high = along(far_low, 1), along(far_high, -1)
                blocks = (coarse_inverse, after, far_low, far_high, before)
        solution, lowered = result[1], result[2]
        parts = run(
            restrict_kernel,
            ((tele_size, coarse_rows, dofs + spare), f32),
            *halo(state, both),
            fine_index,
            *shared,
            lowered,
            target,
            lists,
            held=(5,),
        )
        parts = lax.all_to_all(parts, "tele", 0, 0, tiled=True)
        restricted, coarse, coarse_index = run(
            functools.partial(coarse_first_kernel, blocks=len(blocks)),
            [((coarse_rows, dofs), f32), ((coarse_rows, dofs), bf16), ((coarse_rows, spare), i32)],
            parts,
            *blocks,
            held=range(1, 1 + len(blocks)),
        )
        for sweep in range(SWEEPS - 2):
            coarse = run(
                functools.partial(sweep_kernel, blocks=len(blocks)),
                [((coarse_rows, dofs), bf16)],
                *halo(coarse, "fine"),
                coarse_index,
                *shared,
                restricted,
                *blocks,
                held=(5, *range(7, 7 + len(blocks))),
            )[0]
        last = cycle == CYCLES - 1
        state = run(
            functools.partial(correct_kernel, blocks=len(blocks)),
            ((fine_rows, dofs), f32 if last else bf16),
            *halo(coarse, "fine"),
            coarse_index,
            *shared,
            restricted,
            *blocks,
            target,
            solution,
            held=(5, *range(7, 7 + len(blocks))),
        )
    return state


def solution(mesh):
    both = P(("fine", "tele"))
    return jax.shard_map(
        shards,
        mesh=mesh,
        in_specs=(both, both, both, both, both, both, both, P(), both),
        out_specs=both,
        check_vma=False,
    )
```

```python
import functools

import jax
import jax.numpy as jnp
import numpy as np
from jax import lax
from jax.experimental import pallas as pl
from jax.experimental.pallas import tpu as pltpu
from jax.sharding import PartitionSpec as P

FIELDS = 5
NODES = 4
SWEEPS = 3
CYCLES = 2
LANES = 128
OPPOSITE = (1, 0, 3, 2, 5, 4)


def swapped(block, axis):
    count = lax.axis_size(axis)
    inner = lax.ppermute(block, axis, [(i, i ^ 1) for i in range(count)])
    outer = lax.ppermute(block, axis, [(i, (i - 1 if i % 2 == 0 else i + 1) % count) for i in range(count)])
    return inner, outer


def face_table():
    cube = np.arange(FIELDS * NODES**3).reshape(FIELDS, NODES, NODES, NODES)
    far = NODES - 1
    faces = (cube[:, 0], cube[:, far], cube[:, :, 0], cube[:, :, far], cube[..., 0], cube[..., far])
    table = np.zeros((6 * LANES, cube.size), np.float32)
    for k, face in enumerate(faces):
        nodes = face.reshape(-1)
        table[k * LANES + np.arange(nodes.size), nodes] = 1.0
    return table


def halves(value):
    high = value.astype(jnp.bfloat16)
    low = (value - high.astype(jnp.float32)).astype(jnp.bfloat16)
    return high, low


def exact_dot(left, right):
    high, low = halves(right)
    return jnp.dot(left, high, preferred_element_type=jnp.float32) + jnp.dot(
        left, low, preferred_element_type=jnp.float32
    )


def coupling(states, index, operators, lift):
    count = states[0].shape[0]
    pool = jnp.concatenate([state.astype(jnp.float32) for state in states], axis=0).astype(jnp.bfloat16)
    traces = lax.dot_general(pool, lift, (((1,), (1,)), ((), ())), preferred_element_type=jnp.float32)
    traces = traces.astype(jnp.bfloat16)
    column = lax.broadcasted_iota(jnp.int32, (count, pool.shape[0]), 1)
    face_rows, kinds = [], []
    for k in range(6):
        chosen = jnp.where(index[:, k : k + 1] == column, 1.0, 0.0).astype(jnp.bfloat16)
        across = traces[:, OPPOSITE[k] * LANES : (OPPOSITE[k] + 1) * LANES]
        face_rows.append(jnp.dot(chosen, across, preferred_element_type=jnp.float32))
        kinds.append(jnp.broadcast_to(index[:, 6 + k : 7 + k], (count, LANES)))
    face_rows = jnp.concatenate(face_rows, axis=0)
    kinds = jnp.concatenate(kinds, axis=0)
    types = operators.shape[0] // LANES
    spread = jnp.concatenate(
        [jnp.where(kinds == q, face_rows, 0.0).astype(jnp.bfloat16) for q in range(types)], axis=1
    )
    coupled = jnp.dot(spread, operators, preferred_element_type=jnp.float32)
    side_by_side = jnp.concatenate([coupled[k * count : (k + 1) * count] for k in range(6)], axis=1)
    high = side_by_side.astype(jnp.bfloat16).astype(jnp.float32)
    terms = jnp.concatenate([high, side_by_side - high], axis=0).astype(jnp.bfloat16)
    lifted = jnp.dot(terms, lift, preferred_element_type=jnp.float32)
    return lifted[:count] + lifted[count:]


def apply_inverse(blocks, vector):
    row = lax.broadcasted_iota(jnp.int32, vector.shape, 0)
    result = jnp.zeros(vector.shape, jnp.float32)
    first = 0
    for block in blocks:
        for e in range(block.shape[0]):
            product = lax.dot_general(
                vector, block[e], (((1,), (1,)), ((), ())), preferred_element_type=jnp.float32
            )
            result = jnp.where(row == first + e, product, result)
        first += block.shape[0]
    return result


def pool_rows(links, count, position, turn=0):
    shift = count.bit_length() - 1
    owner, within = links >> shift, (links & (count - 1)) ^ turn
    place = jnp.where(owner == position, 1, jnp.where(owner == (position ^ 1), 2, 0))
    return jnp.where(links >= 0, place * count + within, -1)


def first_kernel(*refs, count):
    sources, (state_ref, index_ref, lists_ref, operators_ref, inverse_ref) = refs[:count], refs[count : count + 5]
    targets, (sems, block_sems) = refs[count + 5 : -2], refs[-2:]
    right_ref, links_ref, faces_ref, coarse_links_ref, coarse_faces_ref, operators_in_ref = targets
    whole = [pltpu.make_async_copy(sources[i], targets[i], sems.at[i]) for i in range(count - 1)]
    step = inverse_ref.shape[0] // block_sems.shape[0]
    blocks = [
        pltpu.make_async_copy(
            sources[-1].at[i * step : (i + 1) * step], inverse_ref.at[i * step : (i + 1) * step], block_sems.at[i]
        )
        for i in range(block_sems.shape[0])
    ]
    for copy in [whole[0], *blocks, *whole[1:]]:
        copy.start()

    tele, column = lax.axis_index("tele"), lax.axis_index("fine")
    tele_size = lax.axis_size("tele")
    whole[0].wait()
    lowered = right_ref[...].astype(jnp.bfloat16)
    row = lax.broadcasted_iota(jnp.int32, lowered.shape, 0)
    result = jnp.zeros(lowered.shape, jnp.float32)
    for e in range(inverse_ref.shape[0]):
        if e % step == 0:
            blocks[e // step].wait()
        product = lax.dot_general(
            lowered, inverse_ref[e], (((1,), (1,)), ((), ())), preferred_element_type=jnp.float32
        )
        result = jnp.where(row == e, product, result)
    state_ref[...] = result.astype(jnp.bfloat16)
    for copy in whole[1:]:
        copy.wait()

    fine_rows = right_ref.shape[0]
    rows = pool_rows(links_ref[...], fine_rows, column * tele_size + tele)
    index = jnp.concatenate([rows.astype(jnp.float32), faces_ref[...].astype(jnp.float32)], axis=0)
    index_ref[...] = index.T.astype(jnp.int32)

    own = coarse_links_ref.shape[0]
    count = own * tele_size
    kinds = coarse_faces_ref[...].astype(jnp.float32)
    lists_ref[...] = jnp.zeros(lists_ref.shape, jnp.float32)
    row = lax.broadcasted_iota(jnp.int32, (count, kinds.shape[1]), 0)
    for t in range(tele_size):
        rows = pool_rows(coarse_links_ref[...], count, column, own * t).astype(jnp.float32)
        for part, values in enumerate((rows, kinds)):
            placed = jnp.zeros(row.shape, jnp.float32)
            for c in range(own):
                placed = jnp.where(row == ((own * tele + c) ^ (own * t)), values[c : c + 1], placed)
            lists_ref[t, :, part * 6 : part * 6 + 6] = placed

    types, size, _ = operators_in_ref.shape
    unit = lax.broadcasted_iota(jnp.int32, (LANES, size), 0) == lax.broadcasted_iota(jnp.int32, (LANES, size), 1)
    unit = jnp.where(unit, 1.0, 0.0).astype(jnp.bfloat16)
    operators_ref[...] = jnp.zeros(operators_ref.shape, jnp.bfloat16)
    for q in range(types):
        turned = lax.dot_general(
            unit, operators_in_ref[q], (((1,), (1,)), ((), ())), preferred_element_type=jnp.float32
        )
        operators_ref[q * LANES : (q + 1) * LANES, :size] = turned.astype(jnp.bfloat16)


def take_kernel(before_ref, after_ref, low_ref, high_ref):
    low_ref[...] = before_ref[0:1]
    high_ref[...] = after_ref[1:2]


def sweep(refs, blocks):
    prev_ref, own_ref, next_ref, index_ref, operators_ref, lift_ref, right_ref = refs
    states = [prev_ref[...], own_ref[...], next_ref[...]]
    coupled = coupling(states, index_ref[...], operators_ref[...], lift_ref[...])
    lowered = (right_ref[...] - coupled).astype(jnp.bfloat16)
    return apply_inverse(blocks, lowered), lowered


def sweep_kernel(*refs, blocks):
    result, lowered = sweep(refs[:7], refs[7 : 7 + blocks])
    outs = refs[7 + blocks :]
    outs[0][...] = result.astype(jnp.bfloat16)
    if len(outs) > 1:
        outs[1][...] = result
        outs[2][...] = lowered


def restrict_kernel(
    prev_ref, own_ref, next_ref, index_ref, operators_ref, lift_ref, lowered_ref, target_ref, lists_ref, out_ref
):
    states = [prev_ref[...], own_ref[...], next_ref[...]]
    coupled = coupling(states, index_ref[...], operators_ref[...], lift_ref[...])
    residual = lowered_ref[...].astype(jnp.float32) - coupled
    tele_size, rows, dofs = out_ref.shape[0], out_ref.shape[1], residual.shape[1]
    shape = (tele_size * rows, residual.shape[0])
    row = lax.broadcasted_iota(jnp.int32, shape, 0)
    element = (row & (rows - 1)) ^ ((row >> (rows.bit_length() - 1)) * (rows // tele_size))
    member = jnp.where((target_ref[...] & (rows - 1)) == element, 1.0, 0.0).astype(jnp.bfloat16)
    partial = exact_dot(member, residual)
    for t in range(tele_size):
        out_ref[t, :, :dofs] = partial[t * rows : (t + 1) * rows]
        out_ref[t, :, dofs:] = lists_ref[t]


def coarse_first_kernel(*refs, blocks):
    parts_ref, inverses, (restricted_ref, state_ref, index_ref) = refs[0], refs[1 : 1 + blocks], refs[1 + blocks :]
    total = parts_ref[0]
    for t in range(1, parts_ref.shape[0]):
        total = total + parts_ref[t]
    dofs = restricted_ref.shape[1]
    restricted = total[:, :dofs]
    restricted_ref[...] = restricted
    index_ref[...] = total[:, dofs:].astype(jnp.int32)
    state_ref[...] = apply_inverse(inverses, restricted.astype(jnp.bfloat16)).astype(jnp.bfloat16)


def correct_kernel(*refs, blocks):
    coarse, _ = sweep(refs[:7], refs[7 : 7 + blocks])
    target_ref, solution_ref, out_ref = refs[7 + blocks :]
    rows, fine = coarse.shape[0], solution_ref.shape[0]
    turn = lax.axis_index("tele") * (rows // lax.axis_size("tele"))
    member = ((target_ref[...] & (rows - 1)) ^ turn) == lax.broadcasted_iota(jnp.int32, (rows, fine), 0)
    added = exact_dot(jnp.where(member, 1.0, 0.0).T.astype(jnp.bfloat16), coarse)
    out_ref[...] = (solution_ref[...] + added).astype(out_ref.dtype)


def run(kernel, outs, *operands, held=(), keep=(), hbm=(), pinned=(), scratch=()):
    count = len(operands)

    def body(*refs):
        kernel(*refs[:count], *refs[count + len(keep) :])

    single = not isinstance(outs, list)
    shapes = [outs] if single else outs
    vmem = pl.BlockSpec(memory_space=pltpu.VMEM)
    moved = sum(o.size * o.dtype.itemsize for o in operands)
    operands = [
        pltpu.with_memory_space_constraint(o, pltpu.HBM if i in hbm else pltpu.VMEM) if i in held or i in hbm else o
        for i, o in enumerate(operands)
    ]
    operands += [pltpu.with_memory_space_constraint(o, pltpu.VMEM) for o in keep]
    result = pl.pallas_call(
        body,
        out_shape=[pltpu.VMEM(s, d) if i in pinned else jax.ShapeDtypeStruct(s, d) for i, (s, d) in enumerate(shapes)],
        in_specs=[pl.BlockSpec(memory_space=pltpu.HBM) if i in hbm else vmem for i in range(len(operands))],
        out_specs=[vmem] * len(shapes),
        scratch_shapes=scratch,
        compiler_params=pltpu.CompilerParams(vmem_limit_bytes=20 << 20),
        cost_estimate=pl.CostEstimate(flops=1 << 28, bytes_accessed=moved, transcendentals=0),
    )(*operands)
    return result[0] if single else result


def shards(
    right_side,
    fine_inverse,
    fine_links,
    fine_faces,
    coarse_inverse,
    coarse_links,
    coarse_faces,
    face_operators,
    agglomerate,
):
    f32, bf16, i32 = jnp.float32, jnp.bfloat16, jnp.int32
    fine_rows, dofs = right_side.shape
    tele_size = lax.axis_size("tele")
    coarse_rows = coarse_inverse.shape[0] * tele_size
    types = face_operators.shape[0]
    spare = -dofs % LANES

    def across(block, bits):
        return lax.ppermute(block, "tele", [(i, i ^ bits) for i in range(tele_size)])

    lift = jnp.asarray(face_table(), bf16)
    target = agglomerate[None, :]
    operands = (
        right_side,
        fine_links.T,
        fine_faces.T,
        coarse_links,
        coarse_faces,
        face_operators,
        fine_inverse,
    )
    state, fine_index, lists, operators, inverse = run(
        functools.partial(first_kernel, count=len(operands)),
        [
            ((fine_rows, dofs), bf16),
            ((fine_rows, 12), i32),
            ((tele_size, coarse_rows, spare), f32),
            ((types * LANES, LANES), bf16),
            (fine_inverse.shape, bf16),
        ],
        *operands,
        hbm=range(len(operands)),
        pinned=(3, 4),
        scratch=[pltpu.VMEM(o.shape, o.dtype) for o in operands[:-1]]
        + [pltpu.SemaphoreType.DMA((len(operands),)), pltpu.SemaphoreType.DMA((4,))],
    )
    shared = (operators, lift)
    own, state = lax.optimization_barrier((coarse_inverse, state))
    near, other = across(own, 1), across(own, tele_size - 1)

    def halo(block, axis):
        inner, outer = swapped(block, axis)
        return outer, block, inner

    both = ("fine", "tele")
    for cycle in range(CYCLES):
        for sweep in range(SWEEPS):
            if cycle == 0 and sweep == 0:
                continue
            outs = [((fine_rows, dofs), bf16)]
            if sweep == SWEEPS - 1:
                outs += [((fine_rows, dofs), f32), ((fine_rows, dofs), bf16)]
            result = run(
                functools.partial(sweep_kernel, blocks=1),
                outs,
                *halo(state, both),
                fine_index,
                *shared,
                right_side,
                inverse,
                held=(5, 7),
            )
            state = result[0]
            if cycle == 0 and sweep == 1:
                near, other, state = lax.optimization_barrier((near, other, state))
                far_low, far_high = run(take_kernel, [((1,) + near.shape[1:], bf16)] * 2, other, near)
                far_low, far_high = across(far_low, 1), across(far_high, tele_size - 1)
                blocks = (coarse_inverse, near, far_low, far_high, other)
        solution, lowered = result[1], result[2]
        parts = run(
            restrict_kernel,
            ((tele_size, coarse_rows, dofs + spare), f32),
            *halo(state, both),
            fine_index,
            *shared,
            lowered,
            target,
            lists,
            held=(5,),
        )
        parts = lax.all_to_all(parts, "tele", 0, 0, tiled=True)
        restricted, coarse, coarse_index = run(
            functools.partial(coarse_first_kernel, blocks=len(blocks)),
            [((coarse_rows, dofs), f32), ((coarse_rows, dofs), bf16), ((coarse_rows, spare), i32)],
            parts,
            *blocks,
            held=range(1, 1 + len(blocks)),
        )
        for sweep in range(SWEEPS - 2):
            coarse = run(
                functools.partial(sweep_kernel, blocks=len(blocks)),
                [((coarse_rows, dofs), bf16)],
                *halo(coarse, "fine"),
                coarse_index,
                *shared,
                restricted,
                *blocks,
                held=(5, *range(7, 7 + len(blocks))),
            )[0]
        last = cycle == CYCLES - 1
        state = run(
            functools.partial(correct_kernel, blocks=len(blocks)),
            ((fine_rows, dofs), f32 if last else bf16),
            *halo(coarse, "fine"),
            coarse_index,
            *shared,
            restricted,
            *blocks,
            target,
            solution,
            held=(5, *range(7, 7 + len(blocks))),
        )
    return state


def solution(mesh):
    both = P(("fine", "tele"))
    return jax.shard_map(
        shards,
        mesh=mesh,
        in_specs=(both, both, both, both, both, both, both, P(), both),
        out_specs=both,
        check_vma=False,
    )
```

```python
import functools

import jax
import jax.numpy as jnp
import numpy as np
from jax import lax
from jax.experimental import pallas as pl
from jax.experimental.pallas import tpu as pltpu
from jax.sharding import PartitionSpec as P

FIELDS = 5
NODES = 4
SWEEPS = 3
CYCLES = 2
LANES = 128
OPPOSITE = (1, 0, 3, 2, 5, 4)


def swapped(block, axis):
    count = lax.axis_size(axis)
    inner = lax.ppermute(block, axis, [(i, i ^ 1) for i in range(count)])
    outer = lax.ppermute(block, axis, [(i, (i - 1 if i % 2 == 0 else i + 1) % count) for i in range(count)])
    return inner, outer


def face_table():
    cube = np.arange(FIELDS * NODES**3).reshape(FIELDS, NODES, NODES, NODES)
    far = NODES - 1
    faces = (cube[:, 0], cube[:, far], cube[:, :, 0], cube[:, :, far], cube[..., 0], cube[..., far])
    table = np.zeros((6 * LANES, cube.size), np.float32)
    for k, face in enumerate(faces):
        nodes = face.reshape(-1)
        table[k * LANES + np.arange(nodes.size), nodes] = 1.0
    return table


def halves(value):
    high = value.astype(jnp.bfloat16)
    low = (value - high.astype(jnp.float32)).astype(jnp.bfloat16)
    return high, low


def exact_dot(left, right):
    high, low = halves(right)
    return jnp.dot(left, high, preferred_element_type=jnp.float32) + jnp.dot(
        left, low, preferred_element_type=jnp.float32
    )


def coupling(states, index, operators, lift):
    count = states[0].shape[0]
    pool = jnp.concatenate([state.astype(jnp.float32) for state in states], axis=0).astype(jnp.bfloat16)
    traces = lax.dot_general(pool, lift, (((1,), (1,)), ((), ())), preferred_element_type=jnp.float32)
    traces = traces.astype(jnp.bfloat16)
    column = lax.broadcasted_iota(jnp.int32, (count, pool.shape[0]), 1)
    face_rows, kinds = [], []
    for k in range(6):
        chosen = jnp.where(index[:, k : k + 1] == column, 1.0, 0.0).astype(jnp.bfloat16)
        across = traces[:, OPPOSITE[k] * LANES : (OPPOSITE[k] + 1) * LANES]
        face_rows.append(jnp.dot(chosen, across, preferred_element_type=jnp.float32))
        kinds.append(jnp.broadcast_to(index[:, 6 + k : 7 + k], (count, LANES)))
    face_rows = jnp.concatenate(face_rows, axis=0)
    kinds = jnp.concatenate(kinds, axis=0)
    types = operators.shape[0] // LANES
    spread = jnp.concatenate(
        [jnp.where(kinds == q, face_rows, 0.0).astype(jnp.bfloat16) for q in range(types)], axis=1
    )
    coupled = jnp.dot(spread, operators, preferred_element_type=jnp.float32)
    side_by_side = jnp.concatenate([coupled[k * count : (k + 1) * count] for k in range(6)], axis=1)
    high = side_by_side.astype(jnp.bfloat16).astype(jnp.float32)
    terms = jnp.concatenate([high, side_by_side - high], axis=0).astype(jnp.bfloat16)
    lifted = jnp.dot(terms, lift, preferred_element_type=jnp.float32)
    return lifted[:count] + lifted[count:]


def apply_inverse(blocks, vector):
    row = lax.broadcasted_iota(jnp.int32, vector.shape, 0)
    result = jnp.zeros(vector.shape, jnp.float32)
    first = 0
    for block in blocks:
        for e in range(block.shape[0]):
            product = lax.dot_general(
                vector, block[e], (((1,), (1,)), ((), ())), preferred_element_type=jnp.float32
            )
            result = jnp.where(row == first + e, product, result)
        first += block.shape[0]
    return result


def pool_rows(links, count, position, turn=0):
    shift = count.bit_length() - 1
    owner, within = links >> shift, (links & (count - 1)) ^ turn
    place = jnp.where(owner == position, 1, jnp.where(owner == (position ^ 1), 2, 0))
    return jnp.where(links >= 0, place * count + within, -1)


def first_kernel(*refs, count):
    sources, (state_ref, index_ref, lists_ref, operators_ref, inverse_ref) = refs[:count], refs[count : count + 5]
    targets, (sems, block_sems) = refs[count + 5 : -2], refs[-2:]
    right_ref, links_ref, faces_ref, coarse_links_ref, coarse_faces_ref, operators_in_ref = targets
    whole = [pltpu.make_async_copy(sources[i], targets[i], sems.at[i]) for i in range(count - 1)]
    step = inverse_ref.shape[0] // block_sems.shape[0]
    blocks = [
        pltpu.make_async_copy(
            sources[-1].at[i * step : (i + 1) * step], inverse_ref.at[i * step : (i + 1) * step], block_sems.at[i]
        )
        for i in range(block_sems.shape[0])
    ]
    for copy in whole + blocks:
        copy.start()

    tele, column = lax.axis_index("tele"), lax.axis_index("fine")
    tele_size = lax.axis_size("tele")
    for copy in whole:
        copy.wait()

    fine_rows = right_ref.shape[0]
    rows = pool_rows(links_ref[...], fine_rows, column * tele_size + tele)
    index = jnp.concatenate([rows.astype(jnp.float32), faces_ref[...].astype(jnp.float32)], axis=0)
    index_ref[...] = index.T.astype(jnp.int32)

    own = coarse_links_ref.shape[0]
    count = own * tele_size
    kinds = coarse_faces_ref[...].astype(jnp.float32)
    lists_ref[...] = jnp.zeros(lists_ref.shape, jnp.float32)
    row = lax.broadcasted_iota(jnp.int32, (count, kinds.shape[1]), 0)
    for t in range(tele_size):
        rows = pool_rows(coarse_links_ref[...], count, column, own * t).astype(jnp.float32)
        for part, values in enumerate((rows, kinds)):
            placed = jnp.zeros(row.shape, jnp.float32)
            for c in range(own):
                placed = jnp.where(row == ((own * tele + c) ^ (own * t)), values[c : c + 1], placed)
            lists_ref[t, :, part * 6 : part * 6 + 6] = placed

    types, size, _ = operators_in_ref.shape
    unit = lax.broadcasted_iota(jnp.int32, (LANES, size), 0) == lax.broadcasted_iota(jnp.int32, (LANES, size), 1)
    unit = jnp.where(unit, 1.0, 0.0).astype(jnp.bfloat16)
    operators_ref[...] = jnp.zeros(operators_ref.shape, jnp.bfloat16)
    for q in range(types):
        turned = lax.dot_general(
            unit, operators_in_ref[q], (((1,), (1,)), ((), ())), preferred_element_type=jnp.float32
        )
        operators_ref[q * LANES : (q + 1) * LANES, :size] = turned.astype(jnp.bfloat16)

    lowered = right_ref[...].astype(jnp.bfloat16)
    row = lax.broadcasted_iota(jnp.int32, lowered.shape, 0)
    result = jnp.zeros(lowered.shape, jnp.float32)
    for e in range(inverse_ref.shape[0]):
        if e % step == 0:
            blocks[e // step].wait()
        product = lax.dot_general(
            lowered, inverse_ref[e], (((1,), (1,)), ((), ())), preferred_element_type=jnp.float32
        )
        result = jnp.where(row == e, product, result)
    state_ref[...] = result.astype(jnp.bfloat16)


def take_kernel(before_ref, after_ref, low_ref, high_ref):
    low_ref[...] = before_ref[0:1]
    high_ref[...] = after_ref[1:2]


def sweep(refs, blocks):
    prev_ref, own_ref, next_ref, index_ref, operators_ref, lift_ref, right_ref = refs
    states = [prev_ref[...], own_ref[...], next_ref[...]]
    coupled = coupling(states, index_ref[...], operators_ref[...], lift_ref[...])
    lowered = (right_ref[...] - coupled).astype(jnp.bfloat16)
    return apply_inverse(blocks, lowered), lowered


def sweep_kernel(*refs, blocks):
    result, lowered = sweep(refs[:7], refs[7 : 7 + blocks])
    outs = refs[7 + blocks :]
    outs[0][...] = result.astype(jnp.bfloat16)
    if len(outs) > 1:
        outs[1][...] = result
        outs[2][...] = lowered


def restrict_kernel(
    prev_ref, own_ref, next_ref, index_ref, operators_ref, lift_ref, lowered_ref, target_ref, lists_ref, out_ref
):
    states = [prev_ref[...], own_ref[...], next_ref[...]]
    coupled = coupling(states, index_ref[...], operators_ref[...], lift_ref[...])
    residual = lowered_ref[...].astype(jnp.float32) - coupled
    tele_size, rows, dofs = out_ref.shape[0], out_ref.shape[1], residual.shape[1]
    shape = (tele_size * rows, residual.shape[0])
    row = lax.broadcasted_iota(jnp.int32, shape, 0)
    element = (row & (rows - 1)) ^ ((row >> (rows.bit_length() - 1)) * (rows // tele_size))
    member = jnp.where((target_ref[...] & (rows - 1)) == element, 1.0, 0.0).astype(jnp.bfloat16)
    partial = exact_dot(member, residual)
    for t in range(tele_size):
        out_ref[t, :, :dofs] = partial[t * rows : (t + 1) * rows]
        out_ref[t, :, dofs:] = lists_ref[t]


def coarse_first_kernel(*refs, blocks):
    parts_ref, inverses, (restricted_ref, state_ref, index_ref) = refs[0], refs[1 : 1 + blocks], refs[1 + blocks :]
    total = parts_ref[0]
    for t in range(1, parts_ref.shape[0]):
        total = total + parts_ref[t]
    dofs = restricted_ref.shape[1]
    restricted = total[:, :dofs]
    restricted_ref[...] = restricted
    index_ref[...] = total[:, dofs:].astype(jnp.int32)
    state_ref[...] = apply_inverse(inverses, restricted.astype(jnp.bfloat16)).astype(jnp.bfloat16)


def correct_kernel(*refs, blocks):
    coarse, _ = sweep(refs[:7], refs[7 : 7 + blocks])
    target_ref, solution_ref, out_ref = refs[7 + blocks :]
    rows, fine = coarse.shape[0], solution_ref.shape[0]
    turn = lax.axis_index("tele") * (rows // lax.axis_size("tele"))
    member = ((target_ref[...] & (rows - 1)) ^ turn) == lax.broadcasted_iota(jnp.int32, (rows, fine), 0)
    added = exact_dot(jnp.where(member, 1.0, 0.0).T.astype(jnp.bfloat16), coarse)
    out_ref[...] = (solution_ref[...] + added).astype(out_ref.dtype)


def run(kernel, outs, *operands, held=(), keep=(), hbm=(), pinned=(), scratch=()):
    count = len(operands)

    def body(*refs):
        kernel(*refs[:count], *refs[count + len(keep) :])

    single = not isinstance(outs, list)
    shapes = [outs] if single else outs
    vmem = pl.BlockSpec(memory_space=pltpu.VMEM)
    moved = sum(o.size * o.dtype.itemsize for o in operands)
    operands = [
        pltpu.with_memory_space_constraint(o, pltpu.HBM if i in hbm else pltpu.VMEM) if i in held or i in hbm else o
        for i, o in enumerate(operands)
    ]
    operands += [pltpu.with_memory_space_constraint(o, pltpu.VMEM) for o in keep]
    result = pl.pallas_call(
        body,
        out_shape=[pltpu.VMEM(s, d) if i in pinned else jax.ShapeDtypeStruct(s, d) for i, (s, d) in enumerate(shapes)],
        in_specs=[pl.BlockSpec(memory_space=pltpu.HBM) if i in hbm else vmem for i in range(len(operands))],
        out_specs=[vmem] * len(shapes),
        scratch_shapes=scratch,
        compiler_params=pltpu.CompilerParams(vmem_limit_bytes=20 << 20),
        cost_estimate=pl.CostEstimate(flops=1 << 32, bytes_accessed=moved, transcendentals=0),
    )(*operands)
    return result[0] if single else result


def shards(
    right_side,
    fine_inverse,
    fine_links,
    fine_faces,
    coarse_inverse,
    coarse_links,
    coarse_faces,
    face_operators,
    agglomerate,
):
    f32, bf16, i32 = jnp.float32, jnp.bfloat16, jnp.int32
    fine_rows, dofs = right_side.shape
    tele_size = lax.axis_size("tele")
    coarse_rows = coarse_inverse.shape[0] * tele_size
    types = face_operators.shape[0]
    spare = -dofs % LANES

    def across(block, bits):
        return lax.ppermute(block, "tele", [(i, i ^ bits) for i in range(tele_size)])

    lift = jnp.asarray(face_table(), bf16)
    target = agglomerate[None, :]
    operands = (
        right_side,
        fine_links.T,
        fine_faces.T,
        coarse_links,
        coarse_faces,
        face_operators,
        fine_inverse,
    )
    state, fine_index, lists, operators, inverse = run(
        functools.partial(first_kernel, count=len(operands)),
        [
            ((fine_rows, dofs), bf16),
            ((fine_rows, 12), i32),
            ((tele_size, coarse_rows, spare), f32),
            ((types * LANES, LANES), bf16),
            (fine_inverse.shape, bf16),
        ],
        *operands,
        hbm=range(len(operands)),
        pinned=(3, 4),
        scratch=[pltpu.VMEM(o.shape, o.dtype) for o in operands[:-1]]
        + [pltpu.SemaphoreType.DMA((len(operands),)), pltpu.SemaphoreType.DMA((4,))],
    )
    shared = (operators, lift)

    def halo(block, axis):
        inner, outer = swapped(block, axis)
        return outer, block, inner

    both = ("fine", "tele")
    for cycle in range(CYCLES):
        for sweep in range(SWEEPS):
            if cycle == 0 and sweep == 0:
                continue
            outer, own, inner = halo(state, both)
            if cycle == 0 and sweep == 1:
                sent, inner = lax.optimization_barrier((coarse_inverse, inner))
                near, other = across(sent, 1), across(sent, tele_size - 1)
            if cycle == 0 and sweep == 2:
                near, other, outer = lax.optimization_barrier((near, other, outer))
                far_low, far_high = run(take_kernel, [((1,) + near.shape[1:], bf16)] * 2, other, near)
                far_low, far_high = across(far_low, 1), across(far_high, tele_size - 1)
                blocks = (coarse_inverse, near, far_low, far_high, other)
            outs = [((fine_rows, dofs), bf16)]
            if sweep == SWEEPS - 1:
                outs += [((fine_rows, dofs), f32), ((fine_rows, dofs), bf16)]
            result = run(
                functools.partial(sweep_kernel, blocks=1),
                outs,
                outer,
                own,
                inner,
                fine_index,
                *shared,
                right_side,
                inverse,
                held=(5, 7),
            )
            state = result[0]
        solution, lowered = result[1], result[2]
        parts = run(
            restrict_kernel,
            ((tele_size, coarse_rows, dofs + spare), f32),
            *halo(state, both),
            fine_index,
            *shared,
            lowered,
            target,
            lists,
            held=(5,),
        )
        parts = lax.all_to_all(parts, "tele", 0, 0, tiled=True)
        restricted, coarse, coarse_index = run(
            functools.partial(coarse_first_kernel, blocks=len(blocks)),
            [((coarse_rows, dofs), f32), ((coarse_rows, dofs), bf16), ((coarse_rows, spare), i32)],
            parts,
            *blocks,
            held=range(1, 1 + len(blocks)),
        )
        for sweep in range(SWEEPS - 2):
            coarse = run(
                functools.partial(sweep_kernel, blocks=len(blocks)),
                [((coarse_rows, dofs), bf16)],
                *halo(coarse, "fine"),
                coarse_index,
                *shared,
                restricted,
                *blocks,
                held=(5, *range(7, 7 + len(blocks))),
            )[0]
        last = cycle == CYCLES - 1
        state = run(
            functools.partial(correct_kernel, blocks=len(blocks)),
            ((fine_rows, dofs), f32 if last else bf16),
            *halo(coarse, "fine"),
            coarse_index,
            *shared,
            restricted,
            *blocks,
            target,
            solution,
            held=(5, *range(7, 7 + len(blocks))),
        )
    return state


def solution(mesh):
    both = P(("fine", "tele"))
    return jax.shard_map(
        shards,
        mesh=mesh,
        in_specs=(both, both, both, both, both, both, both, P(), both),
        out_specs=both,
        check_vma=False,
    )
```

```python
import functools

import jax
import jax.numpy as jnp
import numpy as np
from jax import lax
from jax.experimental import pallas as pl
from jax.experimental.pallas import tpu as pltpu
from jax.sharding import PartitionSpec as P

FIELDS = 5
NODES = 4
SWEEPS = 3
CYCLES = 2
LANES = 128
OPPOSITE = (1, 0, 3, 2, 5, 4)


def swapped(block, axis):
    count = lax.axis_size(axis)
    inner = lax.ppermute(block, axis, [(i, i ^ 1) for i in range(count)])
    outer = lax.ppermute(block, axis, [(i, (i - 1 if i % 2 == 0 else i + 1) % count) for i in range(count)])
    return inner, outer


def face_table():
    cube = np.arange(FIELDS * NODES**3).reshape(FIELDS, NODES, NODES, NODES)
    far = NODES - 1
    faces = (cube[:, 0], cube[:, far], cube[:, :, 0], cube[:, :, far], cube[..., 0], cube[..., far])
    table = np.zeros((6 * LANES, cube.size), np.float32)
    for k, face in enumerate(faces):
        nodes = face.reshape(-1)
        table[k * LANES + np.arange(nodes.size), nodes] = 1.0
    return table


def halves(value):
    high = value.astype(jnp.bfloat16)
    low = (value - high.astype(jnp.float32)).astype(jnp.bfloat16)
    return high, low


def exact_dot(left, right):
    high, low = halves(right)
    return jnp.dot(left, high, preferred_element_type=jnp.float32) + jnp.dot(
        left, low, preferred_element_type=jnp.float32
    )


def coupling(states, index, operators, lift):
    count = states[0].shape[0]
    pool = jnp.concatenate([state.astype(jnp.float32) for state in states], axis=0).astype(jnp.bfloat16)
    traces = lax.dot_general(pool, lift, (((1,), (1,)), ((), ())), preferred_element_type=jnp.float32)
    traces = traces.astype(jnp.bfloat16)
    column = lax.broadcasted_iota(jnp.int32, (count, pool.shape[0]), 1)
    face_rows, kinds = [], []
    for k in range(6):
        chosen = jnp.where(index[:, k : k + 1] == column, 1.0, 0.0).astype(jnp.bfloat16)
        across = traces[:, OPPOSITE[k] * LANES : (OPPOSITE[k] + 1) * LANES]
        face_rows.append(jnp.dot(chosen, across, preferred_element_type=jnp.float32))
        kinds.append(jnp.broadcast_to(index[:, 6 + k : 7 + k], (count, LANES)))
    face_rows = jnp.concatenate(face_rows, axis=0)
    kinds = jnp.concatenate(kinds, axis=0)
    types = operators.shape[1] // LANES
    spread = jnp.concatenate(
        [jnp.where(kinds == q, face_rows, 0.0).astype(jnp.bfloat16) for q in range(types)], axis=1
    )
    coupled = lax.dot_general(spread, operators, (((1,), (1,)), ((), ())), preferred_element_type=jnp.float32)
    side_by_side = jnp.concatenate([coupled[k * count : (k + 1) * count] for k in range(6)], axis=1)
    high = side_by_side.astype(jnp.bfloat16).astype(jnp.float32)
    terms = jnp.concatenate([high, side_by_side - high], axis=0).astype(jnp.bfloat16)
    lifted = jnp.dot(terms, lift, preferred_element_type=jnp.float32)
    return lifted[:count] + lifted[count:]


def apply_inverse(blocks, vector):
    row = lax.broadcasted_iota(jnp.int32, vector.shape, 0)
    result = jnp.zeros(vector.shape, jnp.float32)
    first = 0
    for block in blocks:
        for e in range(block.shape[0]):
            product = lax.dot_general(
                vector, block[e], (((1,), (1,)), ((), ())), preferred_element_type=jnp.float32
            )
            result = jnp.where(row == first + e, product, result)
        first += block.shape[0]
    return result


def pool_rows(links, count, position):
    shift = count.bit_length() - 1
    owner, within = links >> shift, links & (count - 1)
    place = jnp.where(owner == position, 1, jnp.where(owner == (position ^ 1), 2, 0))
    return jnp.where(links >= 0, place * count + within, -1)


def first_kernel(*refs, count):
    sources, (state_ref, index_ref, lists_ref, operators_ref, inverse_ref) = refs[:count], refs[count : count + 5]
    targets, (sems, block_sems) = refs[count + 5 : -2], refs[-2:]
    right_ref, links_ref, faces_ref, coarse_links_ref, coarse_faces_ref, operators_in_ref = targets
    whole = [pltpu.make_async_copy(sources[i], targets[i], sems.at[i]) for i in range(count - 1)]
    step = inverse_ref.shape[0] // block_sems.shape[0]
    blocks = [
        pltpu.make_async_copy(
            sources[-1].at[i * step : (i + 1) * step], inverse_ref.at[i * step : (i + 1) * step], block_sems.at[i]
        )
        for i in range(block_sems.shape[0])
    ]
    for copy in whole + blocks:
        copy.start()

    tele, column = lax.axis_index("tele"), lax.axis_index("fine")
    tele_size = lax.axis_size("tele")
    for copy in whole:
        copy.wait()

    fine_rows = right_ref.shape[0]
    rows = pool_rows(links_ref[...], fine_rows, column * tele_size + tele)
    index = jnp.concatenate([rows.astype(jnp.float32), faces_ref[...].astype(jnp.float32)], axis=0)
    index_ref[...] = index.T.astype(jnp.int32)

    own = coarse_links_ref.shape[0]
    count = own * tele_size
    rows = pool_rows(coarse_links_ref[...], count, column).astype(jnp.float32)
    kinds = coarse_faces_ref[...].astype(jnp.float32)
    lists_ref[...] = jnp.zeros(lists_ref.shape, jnp.float32)
    row = lax.broadcasted_iota(jnp.int32, (count, kinds.shape[1]), 0)
    for part, values in enumerate((rows, kinds)):
        placed = jnp.zeros(row.shape, jnp.float32)
        for c in range(own):
            placed = jnp.where(row == own * tele + c, values[c : c + 1], placed)
        lists_ref[:, part * 6 : part * 6 + 6] = placed

    types, size, _ = operators_in_ref.shape
    operators_ref[...] = jnp.zeros(operators_ref.shape, jnp.bfloat16)
    for q in range(types):
        operators_ref[:size, q * LANES : q * LANES + size] = operators_in_ref[q]

    lowered = right_ref[...].astype(jnp.bfloat16)
    row = lax.broadcasted_iota(jnp.int32, lowered.shape, 0)
    result = jnp.zeros(lowered.shape, jnp.float32)
    for e in range(inverse_ref.shape[0]):
        if e % step == 0:
            blocks[e // step].wait()
        product = lax.dot_general(
            lowered, inverse_ref[e], (((1,), (1,)), ((), ())), preferred_element_type=jnp.float32
        )
        result = jnp.where(row == e, product, result)
    state_ref[...] = result.astype(jnp.bfloat16)


def take_kernel(before_ref, after_ref, low_ref, high_ref):
    low_ref[...] = before_ref[0:1]
    high_ref[...] = after_ref[1:2]


def sweep(refs, blocks):
    prev_ref, own_ref, next_ref, index_ref, operators_ref, lift_ref, right_ref = refs
    states = [prev_ref[...], own_ref[...], next_ref[...]]
    coupled = coupling(states, index_ref[...], operators_ref[...], lift_ref[...])
    lowered = (right_ref[...] - coupled).astype(jnp.bfloat16)
    return apply_inverse(blocks, lowered), lowered


def sweep_kernel(*refs, blocks):
    result, lowered = sweep(refs[:7], refs[7 : 7 + blocks])
    outs = refs[7 + blocks :]
    outs[0][...] = result.astype(jnp.bfloat16)
    if len(outs) > 1:
        outs[1][...] = result
        outs[2][...] = lowered


def restrict_kernel(
    prev_ref, own_ref, next_ref, index_ref, operators_ref, lift_ref, lowered_ref, target_ref, lists_ref, out_ref
):
    states = [prev_ref[...], own_ref[...], next_ref[...]]
    coupled = coupling(states, index_ref[...], operators_ref[...], lift_ref[...])
    residual = lowered_ref[...].astype(jnp.float32) - coupled
    tele_size, rows, dofs = out_ref.shape[0], out_ref.shape[1], residual.shape[1]
    shape = (tele_size * rows, residual.shape[0])
    row = lax.broadcasted_iota(jnp.int32, shape, 0)
    element = (row & (rows - 1)) ^ ((row >> (rows.bit_length() - 1)) * (rows // tele_size))
    member = jnp.where((target_ref[...] & (rows - 1)) == element, 1.0, 0.0).astype(jnp.bfloat16)
    partial = exact_dot(member, residual)
    own = rows // tele_size
    for t in range(tele_size):
        out_ref[t, :, :dofs] = partial[t * rows : (t + 1) * rows]
        for s in range(tele_size):
            out_ref[t, s * own : (s + 1) * own, dofs:] = lists_ref[(s ^ t) * own : ((s ^ t) + 1) * own]


def coarse_first_kernel(*refs, blocks):
    parts_ref, inverses, (restricted_ref, state_ref, index_ref) = refs[0], refs[1 : 1 + blocks], refs[1 + blocks :]
    total = parts_ref[0]
    for t in range(1, parts_ref.shape[0]):
        total = total + parts_ref[t]
    dofs = restricted_ref.shape[1]
    restricted = total[:, :dofs]
    restricted_ref[...] = restricted
    lists = total[:, dofs:].astype(jnp.int32)
    turn = lax.axis_index("tele") * (total.shape[0] // parts_ref.shape[0])
    turned = (lax.broadcasted_iota(jnp.int32, lists.shape, 1) < 6) & (lists >= 0)
    index_ref[...] = jnp.where(turned, lists ^ turn, lists)
    state_ref[...] = apply_inverse(inverses, restricted.astype(jnp.bfloat16)).astype(jnp.bfloat16)


def correct_kernel(*refs, blocks):
    coarse, _ = sweep(refs[:7], refs[7 : 7 + blocks])
    target_ref, solution_ref, out_ref = refs[7 + blocks :]
    rows, fine = coarse.shape[0], solution_ref.shape[0]
    turn = lax.axis_index("tele") * (rows // lax.axis_size("tele"))
    member = ((target_ref[...] & (rows - 1)) ^ turn) == lax.broadcasted_iota(jnp.int32, (rows, fine), 0)
    added = exact_dot(jnp.where(member, 1.0, 0.0).T.astype(jnp.bfloat16), coarse)
    out_ref[...] = (solution_ref[...] + added).astype(out_ref.dtype)


def run(kernel, outs, *operands, held=(), keep=(), hbm=(), pinned=(), scratch=()):
    count = len(operands)

    def body(*refs):
        kernel(*refs[:count], *refs[count + len(keep) :])

    single = not isinstance(outs, list)
    shapes = [outs] if single else outs
    vmem = pl.BlockSpec(memory_space=pltpu.VMEM)
    moved = sum(o.size * o.dtype.itemsize for o in operands)
    operands = [
        pltpu.with_memory_space_constraint(o, pltpu.HBM if i in hbm else pltpu.VMEM) if i in held or i in hbm else o
        for i, o in enumerate(operands)
    ]
    operands += [pltpu.with_memory_space_constraint(o, pltpu.VMEM) for o in keep]
    result = pl.pallas_call(
        body,
        out_shape=[pltpu.VMEM(s, d) if i in pinned else jax.ShapeDtypeStruct(s, d) for i, (s, d) in enumerate(shapes)],
        in_specs=[pl.BlockSpec(memory_space=pltpu.HBM) if i in hbm else vmem for i in range(len(operands))],
        out_specs=[vmem] * len(shapes),
        scratch_shapes=scratch,
        compiler_params=pltpu.CompilerParams(vmem_limit_bytes=20 << 20),
        cost_estimate=pl.CostEstimate(flops=1 << 32, bytes_accessed=moved, transcendentals=0),
    )(*operands)
    return result[0] if single else result


def shards(
    right_side,
    fine_inverse,
    fine_links,
    fine_faces,
    coarse_inverse,
    coarse_links,
    coarse_faces,
    face_operators,
    agglomerate,
):
    f32, bf16, i32 = jnp.float32, jnp.bfloat16, jnp.int32
    fine_rows, dofs = right_side.shape
    tele_size = lax.axis_size("tele")
    coarse_rows = coarse_inverse.shape[0] * tele_size
    types = face_operators.shape[0]
    spare = -dofs % LANES

    def across(block, bits):
        return lax.ppermute(block, "tele", [(i, i ^ bits) for i in range(tele_size)])

    lift = jnp.asarray(face_table(), bf16)
    target = agglomerate[None, :]
    operands = (
        right_side,
        fine_links.T,
        fine_faces.T,
        coarse_links,
        coarse_faces,
        face_operators,
        fine_inverse,
    )
    state, fine_index, lists, operators, inverse = run(
        functools.partial(first_kernel, count=len(operands)),
        [
            ((fine_rows, dofs), bf16),
            ((fine_rows, 12), i32),
            ((coarse_rows, spare), f32),
            ((LANES, types * LANES), bf16),
            (fine_inverse.shape, bf16),
        ],
        *operands,
        hbm=range(len(operands)),
        pinned=(3, 4),
        scratch=[pltpu.VMEM(o.shape, o.dtype) for o in operands[:-1]]
        + [pltpu.SemaphoreType.DMA((len(operands),)), pltpu.SemaphoreType.DMA((4,))],
    )
    shared = (operators, lift)

    def halo(block, axis):
        inner, outer = swapped(block, axis)
        return outer, block, inner

    both = ("fine", "tele")
    for cycle in range(CYCLES):
        for sweep in range(SWEEPS):
            if cycle == 0 and sweep == 0:
                continue
            outer, own, inner = halo(state, both)
            if cycle == 0 and sweep == 1:
                sent, _ = lax.optimization_barrier((coarse_inverse, outer))
                near, other = across(sent, 1), across(sent, tele_size - 1)
            outs = [((fine_rows, dofs), bf16)]
            if sweep == SWEEPS - 1:
                outs += [((fine_rows, dofs), f32), ((fine_rows, dofs), bf16)]
            result = run(
                functools.partial(sweep_kernel, blocks=1),
                outs,
                outer,
                own,
                inner,
                fine_index,
                *shared,
                right_side,
                inverse,
                held=(5, 7),
            )
            state = result[0]
            if cycle == 0 and sweep == 2:
                far_shape = ((1,) + near.shape[1:], bf16)
                far_low, far_high = run(take_kernel, [far_shape] * 2, other, near, keep=(state,))
                far_low, far_high = across(far_low, 1), across(far_high, tele_size - 1)
                blocks = (coarse_inverse, near, far_low, far_high, other)
        solution, lowered = result[1], result[2]
        parts = run(
            restrict_kernel,
            ((tele_size, coarse_rows, dofs + spare), f32),
            *halo(state, both),
            fine_index,
            *shared,
            lowered,
            target,
            lists,
            held=(5,),
        )
        parts = lax.all_to_all(parts, "tele", 0, 0, tiled=True)
        restricted, coarse, coarse_index = run(
            functools.partial(coarse_first_kernel, blocks=len(blocks)),
            [((coarse_rows, dofs), f32), ((coarse_rows, dofs), bf16), ((coarse_rows, spare), i32)],
            parts,
            *blocks,
            held=range(1, 1 + len(blocks)),
        )
        for sweep in range(SWEEPS - 2):
            coarse = run(
                functools.partial(sweep_kernel, blocks=len(blocks)),
                [((coarse_rows, dofs), bf16)],
                *halo(coarse, "fine"),
                coarse_index,
                *shared,
                restricted,
                *blocks,
                held=(5, *range(7, 7 + len(blocks))),
            )[0]
        last = cycle == CYCLES - 1
        state = run(
            functools.partial(correct_kernel, blocks=len(blocks)),
            ((fine_rows, dofs), f32 if last else bf16),
            *halo(coarse, "fine"),
            coarse_index,
            *shared,
            restricted,
            *blocks,
            target,
            solution,
            held=(5, *range(7, 7 + len(blocks))),
        )
    return state


def solution(mesh):
    both = P(("fine", "tele"))
    return jax.shard_map(
        shards,
        mesh=mesh,
        in_specs=(both, both, both, both, both, both, both, P(), both),
        out_specs=both,
        check_vma=False,
    )
```

```python
import functools

import jax
import jax.numpy as jnp
import numpy as np
from jax import lax
from jax.experimental import pallas as pl
from jax.experimental.pallas import tpu as pltpu
from jax.sharding import PartitionSpec as P

FIELDS = 5
NODES = 4
SWEEPS = 3
CYCLES = 2
LANES = 128
OPPOSITE = (1, 0, 3, 2, 5, 4)


def swapped(block, axis):
    count = lax.axis_size(axis)
    inner = lax.ppermute(block, axis, [(i, i ^ 1) for i in range(count)])
    outer = lax.ppermute(block, axis, [(i, (i - 1 if i % 2 == 0 else i + 1) % count) for i in range(count)])
    return inner, outer


def face_table():
    cube = np.arange(FIELDS * NODES**3).reshape(FIELDS, NODES, NODES, NODES)
    far = NODES - 1
    faces = (cube[:, 0], cube[:, far], cube[:, :, 0], cube[:, :, far], cube[..., 0], cube[..., far])
    table = np.zeros((6 * LANES, cube.size), np.float32)
    for k, face in enumerate(faces):
        nodes = face.reshape(-1)
        table[k * LANES + np.arange(nodes.size), nodes] = 1.0
    return table


def halves(value):
    high = value.astype(jnp.bfloat16)
    low = (value - high.astype(jnp.float32)).astype(jnp.bfloat16)
    return high, low


def exact_dot(left, right):
    high, low = halves(right)
    return jnp.dot(left, high, preferred_element_type=jnp.float32) + jnp.dot(
        left, low, preferred_element_type=jnp.float32
    )


def coupling(states, index, operators, pick, lift):
    count = states[0].shape[0]
    pool = jnp.concatenate([state.astype(jnp.float32) for state in states], axis=0).astype(jnp.bfloat16)
    traces = jnp.dot(pool, pick, preferred_element_type=jnp.float32).astype(jnp.bfloat16)
    column = lax.broadcasted_iota(jnp.int32, (count, pool.shape[0]), 1)
    face_rows, kinds = [], []
    for k in range(6):
        chosen = jnp.where(index[:, k : k + 1] == column, 1.0, 0.0).astype(jnp.bfloat16)
        across = traces[:, OPPOSITE[k] * LANES : (OPPOSITE[k] + 1) * LANES]
        face_rows.append(jnp.dot(chosen, across, preferred_element_type=jnp.float32))
        kinds.append(jnp.broadcast_to(index[:, 6 + k : 7 + k], (count, LANES)))
    face_rows = jnp.concatenate(face_rows, axis=0)
    kinds = jnp.concatenate(kinds, axis=0)
    types = operators.shape[0] // LANES
    spread = jnp.concatenate(
        [jnp.where(kinds == q, face_rows, 0.0).astype(jnp.bfloat16) for q in range(types)], axis=1
    )
    coupled = jnp.dot(spread, operators, preferred_element_type=jnp.float32)
    side_by_side = jnp.concatenate([coupled[k * count : (k + 1) * count] for k in range(6)], axis=1)
    high = side_by_side.astype(jnp.bfloat16).astype(jnp.float32)
    terms = jnp.concatenate([high, side_by_side - high], axis=0).astype(jnp.bfloat16)
    lifted = jnp.dot(terms, lift, preferred_element_type=jnp.float32)
    return lifted[:count] + lifted[count:]


def apply_inverse(blocks, vector, turned=False):
    contracted = (((1,), (0 if turned else 1,)), ((), ()))
    row = lax.broadcasted_iota(jnp.int32, vector.shape, 0)
    result = jnp.zeros(vector.shape, jnp.float32)
    first = 0
    for block in blocks:
        for e in range(block.shape[0]):
            product = lax.dot_general(vector, block[e], contracted, preferred_element_type=jnp.float32)
            result = jnp.where(row == first + e, product, result)
        first += block.shape[0]
    return result


def pool_rows(links, count, position):
    shift = count.bit_length() - 1
    owner, within = links >> shift, links & (count - 1)
    place = jnp.where(owner == position, 1, jnp.where(owner == (position ^ 1), 0, 2))
    return jnp.where(links >= 0, place * count + within, -1)


def first_kernel(*refs, count):
    sources, (state_ref, index_ref, lists_ref, operators_ref, inverse_ref) = refs[:count], refs[count : count + 5]
    targets, (sems, block_sems) = refs[count + 5 : -2], refs[-2:]
    right_ref, links_ref, faces_ref, coarse_links_ref, coarse_faces_ref, operators_in_ref = targets
    whole = [pltpu.make_async_copy(sources[i], targets[i], sems.at[i]) for i in range(count - 1)]
    step = inverse_ref.shape[0] // block_sems.shape[0]
    blocks = [
        pltpu.make_async_copy(
            sources[-1].at[i * step : (i + 1) * step], inverse_ref.at[i * step : (i + 1) * step], block_sems.at[i]
        )
        for i in range(block_sems.shape[0])
    ]
    for copy in [whole[0], *blocks, *whole[1:]]:
        copy.start()

    tele, column = lax.axis_index("tele"), lax.axis_index("fine")
    tele_size = lax.axis_size("tele")
    whole[0].wait()
    lowered = right_ref[...].astype(jnp.bfloat16)
    row = lax.broadcasted_iota(jnp.int32, lowered.shape, 0)
    result = jnp.zeros(lowered.shape, jnp.float32)
    for e in range(inverse_ref.shape[0]):
        if e % step == 0:
            blocks[e // step].wait()
        product = lax.dot_general(
            lowered, inverse_ref[e], (((1,), (1,)), ((), ())), preferred_element_type=jnp.float32
        )
        result = jnp.where(row == e, product, result)
    state_ref[...] = result.astype(jnp.bfloat16)
    for copy in whole[1:]:
        copy.wait()

    fine_rows = right_ref.shape[0]
    rows = pool_rows(links_ref[...], fine_rows, column * tele_size + tele)
    index = jnp.concatenate([rows.astype(jnp.float32), faces_ref[...].astype(jnp.float32)], axis=0)
    index_ref[...] = index.T.astype(jnp.int32)

    own = coarse_links_ref.shape[0]
    count = own * tele_size
    rows = pool_rows(coarse_links_ref[...], count, column).astype(jnp.float32)
    kinds = coarse_faces_ref[...].astype(jnp.float32)
    lists_ref[...] = jnp.zeros(lists_ref.shape, jnp.float32)
    row = lax.broadcasted_iota(jnp.int32, (count, kinds.shape[1]), 0)
    for part, values in enumerate((rows, kinds)):
        placed = jnp.zeros(row.shape, jnp.float32)
        for c in range(own):
            placed = jnp.where(row == own * tele + c, values[c : c + 1], placed)
        lists_ref[:, part * 6 : part * 6 + 6] = placed

    types, size, _ = operators_in_ref.shape
    unit = lax.broadcasted_iota(jnp.int32, (LANES, size), 0) == lax.broadcasted_iota(jnp.int32, (LANES, size), 1)
    unit = jnp.where(unit, 1.0, 0.0).astype(jnp.bfloat16)
    operators_ref[...] = jnp.zeros(operators_ref.shape, jnp.bfloat16)
    for q in range(types):
        turned = lax.dot_general(
            unit, operators_in_ref[q], (((1,), (1,)), ((), ())), preferred_element_type=jnp.float32
        )
        operators_ref[q * LANES : (q + 1) * LANES, :size] = turned.astype(jnp.bfloat16)


def turn_kernel(in_ref, out_ref):
    size = in_ref.shape[1]
    unit = lax.broadcasted_iota(jnp.int32, (size, size), 0) == lax.broadcasted_iota(jnp.int32, (size, size), 1)
    unit = jnp.where(unit, 1.0, 0.0).astype(jnp.bfloat16)
    for e in range(in_ref.shape[0]):
        turned = lax.dot_general(unit, in_ref[e], (((1,), (1,)), ((), ())), preferred_element_type=jnp.float32)
        out_ref[e] = turned.astype(jnp.bfloat16)


def take_kernel(before_ref, after_ref, low_ref, high_ref):
    low_ref[...] = before_ref[0:1]
    high_ref[...] = after_ref[1:2]


def sweep(refs, blocks, turned=False):
    prev_ref, own_ref, next_ref, index_ref, operators_ref, pick_ref, lift_ref, right_ref = refs
    states = [prev_ref[...], own_ref[...], next_ref[...]]
    coupled = coupling(states, index_ref[...], operators_ref[...], pick_ref[...], lift_ref[...])
    lowered = (right_ref[...] - coupled).astype(jnp.bfloat16)
    return apply_inverse(blocks, lowered, turned), lowered


def sweep_kernel(*refs, blocks, turned=False):
    result, lowered = sweep(refs[:8], refs[8 : 8 + blocks], turned)
    outs = refs[8 + blocks :]
    outs[0][...] = result.astype(jnp.bfloat16)
    if len(outs) > 1:
        outs[1][...] = result
        outs[2][...] = lowered


def restrict_kernel(
    prev_ref, own_ref, next_ref, index_ref, operators_ref, pick_ref, lift_ref, lowered_ref, target_ref, lists_ref, out_ref
):
    states = [prev_ref[...], own_ref[...], next_ref[...]]
    coupled = coupling(states, index_ref[...], operators_ref[...], pick_ref[...], lift_ref[...])
    residual = lowered_ref[...].astype(jnp.float32) - coupled
    tele_size, rows, dofs = out_ref.shape[0], out_ref.shape[1], residual.shape[1]
    shape = (tele_size * rows, residual.shape[0])
    row = lax.broadcasted_iota(jnp.int32, shape, 0)
    element = (row & (rows - 1)) ^ ((row >> (rows.bit_length() - 1)) * (rows // tele_size))
    member = jnp.where((target_ref[...] & (rows - 1)) == element, 1.0, 0.0).astype(jnp.bfloat16)
    partial = exact_dot(member, residual)
    own = rows // tele_size
    for t in range(tele_size):
        out_ref[t, :, :dofs] = partial[t * rows : (t + 1) * rows]
        for s in range(tele_size):
            out_ref[t, s * own : (s + 1) * own, dofs:] = lists_ref[(s ^ t) * own : ((s ^ t) + 1) * own]


def coarse_first_kernel(*refs, blocks):
    parts_ref, inverses, (restricted_ref, state_ref, index_ref) = refs[0], refs[1 : 1 + blocks], refs[1 + blocks :]
    total = parts_ref[0]
    for t in range(1, parts_ref.shape[0]):
        total = total + parts_ref[t]
    dofs = restricted_ref.shape[1]
    restricted = total[:, :dofs]
    restricted_ref[...] = restricted
    lists = total[:, dofs:].astype(jnp.int32)
    turn = lax.axis_index("tele") * (total.shape[0] // parts_ref.shape[0])
    turned = (lax.broadcasted_iota(jnp.int32, lists.shape, 1) < 6) & (lists >= 0)
    index_ref[...] = jnp.where(turned, lists ^ turn, lists)
    state_ref[...] = apply_inverse(inverses, restricted.astype(jnp.bfloat16)).astype(jnp.bfloat16)


def correct_kernel(*refs, blocks):
    coarse, _ = sweep(refs[:8], refs[8 : 8 + blocks])
    target_ref, solution_ref, out_ref = refs[8 + blocks :]
    rows, fine = coarse.shape[0], solution_ref.shape[0]
    turn = lax.axis_index("tele") * (rows // lax.axis_size("tele"))
    member = ((target_ref[...] & (rows - 1)) ^ turn) == lax.broadcasted_iota(jnp.int32, (rows, fine), 0)
    added = exact_dot(jnp.where(member, 1.0, 0.0).T.astype(jnp.bfloat16), coarse)
    out_ref[...] = (solution_ref[...] + added).astype(out_ref.dtype)


def run(kernel, outs, *operands, held=(), keep=(), hbm=(), pinned=(), scratch=()):
    count = len(operands)

    def body(*refs):
        kernel(*refs[:count], *refs[count + len(keep) :])

    single = not isinstance(outs, list)
    shapes = [outs] if single else outs
    vmem = pl.BlockSpec(memory_space=pltpu.VMEM)
    moved = sum(o.size * o.dtype.itemsize for o in operands)
    operands = [
        pltpu.with_memory_space_constraint(o, pltpu.HBM if i in hbm else pltpu.VMEM) if i in held or i in hbm else o
        for i, o in enumerate(operands)
    ]
    operands += [pltpu.with_memory_space_constraint(o, pltpu.VMEM) for o in keep]
    result = pl.pallas_call(
        body,
        out_shape=[pltpu.VMEM(s, d) if i in pinned else jax.ShapeDtypeStruct(s, d) for i, (s, d) in enumerate(shapes)],
        in_specs=[pl.BlockSpec(memory_space=pltpu.HBM) if i in hbm else vmem for i in range(len(operands))],
        out_specs=[vmem] * len(shapes),
        scratch_shapes=scratch,
        compiler_params=pltpu.CompilerParams(vmem_limit_bytes=20 << 20),
        cost_estimate=pl.CostEstimate(flops=1 << 32, bytes_accessed=moved, transcendentals=0),
    )(*operands)
    return result[0] if single else result


def shards(
    right_side,
    fine_inverse,
    fine_links,
    fine_faces,
    coarse_inverse,
    coarse_links,
    coarse_faces,
    face_operators,
    agglomerate,
):
    f32, bf16, i32 = jnp.float32, jnp.bfloat16, jnp.int32
    fine_rows, dofs = right_side.shape
    tele_size = lax.axis_size("tele")
    coarse_rows = coarse_inverse.shape[0] * tele_size
    types = face_operators.shape[0]
    spare = -dofs % LANES

    def across(block, bits):
        return lax.ppermute(block, "tele", [(i, i ^ bits) for i in range(tele_size)])

    table = face_table()
    pick, lift = jnp.asarray(table.T.copy(), bf16), jnp.asarray(table, bf16)
    target = agglomerate[None, :]
    operands = (
        right_side,
        fine_links.T,
        fine_faces.T,
        coarse_links,
        coarse_faces,
        face_operators,
        fine_inverse,
    )
    state, fine_index, lists, operators, inverse = run(
        functools.partial(first_kernel, count=len(operands)),
        [
            ((fine_rows, dofs), bf16),
            ((fine_rows, 12), i32),
            ((coarse_rows, spare), f32),
            ((types * LANES, LANES), bf16),
            (fine_inverse.shape, bf16),
        ],
        *operands,
        hbm=range(len(operands)),
        pinned=(3, 4),
        scratch=[pltpu.VMEM(o.shape, o.dtype) for o in operands[:-1]]
        + [pltpu.SemaphoreType.DMA((len(operands),)), pltpu.SemaphoreType.DMA((4,))],
    )
    shared = (operators, pick, lift)

    def halo(block, axis):
        inner, outer = swapped(block, axis)
        return inner, block, outer

    both = ("fine", "tele")
    for cycle in range(CYCLES):
        for sweep in range(SWEEPS):
            if cycle == 0 and sweep == 0:
                continue
            inner, own, outer = halo(state, both)
            if cycle == 0 and sweep == 1:
                sent, inner = lax.optimization_barrier((coarse_inverse, inner))
                near, other = across(sent, 1), across(sent, tele_size - 1)
            if cycle == 0 and sweep == 2:
                near, other, outer = lax.optimization_barrier((near, other, outer))
                far_low, far_high = run(take_kernel, [((1,) + near.shape[1:], bf16)] * 2, other, near)
                far_low, far_high = across(far_low, 1), across(far_high, tele_size - 1)
                blocks = (coarse_inverse, near, far_low, far_high, other)
            turned = (cycle, sweep) != (0, 1)
            if cycle == 0 and sweep == 2:
                inverse = run(turn_kernel, (inverse.shape, bf16), inverse, held=(0,), keep=(state,), pinned=(0,))
            outs = [((fine_rows, dofs), bf16)]
            if sweep == SWEEPS - 1:
                outs += [((fine_rows, dofs), f32), ((fine_rows, dofs), bf16)]
            result = run(
                functools.partial(sweep_kernel, blocks=1, turned=turned),
                outs,
                inner,
                own,
                outer,
                fine_index,
                *shared,
                right_side,
                inverse,
                held=(5, 6, 8),
            )
            state = result[0]
        solution, lowered = result[1], result[2]
        parts = run(
            restrict_kernel,
            ((tele_size, coarse_rows, dofs + spare), f32),
            *halo(state, both),
            fine_index,
            *shared,
            lowered,
            target,
            lists,
            held=(5, 6),
        )
        parts = lax.all_to_all(parts, "tele", 0, 0, tiled=True)
        restricted, coarse, coarse_index = run(
            functools.partial(coarse_first_kernel, blocks=len(blocks)),
            [((coarse_rows, dofs), f32), ((coarse_rows, dofs), bf16), ((coarse_rows, spare), i32)],
            parts,
            *blocks,
            held=range(1, 1 + len(blocks)),
        )
        for sweep in range(SWEEPS - 2):
            coarse = run(
                functools.partial(sweep_kernel, blocks=len(blocks)),
                [((coarse_rows, dofs), bf16)],
                *halo(coarse, "fine"),
                coarse_index,
                *shared,
                restricted,
                *blocks,
                held=(5, 6, *range(8, 8 + len(blocks))),
            )[0]
        last = cycle == CYCLES - 1
        state = run(
            functools.partial(correct_kernel, blocks=len(blocks)),
            ((fine_rows, dofs), f32 if last else bf16),
            *halo(coarse, "fine"),
            coarse_index,
            *shared,
            restricted,
            *blocks,
            target,
            solution,
            held=(5, 6, *range(8, 8 + len(blocks))),
        )
    return state


def solution(mesh):
    both = P(("fine", "tele"))
    return jax.shard_map(
        shards,
        mesh=mesh,
        in_specs=(both, both, both, both, both, both, both, P(), both),
        out_specs=both,
        check_vma=False,
    )
```

```python
import functools

import jax
import jax.numpy as jnp
import numpy as np
from jax import lax
from jax.experimental import pallas as pl
from jax.experimental.pallas import tpu as pltpu
from jax.sharding import PartitionSpec as P

FIELDS = 5
NODES = 4
SWEEPS = 3
CYCLES = 2
LANES = 128
OPPOSITE = (1, 0, 3, 2, 5, 4)


def swapped(block, axis):
    count = lax.axis_size(axis)
    inner = lax.ppermute(block, axis, [(i, i ^ 1) for i in range(count)])
    outer = lax.ppermute(block, axis, [(i, (i - 1 if i % 2 == 0 else i + 1) % count) for i in range(count)])
    return inner, outer


def face_table():
    cube = np.arange(FIELDS * NODES**3).reshape(FIELDS, NODES, NODES, NODES)
    far = NODES - 1
    faces = (cube[:, 0], cube[:, far], cube[:, :, 0], cube[:, :, far], cube[..., 0], cube[..., far])
    table = np.zeros((6 * LANES, cube.size), np.float32)
    for k, face in enumerate(faces):
        nodes = face.reshape(-1)
        table[k * LANES + np.arange(nodes.size), nodes] = 1.0
    return table


def halves(value):
    high = value.astype(jnp.bfloat16)
    low = (value - high.astype(jnp.float32)).astype(jnp.bfloat16)
    return high, low


def exact_dot(left, right):
    high, low = halves(right)
    return jnp.dot(left, high, preferred_element_type=jnp.float32) + jnp.dot(
        left, low, preferred_element_type=jnp.float32
    )


def coupling(states, index, operators, pick, lift):
    count = states[0].shape[0]
    pool = jnp.concatenate([state.astype(jnp.float32) for state in states], axis=0).astype(jnp.bfloat16)
    traces = jnp.dot(pool, pick, preferred_element_type=jnp.float32).astype(jnp.bfloat16)
    column = lax.broadcasted_iota(jnp.int32, (count, pool.shape[0]), 1)
    face_rows, kinds = [], []
    for k in range(6):
        chosen = jnp.where(index[:, k : k + 1] == column, 1.0, 0.0).astype(jnp.bfloat16)
        across = traces[:, OPPOSITE[k] * LANES : (OPPOSITE[k] + 1) * LANES]
        face_rows.append(jnp.dot(chosen, across, preferred_element_type=jnp.float32))
        kinds.append(jnp.broadcast_to(index[:, 6 + k : 7 + k], (count, LANES)))
    face_rows = jnp.concatenate(face_rows, axis=0)
    kinds = jnp.concatenate(kinds, axis=0)
    types = operators.shape[0] // LANES
    spread = jnp.concatenate(
        [jnp.where(kinds == q, face_rows, 0.0).astype(jnp.bfloat16) for q in range(types)], axis=1
    )
    coupled = jnp.dot(spread, operators, preferred_element_type=jnp.float32)
    side_by_side = jnp.concatenate([coupled[k * count : (k + 1) * count] for k in range(6)], axis=1)
    high = side_by_side.astype(jnp.bfloat16).astype(jnp.float32)
    terms = jnp.concatenate([high, side_by_side - high], axis=0).astype(jnp.bfloat16)
    lifted = jnp.dot(terms, lift, preferred_element_type=jnp.float32)
    return lifted[:count] + lifted[count:]


def apply_inverse(blocks, vector, turned=False):
    contracted = (((1,), (0 if turned else 1,)), ((), ()))
    row = lax.broadcasted_iota(jnp.int32, vector.shape, 0)
    result = jnp.zeros(vector.shape, jnp.float32)
    first = 0
    for block in blocks:
        for e in range(block.shape[0]):
            product = lax.dot_general(vector, block[e], contracted, preferred_element_type=jnp.float32)
            result = jnp.where(row == first + e, product, result)
        first += block.shape[0]
    return result


def pool_rows(links, count, position):
    shift = count.bit_length() - 1
    owner, within = links >> shift, links & (count - 1)
    place = jnp.where(owner == position, 1, jnp.where(owner == (position ^ 1), 0, 2))
    return jnp.where(links >= 0, place * count + within, -1)


def first_kernel(*refs, count):
    sources, (state_ref, index_ref, lists_ref, operators_ref, inverse_ref) = refs[:count], refs[count : count + 5]
    targets, (sems, block_sems) = refs[count + 5 : -2], refs[-2:]
    right_ref, links_ref, faces_ref, coarse_links_ref, coarse_faces_ref, operators_in_ref = targets
    whole = [pltpu.make_async_copy(sources[i], targets[i], sems.at[i]) for i in range(count - 1)]
    step = inverse_ref.shape[0] // block_sems.shape[0]
    blocks = [
        pltpu.make_async_copy(
            sources[-1].at[i * step : (i + 1) * step], inverse_ref.at[i * step : (i + 1) * step], block_sems.at[i]
        )
        for i in range(block_sems.shape[0])
    ]
    for copy in [whole[0], *blocks, *whole[1:]]:
        copy.start()

    tele, column = lax.axis_index("tele"), lax.axis_index("fine")
    tele_size = lax.axis_size("tele")
    whole[0].wait()
    lowered = right_ref[...].astype(jnp.bfloat16)
    row = lax.broadcasted_iota(jnp.int32, lowered.shape, 0)
    result = jnp.zeros(lowered.shape, jnp.float32)
    for e in range(inverse_ref.shape[0]):
        if e % step == 0:
            blocks[e // step].wait()
        product = lax.dot_general(
            lowered, inverse_ref[e], (((1,), (1,)), ((), ())), preferred_element_type=jnp.float32
        )
        result = jnp.where(row == e, product, result)
    state_ref[...] = result.astype(jnp.bfloat16)
    for copy in whole[1:]:
        copy.wait()

    fine_rows = right_ref.shape[0]
    rows = pool_rows(links_ref[...], fine_rows, column * tele_size + tele)
    index = jnp.concatenate([rows.astype(jnp.float32), faces_ref[...].astype(jnp.float32)], axis=0)
    index_ref[...] = index.T.astype(jnp.int32)

    own = coarse_links_ref.shape[0]
    count = own * tele_size
    rows = pool_rows(coarse_links_ref[...], count, column).astype(jnp.float32)
    kinds = coarse_faces_ref[...].astype(jnp.float32)
    lists_ref[...] = jnp.zeros(lists_ref.shape, jnp.float32)
    row = lax.broadcasted_iota(jnp.int32, (count, kinds.shape[1]), 0)
    for part, values in enumerate((rows, kinds)):
        placed = jnp.zeros(row.shape, jnp.float32)
        for c in range(own):
            placed = jnp.where(row == own * tele + c, values[c : c + 1], placed)
        lists_ref[:, part * 6 : part * 6 + 6] = placed

    types, size, _ = operators_in_ref.shape
    unit = lax.broadcasted_iota(jnp.int32, (LANES, size), 0) == lax.broadcasted_iota(jnp.int32, (LANES, size), 1)
    unit = jnp.where(unit, 1.0, 0.0).astype(jnp.bfloat16)
    operators_ref[...] = jnp.zeros(operators_ref.shape, jnp.bfloat16)
    for q in range(types):
        turned = lax.dot_general(
            unit, operators_in_ref[q], (((1,), (1,)), ((), ())), preferred_element_type=jnp.float32
        )
        operators_ref[q * LANES : (q + 1) * LANES, :size] = turned.astype(jnp.bfloat16)


def turn_kernel(*refs):
    out_ref = refs[-1]
    size = out_ref.shape[1]
    unit = lax.broadcasted_iota(jnp.int32, (size, size), 0) == lax.broadcasted_iota(jnp.int32, (size, size), 1)
    unit = jnp.where(unit, 1.0, 0.0).astype(jnp.bfloat16)
    blocks = [(ref, e) for ref in refs[:-1] for e in range(ref.shape[0])]
    for place, (ref, e) in enumerate(blocks):
        turned = lax.dot_general(unit, ref[e], (((1,), (1,)), ((), ())), preferred_element_type=jnp.float32)
        out_ref[place] = turned.astype(jnp.bfloat16)


def take_kernel(before_ref, after_ref, low_ref, high_ref):
    low_ref[...] = before_ref[0:1]
    high_ref[...] = after_ref[1:2]


def sweep(refs, blocks, turned=False):
    prev_ref, own_ref, next_ref, index_ref, operators_ref, pick_ref, lift_ref, right_ref = refs
    states = [prev_ref[...], own_ref[...], next_ref[...]]
    coupled = coupling(states, index_ref[...], operators_ref[...], pick_ref[...], lift_ref[...])
    lowered = (right_ref[...] - coupled).astype(jnp.bfloat16)
    return apply_inverse(blocks, lowered, turned), lowered


def sweep_kernel(*refs, blocks, turned=False):
    result, lowered = sweep(refs[:8], refs[8 : 8 + blocks], turned)
    outs = refs[8 + blocks :]
    outs[0][...] = result.astype(jnp.bfloat16)
    if len(outs) > 1:
        outs[1][...] = result
        outs[2][...] = lowered


def restrict_kernel(
    prev_ref, own_ref, next_ref, index_ref, operators_ref, pick_ref, lift_ref, lowered_ref, target_ref, lists_ref, out_ref
):
    states = [prev_ref[...], own_ref[...], next_ref[...]]
    coupled = coupling(states, index_ref[...], operators_ref[...], pick_ref[...], lift_ref[...])
    residual = lowered_ref[...].astype(jnp.float32) - coupled
    tele_size, rows, dofs = out_ref.shape[0], out_ref.shape[1], residual.shape[1]
    shape = (tele_size * rows, residual.shape[0])
    row = lax.broadcasted_iota(jnp.int32, shape, 0)
    element = (row & (rows - 1)) ^ ((row >> (rows.bit_length() - 1)) * (rows // tele_size))
    member = jnp.where((target_ref[...] & (rows - 1)) == element, 1.0, 0.0).astype(jnp.bfloat16)
    partial = exact_dot(member, residual)
    own = rows // tele_size
    for t in range(tele_size):
        out_ref[t, :, :dofs] = partial[t * rows : (t + 1) * rows]
        for s in range(tele_size):
            out_ref[t, s * own : (s + 1) * own, dofs:] = lists_ref[(s ^ t) * own : ((s ^ t) + 1) * own]


def coarse_first_kernel(*refs, blocks, turned):
    parts_ref, inverses, (restricted_ref, state_ref, index_ref) = refs[0], refs[1 : 1 + blocks], refs[1 + blocks :]
    total = parts_ref[0]
    for t in range(1, parts_ref.shape[0]):
        total = total + parts_ref[t]
    dofs = restricted_ref.shape[1]
    restricted = total[:, :dofs]
    restricted_ref[...] = restricted
    lists = total[:, dofs:].astype(jnp.int32)
    turn = lax.axis_index("tele") * (total.shape[0] // parts_ref.shape[0])
    moved = (lax.broadcasted_iota(jnp.int32, lists.shape, 1) < 6) & (lists >= 0)
    index_ref[...] = jnp.where(moved, lists ^ turn, lists)
    state_ref[...] = apply_inverse(inverses, restricted.astype(jnp.bfloat16), turned).astype(jnp.bfloat16)


def correct_kernel(*refs, blocks):
    coarse, _ = sweep(refs[:8], refs[8 : 8 + blocks], True)
    target_ref, solution_ref, out_ref = refs[8 + blocks :]
    rows, fine = coarse.shape[0], solution_ref.shape[0]
    turn = lax.axis_index("tele") * (rows // lax.axis_size("tele"))
    member = ((target_ref[...] & (rows - 1)) ^ turn) == lax.broadcasted_iota(jnp.int32, (rows, fine), 0)
    added = exact_dot(jnp.where(member, 1.0, 0.0).T.astype(jnp.bfloat16), coarse)
    out_ref[...] = (solution_ref[...] + added).astype(out_ref.dtype)


def run(kernel, outs, *operands, held=(), keep=(), hbm=(), pinned=(), scratch=()):
    count = len(operands)

    def body(*refs):
        kernel(*refs[:count], *refs[count + len(keep) :])

    single = not isinstance(outs, list)
    shapes = [outs] if single else outs
    vmem = pl.BlockSpec(memory_space=pltpu.VMEM)
    moved = sum(o.size * o.dtype.itemsize for o in operands)
    operands = [
        pltpu.with_memory_space_constraint(o, pltpu.HBM if i in hbm else pltpu.VMEM) if i in held or i in hbm else o
        for i, o in enumerate(operands)
    ]
    operands += [pltpu.with_memory_space_constraint(o, pltpu.VMEM) for o in keep]
    result = pl.pallas_call(
        body,
        out_shape=[pltpu.VMEM(s, d) if i in pinned else jax.ShapeDtypeStruct(s, d) for i, (s, d) in enumerate(shapes)],
        in_specs=[pl.BlockSpec(memory_space=pltpu.HBM) if i in hbm else vmem for i in range(len(operands))],
        out_specs=[vmem] * len(shapes),
        scratch_shapes=scratch,
        compiler_params=pltpu.CompilerParams(vmem_limit_bytes=20 << 20),
        cost_estimate=pl.CostEstimate(flops=1 << 32, bytes_accessed=moved, transcendentals=0),
    )(*operands)
    return result[0] if single else result


def shards(
    right_side,
    fine_inverse,
    fine_links,
    fine_faces,
    coarse_inverse,
    coarse_links,
    coarse_faces,
    face_operators,
    agglomerate,
):
    f32, bf16, i32 = jnp.float32, jnp.bfloat16, jnp.int32
    fine_rows, dofs = right_side.shape
    tele_size = lax.axis_size("tele")
    coarse_rows = coarse_inverse.shape[0] * tele_size
    types = face_operators.shape[0]
    spare = -dofs % LANES

    def across(block, bits):
        return lax.ppermute(block, "tele", [(i, i ^ bits) for i in range(tele_size)])

    table = face_table()
    pick, lift = jnp.asarray(table.T.copy(), bf16), jnp.asarray(table, bf16)
    target = agglomerate[None, :]
    operands = (
        right_side,
        fine_links.T,
        fine_faces.T,
        coarse_links,
        coarse_faces,
        face_operators,
        fine_inverse,
    )
    state, fine_index, lists, operators, inverse = run(
        functools.partial(first_kernel, count=len(operands)),
        [
            ((fine_rows, dofs), bf16),
            ((fine_rows, 12), i32),
            ((coarse_rows, spare), f32),
            ((types * LANES, LANES), bf16),
            (fine_inverse.shape, bf16),
        ],
        *operands,
        hbm=range(len(operands)),
        pinned=(3, 4),
        scratch=[pltpu.VMEM(o.shape, o.dtype) for o in operands[:-1]]
        + [pltpu.SemaphoreType.DMA((len(operands),)), pltpu.SemaphoreType.DMA((4,))],
    )
    shared = (operators, pick, lift)

    def halo(block, axis):
        inner, outer = swapped(block, axis)
        return inner, block, outer

    both = ("fine", "tele")
    for cycle in range(CYCLES):
        for sweep in range(SWEEPS):
            if cycle == 0 and sweep == 0:
                continue
            inner, own, outer = halo(state, both)
            if cycle == 0 and sweep == 1:
                sent, inner = lax.optimization_barrier((coarse_inverse, inner))
                near, other = across(sent, 1), across(sent, tele_size - 1)
            if cycle == 0 and sweep == 2:
                near, other, outer = lax.optimization_barrier((near, other, outer))
                far_low, far_high = run(take_kernel, [((1,) + near.shape[1:], bf16)] * 2, other, near)
                far_low, far_high = across(far_low, 1), across(far_high, tele_size - 1)
                blocks = (coarse_inverse, near, far_low, far_high, other)
            turned = (cycle, sweep) != (0, 1)
            if cycle == 0 and sweep == 2:
                inverse = run(turn_kernel, (inverse.shape, bf16), inverse, held=(0,), keep=(state,), pinned=(0,))
            outs = [((fine_rows, dofs), bf16)]
            if sweep == SWEEPS - 1:
                outs += [((fine_rows, dofs), f32), ((fine_rows, dofs), bf16)]
            result = run(
                functools.partial(sweep_kernel, blocks=1, turned=turned),
                outs,
                inner,
                own,
                outer,
                fine_index,
                *shared,
                right_side,
                inverse,
                held=(5, 6, 8),
            )
            state = result[0]
        solution, lowered = result[1], result[2]
        parts = run(
            restrict_kernel,
            ((tele_size, coarse_rows, dofs + spare), f32),
            *halo(state, both),
            fine_index,
            *shared,
            lowered,
            target,
            lists,
            held=(5, 6),
        )
        parts = lax.all_to_all(parts, "tele", 0, 0, tiled=True)
        restricted, coarse, coarse_index = run(
            functools.partial(coarse_first_kernel, blocks=len(blocks), turned=cycle > 0),
            [((coarse_rows, dofs), f32), ((coarse_rows, dofs), bf16), ((coarse_rows, spare), i32)],
            parts,
            *blocks,
            held=range(1, 1 + len(blocks)),
        )
        if cycle == 0:
            turned_shape = ((coarse_rows, dofs, dofs), bf16)
            held = range(len(blocks))
            blocks = (run(turn_kernel, turned_shape, *blocks, held=held, keep=(coarse,), pinned=(0,)),)
        for sweep in range(SWEEPS - 2):
            coarse = run(
                functools.partial(sweep_kernel, blocks=len(blocks), turned=True),
                [((coarse_rows, dofs), bf16)],
                *halo(coarse, "fine"),
                coarse_index,
                *shared,
                restricted,
                *blocks,
                held=(5, 6, *range(8, 8 + len(blocks))),
            )[0]
        last = cycle == CYCLES - 1
        state = run(
            functools.partial(correct_kernel, blocks=len(blocks)),
            ((fine_rows, dofs), f32 if last else bf16),
            *halo(coarse, "fine"),
            coarse_index,
            *shared,
            restricted,
            *blocks,
            target,
            solution,
            held=(5, 6, *range(8, 8 + len(blocks))),
        )
    return state


def solution(mesh):
    both = P(("fine", "tele"))
    return jax.shard_map(
        shards,
        mesh=mesh,
        in_specs=(both, both, both, both, both, both, both, P(), both),
        out_specs=both,
        check_vma=False,
    )
```

```python
import functools

import jax
import jax.numpy as jnp
import numpy as np
from jax import lax
from jax.experimental import pallas as pl
from jax.experimental.pallas import tpu as pltpu
from jax.sharding import PartitionSpec as P

FIELDS = 5
NODES = 4
SWEEPS = 3
CYCLES = 2
LANES = 128
OPPOSITE = (1, 0, 3, 2, 5, 4)


def swapped(block, axis, wide=None):
    count = lax.axis_size(axis)
    inner = lax.ppermute(block, axis, [(i, i ^ 1) for i in range(count)])
    wide = block if wide is None else wide
    outer = lax.ppermute(wide, axis, [(i, (i - 1 if i % 2 == 0 else i + 1) % count) for i in range(count)])
    return inner, outer


def face_table():
    cube = np.arange(FIELDS * NODES**3).reshape(FIELDS, NODES, NODES, NODES)
    far = NODES - 1
    faces = (cube[:, 0], cube[:, far], cube[:, :, 0], cube[:, :, far], cube[..., 0], cube[..., far])
    table = np.zeros((6 * LANES, cube.size), np.float32)
    for k, face in enumerate(faces):
        nodes = face.reshape(-1)
        table[k * LANES + np.arange(nodes.size), nodes] = 1.0
    return table


def halves(value):
    high = value.astype(jnp.bfloat16)
    low = (value - high.astype(jnp.float32)).astype(jnp.bfloat16)
    return high, low


def exact_dot(left, right):
    high, low = halves(right)
    return jnp.dot(left, high, preferred_element_type=jnp.float32) + jnp.dot(
        left, low, preferred_element_type=jnp.float32
    )


def coupling(states, index, operators, pick, lift):
    count = states[0].shape[0]
    pool = jnp.concatenate([state.astype(jnp.float32) for state in states], axis=0).astype(jnp.bfloat16)
    traces = jnp.dot(pool, pick, preferred_element_type=jnp.float32).astype(jnp.bfloat16)
    column = lax.broadcasted_iota(jnp.int32, (count, pool.shape[0]), 1)
    face_rows, kinds = [], []
    for k in range(6):
        chosen = jnp.where(index[:, k : k + 1] == column, 1.0, 0.0).astype(jnp.bfloat16)
        across = traces[:, OPPOSITE[k] * LANES : (OPPOSITE[k] + 1) * LANES]
        face_rows.append(jnp.dot(chosen, across, preferred_element_type=jnp.float32))
        kinds.append(jnp.broadcast_to(index[:, 6 + k : 7 + k], (count, LANES)))
    face_rows = jnp.concatenate(face_rows, axis=0)
    kinds = jnp.concatenate(kinds, axis=0)
    types = operators.shape[0] // LANES
    spread = jnp.concatenate(
        [jnp.where(kinds == q, face_rows, 0.0).astype(jnp.bfloat16) for q in range(types)], axis=1
    )
    coupled = jnp.dot(spread, operators, preferred_element_type=jnp.float32)
    side_by_side = jnp.concatenate([coupled[k * count : (k + 1) * count] for k in range(6)], axis=1)
    high = side_by_side.astype(jnp.bfloat16).astype(jnp.float32)
    terms = jnp.concatenate([high, side_by_side - high], axis=0).astype(jnp.bfloat16)
    lifted = jnp.dot(terms, lift, preferred_element_type=jnp.float32)
    return lifted[:count] + lifted[count:]


def apply_inverse(blocks, vector, turned=False):
    contracted = (((1,), (0 if turned else 1,)), ((), ()))
    row = lax.broadcasted_iota(jnp.int32, vector.shape, 0)
    result = jnp.zeros(vector.shape, jnp.float32)
    first = 0
    for block in blocks:
        for e in range(block.shape[0]):
            product = lax.dot_general(vector, block[e], contracted, preferred_element_type=jnp.float32)
            result = jnp.where(row == first + e, product, result)
        first += block.shape[0]
    return result


def pool_rows(links, count, position):
    shift = count.bit_length() - 1
    owner, within = links >> shift, links & (count - 1)
    place = jnp.where(owner == position, 1, jnp.where(owner == (position ^ 1), 0, 2))
    return jnp.where(links >= 0, place * count + within, -1)


def first_kernel(*refs, count):
    sources, (state_ref, index_ref, lists_ref, operators_ref, inverse_ref, wide_ref) = refs[:count], refs[count : count + 6]
    targets, (sems, block_sems) = refs[count + 6 : -2], refs[-2:]
    right_ref, links_ref, faces_ref, coarse_links_ref, coarse_faces_ref, operators_in_ref = targets
    whole = [pltpu.make_async_copy(sources[i], targets[i], sems.at[i]) for i in range(count - 1)]
    step = inverse_ref.shape[0] // block_sems.shape[0]
    blocks = [
        pltpu.make_async_copy(
            sources[-1].at[i * step : (i + 1) * step], inverse_ref.at[i * step : (i + 1) * step], block_sems.at[i]
        )
        for i in range(block_sems.shape[0])
    ]
    for copy in [whole[0], *blocks, *whole[1:]]:
        copy.start()

    tele, column = lax.axis_index("tele"), lax.axis_index("fine")
    tele_size = lax.axis_size("tele")
    whole[0].wait()
    lowered = right_ref[...].astype(jnp.bfloat16)
    row = lax.broadcasted_iota(jnp.int32, lowered.shape, 0)
    result = jnp.zeros(lowered.shape, jnp.float32)
    for e in range(inverse_ref.shape[0]):
        if e % step == 0:
            blocks[e // step].wait()
        product = lax.dot_general(
            lowered, inverse_ref[e], (((1,), (1,)), ((), ())), preferred_element_type=jnp.float32
        )
        result = jnp.where(row == e, product, result)
    state_ref[...] = result.astype(jnp.bfloat16)
    wide_ref[...] = jnp.zeros(wide_ref.shape, jnp.bfloat16)
    wide_ref[: result.shape[0]] = result.astype(jnp.bfloat16)
    for copy in whole[1:]:
        copy.wait()

    fine_rows = right_ref.shape[0]
    rows = pool_rows(links_ref[...], fine_rows, column * tele_size + tele)
    index = jnp.concatenate([rows.astype(jnp.float32), faces_ref[...].astype(jnp.float32)], axis=0)
    index_ref[...] = index.T.astype(jnp.int32)

    own = coarse_links_ref.shape[0]
    count = own * tele_size
    rows = pool_rows(coarse_links_ref[...], count, column).astype(jnp.float32)
    kinds = coarse_faces_ref[...].astype(jnp.float32)
    lists_ref[...] = jnp.zeros(lists_ref.shape, jnp.float32)
    row = lax.broadcasted_iota(jnp.int32, (count, kinds.shape[1]), 0)
    for part, values in enumerate((rows, kinds)):
        placed = jnp.zeros(row.shape, jnp.float32)
        for c in range(own):
            placed = jnp.where(row == own * tele + c, values[c : c + 1], placed)
        lists_ref[:, part * 6 : part * 6 + 6] = placed

    types, size, _ = operators_in_ref.shape
    unit = lax.broadcasted_iota(jnp.int32, (LANES, size), 0) == lax.broadcasted_iota(jnp.int32, (LANES, size), 1)
    unit = jnp.where(unit, 1.0, 0.0).astype(jnp.bfloat16)
    operators_ref[...] = jnp.zeros(operators_ref.shape, jnp.bfloat16)
    for q in range(types):
        turned = lax.dot_general(
            unit, operators_in_ref[q], (((1,), (1,)), ((), ())), preferred_element_type=jnp.float32
        )
        operators_ref[q * LANES : (q + 1) * LANES, :size] = turned.astype(jnp.bfloat16)


def turn_kernel(*refs):
    out_ref = refs[-1]
    size = out_ref.shape[1]
    unit = lax.broadcasted_iota(jnp.int32, (size, size), 0) == lax.broadcasted_iota(jnp.int32, (size, size), 1)
    unit = jnp.where(unit, 1.0, 0.0).astype(jnp.bfloat16)
    blocks = [(ref, e) for ref in refs[:-1] for e in range(ref.shape[0])]
    for place, (ref, e) in enumerate(blocks):
        turned = lax.dot_general(unit, ref[e], (((1,), (1,)), ((), ())), preferred_element_type=jnp.float32)
        out_ref[place] = turned.astype(jnp.bfloat16)


def take_kernel(before_ref, after_ref, low_ref, high_ref):
    low_ref[...] = before_ref[0:1]
    high_ref[...] = after_ref[1:2]


def sweep(refs, blocks, turned=False):
    prev_ref, own_ref, next_ref, index_ref, operators_ref, pick_ref, lift_ref, right_ref = refs
    states = [prev_ref[...], own_ref[...], next_ref[: own_ref.shape[0]]]
    coupled = coupling(states, index_ref[...], operators_ref[...], pick_ref[...], lift_ref[...])
    lowered = (right_ref[...] - coupled).astype(jnp.bfloat16)
    return apply_inverse(blocks, lowered, turned), lowered


def sweep_kernel(*refs, blocks, turned=False):
    result, lowered = sweep(refs[:8], refs[8 : 8 + blocks], turned)
    outs = refs[8 + blocks :]
    outs[0][...] = result.astype(jnp.bfloat16)
    if len(outs) > 1:
        outs[1][...] = result
        outs[2][...] = lowered


def restrict_kernel(
    prev_ref, own_ref, next_ref, index_ref, operators_ref, pick_ref, lift_ref, lowered_ref, target_ref, lists_ref, out_ref
):
    states = [prev_ref[...], own_ref[...], next_ref[...]]
    coupled = coupling(states, index_ref[...], operators_ref[...], pick_ref[...], lift_ref[...])
    residual = lowered_ref[...].astype(jnp.float32) - coupled
    tele_size, rows, dofs = out_ref.shape[0], out_ref.shape[1], residual.shape[1]
    shape = (tele_size * rows, residual.shape[0])
    row = lax.broadcasted_iota(jnp.int32, shape, 0)
    element = (row & (rows - 1)) ^ ((row >> (rows.bit_length() - 1)) * (rows // tele_size))
    member = jnp.where((target_ref[...] & (rows - 1)) == element, 1.0, 0.0).astype(jnp.bfloat16)
    partial = exact_dot(member, residual)
    own = rows // tele_size
    for t in range(tele_size):
        out_ref[t, :, :dofs] = partial[t * rows : (t + 1) * rows]
        for s in range(tele_size):
            out_ref[t, s * own : (s + 1) * own, dofs:] = lists_ref[(s ^ t) * own : ((s ^ t) + 1) * own]


def coarse_first_kernel(*refs, blocks, turned):
    parts_ref, inverses, (restricted_ref, state_ref, index_ref) = refs[0], refs[1 : 1 + blocks], refs[1 + blocks :]
    total = parts_ref[0]
    for t in range(1, parts_ref.shape[0]):
        total = total + parts_ref[t]
    dofs = restricted_ref.shape[1]
    restricted = total[:, :dofs]
    restricted_ref[...] = restricted
    lists = total[:, dofs:].astype(jnp.int32)
    turn = lax.axis_index("tele") * (total.shape[0] // parts_ref.shape[0])
    moved = (lax.broadcasted_iota(jnp.int32, lists.shape, 1) < 6) & (lists >= 0)
    index_ref[...] = jnp.where(moved, lists ^ turn, lists)
    state_ref[...] = apply_inverse(inverses, restricted.astype(jnp.bfloat16), turned).astype(jnp.bfloat16)


def correct_kernel(*refs, blocks):
    coarse, _ = sweep(refs[:8], refs[8 : 8 + blocks], True)
    target_ref, solution_ref, out_ref = refs[8 + blocks :]
    rows, fine = coarse.shape[0], solution_ref.shape[0]
    turn = lax.axis_index("tele") * (rows // lax.axis_size("tele"))
    member = ((target_ref[...] & (rows - 1)) ^ turn) == lax.broadcasted_iota(jnp.int32, (rows, fine), 0)
    added = exact_dot(jnp.where(member, 1.0, 0.0).T.astype(jnp.bfloat16), coarse)
    out_ref[...] = (solution_ref[...] + added).astype(out_ref.dtype)


def run(kernel, outs, *operands, held=(), keep=(), hbm=(), pinned=(), scratch=()):
    count = len(operands)

    def body(*refs):
        kernel(*refs[:count], *refs[count + len(keep) :])

    single = not isinstance(outs, list)
    shapes = [outs] if single else outs
    vmem = pl.BlockSpec(memory_space=pltpu.VMEM)
    moved = sum(o.size * o.dtype.itemsize for o in operands)
    operands = [
        pltpu.with_memory_space_constraint(o, pltpu.HBM if i in hbm else pltpu.VMEM) if i in held or i in hbm else o
        for i, o in enumerate(operands)
    ]
    operands += [pltpu.with_memory_space_constraint(o, pltpu.VMEM) for o in keep]
    result = pl.pallas_call(
        body,
        out_shape=[pltpu.VMEM(s, d) if i in pinned else jax.ShapeDtypeStruct(s, d) for i, (s, d) in enumerate(shapes)],
        in_specs=[pl.BlockSpec(memory_space=pltpu.HBM) if i in hbm else vmem for i in range(len(operands))],
        out_specs=[vmem] * len(shapes),
        scratch_shapes=scratch,
        compiler_params=pltpu.CompilerParams(vmem_limit_bytes=20 << 20),
        cost_estimate=pl.CostEstimate(flops=1 << 32, bytes_accessed=moved, transcendentals=0),
    )(*operands)
    return result[0] if single else result


def shards(
    right_side,
    fine_inverse,
    fine_links,
    fine_faces,
    coarse_inverse,
    coarse_links,
    coarse_faces,
    face_operators,
    agglomerate,
):
    f32, bf16, i32 = jnp.float32, jnp.bfloat16, jnp.int32
    fine_rows, dofs = right_side.shape
    tele_size = lax.axis_size("tele")
    coarse_rows = coarse_inverse.shape[0] * tele_size
    types = face_operators.shape[0]
    spare = -dofs % LANES

    def across(block, bits):
        return lax.ppermute(block, "tele", [(i, i ^ bits) for i in range(tele_size)])

    table = face_table()
    pick, lift = jnp.asarray(table.T.copy(), bf16), jnp.asarray(table, bf16)
    target = agglomerate[None, :]
    operands = (
        right_side,
        fine_links.T,
        fine_faces.T,
        coarse_links,
        coarse_faces,
        face_operators,
        fine_inverse,
    )
    state, fine_index, lists, operators, inverse, wide = run(
        functools.partial(first_kernel, count=len(operands)),
        [
            ((fine_rows, dofs), bf16),
            ((fine_rows, 12), i32),
            ((coarse_rows, spare), f32),
            ((types * LANES, LANES), bf16),
            (fine_inverse.shape, bf16),
            ((2 * fine_rows, dofs), bf16),
        ],
        *operands,
        hbm=range(len(operands)),
        pinned=(3, 4),
        scratch=[pltpu.VMEM(o.shape, o.dtype) for o in operands[:-1]]
        + [pltpu.SemaphoreType.DMA((len(operands),)), pltpu.SemaphoreType.DMA((4,))],
    )
    shared = (operators, pick, lift)

    def halo(block, axis, wide=None):
        inner, outer = swapped(block, axis, wide)
        return inner, block, outer

    both = ("fine", "tele")
    for cycle in range(CYCLES):
        for sweep in range(SWEEPS):
            if cycle == 0 and sweep == 0:
                continue
            inner, own, outer = halo(state, both, wide if (cycle, sweep) == (0, 1) else None)
            if cycle == 0 and sweep == 1:
                sent, inner = lax.optimization_barrier((coarse_inverse, inner))
                near, other = across(sent, 1), across(sent, tele_size - 1)
            if cycle == 0 and sweep == 2:
                near, other, outer = lax.optimization_barrier((near, other, outer))
                far_low, far_high = run(take_kernel, [((1,) + near.shape[1:], bf16)] * 2, other, near)
                far_low, far_high = across(far_low, 1), across(far_high, tele_size - 1)
                blocks = (coarse_inverse, near, far_low, far_high, other)
            turned = (cycle, sweep) != (0, 1)
            if cycle == 0 and sweep == 2:
                inverse = run(turn_kernel, (inverse.shape, bf16), inverse, held=(0,), keep=(state,), pinned=(0,))
            outs = [((fine_rows, dofs), bf16)]
            if sweep == SWEEPS - 1:
                outs += [((fine_rows, dofs), f32), ((fine_rows, dofs), bf16)]
            result = run(
                functools.partial(sweep_kernel, blocks=1, turned=turned),
                outs,
                inner,
                own,
                outer,
                fine_index,
                *shared,
                right_side,
                inverse,
                held=(5, 6, 8),
            )
            state = result[0]
        solution, lowered = result[1], result[2]
        parts = run(
            restrict_kernel,
            ((tele_size, coarse_rows, dofs + spare), f32),
            *halo(state, both),
            fine_index,
            *shared,
            lowered,
            target,
            lists,
            held=(5, 6),
        )
        parts = lax.all_to_all(parts, "tele", 0, 0, tiled=True)
        restricted, coarse, coarse_index = run(
            functools.partial(coarse_first_kernel, blocks=len(blocks), turned=cycle > 0),
            [((coarse_rows, dofs), f32), ((coarse_rows, dofs), bf16), ((coarse_rows, spare), i32)],
            parts,
            *blocks,
            held=range(1, 1 + len(blocks)),
        )
        if cycle == 0:
            turned_shape = ((coarse_rows, dofs, dofs), bf16)
            held = range(len(blocks))
            blocks = (run(turn_kernel, turned_shape, *blocks, held=held, keep=(coarse,), pinned=(0,)),)
        for sweep in range(SWEEPS - 2):
            coarse = run(
                functools.partial(sweep_kernel, blocks=len(blocks), turned=True),
                [((coarse_rows, dofs), bf16)],
                *halo(coarse, "fine"),
                coarse_index,
                *shared,
                restricted,
                *blocks,
                held=(5, 6, *range(8, 8 + len(blocks))),
            )[0]
        last = cycle == CYCLES - 1
        state = run(
            functools.partial(correct_kernel, blocks=len(blocks)),
            ((fine_rows, dofs), f32 if last else bf16),
            *halo(coarse, "fine"),
            coarse_index,
            *shared,
            restricted,
            *blocks,
            target,
            solution,
            held=(5, 6, *range(8, 8 + len(blocks))),
        )
    return state


def solution(mesh):
    both = P(("fine", "tele"))
    return jax.shard_map(
        shards,
        mesh=mesh,
        in_specs=(both, both, both, both, both, both, both, P(), both),
        out_specs=both,
        check_vma=False,
    )
```

```python
import functools

import jax
import jax.numpy as jnp
import numpy as np
from jax import lax
from jax.experimental import pallas as pl
from jax.experimental.pallas import tpu as pltpu
from jax.sharding import PartitionSpec as P

FIELDS = 5
NODES = 4
SWEEPS = 3
CYCLES = 2
LANES = 128
OPPOSITE = (1, 0, 3, 2, 5, 4)


def swapped(block, axis):
    count = lax.axis_size(axis)
    inner = lax.ppermute(block, axis, [(i, i ^ 1) for i in range(count)])
    outer = lax.ppermute(block, axis, [(i, (i - 1 if i % 2 == 0 else i + 1) % count) for i in range(count)])
    return inner, outer


def face_table():
    cube = np.arange(FIELDS * NODES**3).reshape(FIELDS, NODES, NODES, NODES)
    far = NODES - 1
    faces = (cube[:, 0], cube[:, far], cube[:, :, 0], cube[:, :, far], cube[..., 0], cube[..., far])
    table = np.zeros((6 * LANES, cube.size), np.float32)
    for k, face in enumerate(faces):
        nodes = face.reshape(-1)
        table[k * LANES + np.arange(nodes.size), nodes] = 1.0
    return table


def halves(value):
    high = value.astype(jnp.bfloat16)
    low = (value - high.astype(jnp.float32)).astype(jnp.bfloat16)
    return high, low


def exact_dot(left, right):
    high, low = halves(right)
    return jnp.dot(left, high, preferred_element_type=jnp.float32) + jnp.dot(
        left, low, preferred_element_type=jnp.float32
    )


def coupling(states, index, operators, pick, lift):
    count = states[0].shape[0]
    pool = jnp.concatenate([state.astype(jnp.float32) for state in states], axis=0).astype(jnp.bfloat16)
    traces = jnp.dot(pool, pick, preferred_element_type=jnp.float32).astype(jnp.bfloat16)
    column = lax.broadcasted_iota(jnp.int32, (count, pool.shape[0]), 1)
    face_rows, kinds = [], []
    for k in range(6):
        chosen = jnp.where(index[:, k : k + 1] == column, 1.0, 0.0).astype(jnp.bfloat16)
        across = traces[:, OPPOSITE[k] * LANES : (OPPOSITE[k] + 1) * LANES]
        face_rows.append(jnp.dot(chosen, across, preferred_element_type=jnp.float32))
        kinds.append(jnp.broadcast_to(index[:, 6 + k : 7 + k], (count, LANES)))
    face_rows = jnp.concatenate(face_rows, axis=0)
    kinds = jnp.concatenate(kinds, axis=0)
    types = operators.shape[0] // LANES
    spread = jnp.concatenate(
        [jnp.where(kinds == q, face_rows, 0.0).astype(jnp.bfloat16) for q in range(types)], axis=1
    )
    coupled = jnp.dot(spread, operators, preferred_element_type=jnp.float32)
    side_by_side = jnp.concatenate([coupled[k * count : (k + 1) * count] for k in range(6)], axis=1)
    high = side_by_side.astype(jnp.bfloat16).astype(jnp.float32)
    terms = jnp.concatenate([high, side_by_side - high], axis=0).astype(jnp.bfloat16)
    lifted = jnp.dot(terms, lift, preferred_element_type=jnp.float32)
    return lifted[:count] + lifted[count:]


def apply_inverse(blocks, vector, turned=False):
    contracted = (((1,), (0 if turned else 1,)), ((), ()))
    row = lax.broadcasted_iota(jnp.int32, vector.shape, 0)
    result = jnp.zeros(vector.shape, jnp.float32)
    first = 0
    for block in blocks:
        for e in range(block.shape[0]):
            product = lax.dot_general(vector, block[e], contracted, preferred_element_type=jnp.float32)
            result = jnp.where(row == first + e, product, result)
        first += block.shape[0]
    return result


def pool_rows(links, count, position):
    shift = count.bit_length() - 1
    owner, within = links >> shift, links & (count - 1)
    place = jnp.where(owner == position, 1, jnp.where(owner == (position ^ 1), 0, 2))
    return jnp.where(links >= 0, place * count + within, -1)


def first_kernel(*refs, count):
    sources, (state_ref, index_ref, lists_ref, operators_ref, inverse_ref) = refs[:count], refs[count : count + 5]
    targets, (sems, block_sems) = refs[count + 5 : -2], refs[-2:]
    right_ref, links_ref, faces_ref, coarse_links_ref, coarse_faces_ref, operators_in_ref = targets
    whole = [pltpu.make_async_copy(sources[i], targets[i], sems.at[i]) for i in range(count - 1)]
    step = inverse_ref.shape[0] // block_sems.shape[0]
    blocks = [
        pltpu.make_async_copy(
            sources[-1].at[i * step : (i + 1) * step], inverse_ref.at[i * step : (i + 1) * step], block_sems.at[i]
        )
        for i in range(block_sems.shape[0])
    ]
    for copy in [whole[0], *blocks, *whole[1:]]:
        copy.start()

    tele, column = lax.axis_index("tele"), lax.axis_index("fine")
    tele_size = lax.axis_size("tele")
    whole[0].wait()
    lowered = right_ref[...].astype(jnp.bfloat16)
    row = lax.broadcasted_iota(jnp.int32, lowered.shape, 0)
    result = jnp.zeros(lowered.shape, jnp.float32)
    for e in range(inverse_ref.shape[0]):
        if e % step == 0:
            blocks[e // step].wait()
        product = lax.dot_general(
            lowered, inverse_ref[e], (((1,), (1,)), ((), ())), preferred_element_type=jnp.float32
        )
        result = jnp.where(row == e, product, result)
    state_ref[...] = result.astype(jnp.bfloat16)
    for copy in whole[1:]:
        copy.wait()

    fine_rows = right_ref.shape[0]
    rows = pool_rows(links_ref[...], fine_rows, column * tele_size + tele)
    index = jnp.concatenate([rows.astype(jnp.float32), faces_ref[...].astype(jnp.float32)], axis=0)
    index_ref[...] = index.T.astype(jnp.int32)

    own = coarse_links_ref.shape[0]
    count = own * tele_size
    rows = pool_rows(coarse_links_ref[...], count, column).astype(jnp.float32)
    kinds = coarse_faces_ref[...].astype(jnp.float32)
    lists_ref[...] = jnp.zeros(lists_ref.shape, jnp.float32)
    row = lax.broadcasted_iota(jnp.int32, (count, kinds.shape[1]), 0)
    for part, values in enumerate((rows, kinds)):
        placed = jnp.zeros(row.shape, jnp.float32)
        for c in range(own):
            placed = jnp.where(row == own * tele + c, values[c : c + 1], placed)
        lists_ref[:, part * 6 : part * 6 + 6] = placed

    types, size, _ = operators_in_ref.shape
    unit = lax.broadcasted_iota(jnp.int32, (LANES, size), 0) == lax.broadcasted_iota(jnp.int32, (LANES, size), 1)
    unit = jnp.where(unit, 1.0, 0.0).astype(jnp.bfloat16)
    operators_ref[...] = jnp.zeros(operators_ref.shape, jnp.bfloat16)
    for q in range(types):
        turned = lax.dot_general(
            unit, operators_in_ref[q], (((1,), (1,)), ((), ())), preferred_element_type=jnp.float32
        )
        operators_ref[q * LANES : (q + 1) * LANES, :size] = turned.astype(jnp.bfloat16)


def turn_kernel(*refs):
    out_ref = refs[-1]
    size = out_ref.shape[1]
    unit = lax.broadcasted_iota(jnp.int32, (size, size), 0) == lax.broadcasted_iota(jnp.int32, (size, size), 1)
    unit = jnp.where(unit, 1.0, 0.0).astype(jnp.bfloat16)
    blocks = [(ref, e) for ref in refs[:-1] for e in range(ref.shape[0])]
    for place, (ref, e) in enumerate(blocks):
        turned = lax.dot_general(unit, ref[e], (((1,), (1,)), ((), ())), preferred_element_type=jnp.float32)
        out_ref[place] = turned.astype(jnp.bfloat16)


def sweep(refs, blocks, turned=False):
    prev_ref, own_ref, next_ref, index_ref, operators_ref, pick_ref, lift_ref, right_ref = refs
    states = [prev_ref[...], own_ref[...], next_ref[...]]
    coupled = coupling(states, index_ref[...], operators_ref[...], pick_ref[...], lift_ref[...])
    lowered = (right_ref[...] - coupled).astype(jnp.bfloat16)
    return apply_inverse(blocks, lowered, turned), lowered


def sweep_kernel(*refs, blocks, turned=False):
    result, lowered = sweep(refs[:8], refs[8 : 8 + blocks], turned)
    outs = refs[8 + blocks :]
    outs[0][...] = result.astype(jnp.bfloat16)
    if len(outs) > 1:
        outs[1][...] = result
        outs[2][...] = lowered


def restrict_kernel(
    prev_ref, own_ref, next_ref, index_ref, operators_ref, pick_ref, lift_ref, lowered_ref, target_ref, lists_ref, out_ref
):
    states = [prev_ref[...], own_ref[...], next_ref[...]]
    coupled = coupling(states, index_ref[...], operators_ref[...], pick_ref[...], lift_ref[...])
    residual = lowered_ref[...].astype(jnp.float32) - coupled
    tele_size, rows, dofs = out_ref.shape[0], out_ref.shape[1], residual.shape[1]
    shape = (tele_size * rows, residual.shape[0])
    row = lax.broadcasted_iota(jnp.int32, shape, 0)
    element = (row & (rows - 1)) ^ ((row >> (rows.bit_length() - 1)) * (rows // tele_size))
    member = jnp.where((target_ref[...] & (rows - 1)) == element, 1.0, 0.0).astype(jnp.bfloat16)
    partial = exact_dot(member, residual)
    own = rows // tele_size
    for t in range(tele_size):
        out_ref[t, :, :dofs] = partial[t * rows : (t + 1) * rows]
        for s in range(tele_size):
            out_ref[t, s * own : (s + 1) * own, dofs:] = lists_ref[(s ^ t) * own : ((s ^ t) + 1) * own]


def coarse_first_kernel(*refs, blocks, turned):
    parts_ref, inverses, (restricted_ref, state_ref, index_ref) = refs[0], refs[1 : 1 + blocks], refs[1 + blocks :]
    total = parts_ref[0]
    for t in range(1, parts_ref.shape[0]):
        total = total + parts_ref[t]
    dofs = restricted_ref.shape[1]
    restricted = total[:, :dofs]
    restricted_ref[...] = restricted
    lists = total[:, dofs:].astype(jnp.int32)
    turn = lax.axis_index("tele") * (total.shape[0] // parts_ref.shape[0])
    moved = (lax.broadcasted_iota(jnp.int32, lists.shape, 1) < 6) & (lists >= 0)
    index_ref[...] = jnp.where(moved, lists ^ turn, lists)
    state_ref[...] = apply_inverse(inverses, restricted.astype(jnp.bfloat16), turned).astype(jnp.bfloat16)


def correct_kernel(*refs, blocks):
    coarse, _ = sweep(refs[:8], refs[8 : 8 + blocks], True)
    target_ref, solution_ref, out_ref = refs[8 + blocks :]
    rows, fine = coarse.shape[0], solution_ref.shape[0]
    turn = lax.axis_index("tele") * (rows // lax.axis_size("tele"))
    member = ((target_ref[...] & (rows - 1)) ^ turn) == lax.broadcasted_iota(jnp.int32, (rows, fine), 0)
    added = exact_dot(jnp.where(member, 1.0, 0.0).T.astype(jnp.bfloat16), coarse)
    out_ref[...] = (solution_ref[...] + added).astype(out_ref.dtype)


def run(kernel, outs, *operands, held=(), keep=(), hbm=(), pinned=(), scratch=()):
    count = len(operands)

    def body(*refs):
        kernel(*refs[:count], *refs[count + len(keep) :])

    single = not isinstance(outs, list)
    shapes = [outs] if single else outs
    vmem = pl.BlockSpec(memory_space=pltpu.VMEM)
    moved = sum(o.size * o.dtype.itemsize for o in operands)
    operands = [
        pltpu.with_memory_space_constraint(o, pltpu.HBM if i in hbm else pltpu.VMEM) if i in held or i in hbm else o
        for i, o in enumerate(operands)
    ]
    operands += [pltpu.with_memory_space_constraint(o, pltpu.VMEM) for o in keep]
    result = pl.pallas_call(
        body,
        out_shape=[pltpu.VMEM(s, d) if i in pinned else jax.ShapeDtypeStruct(s, d) for i, (s, d) in enumerate(shapes)],
        in_specs=[pl.BlockSpec(memory_space=pltpu.HBM) if i in hbm else vmem for i in range(len(operands))],
        out_specs=[vmem] * len(shapes),
        scratch_shapes=scratch,
        compiler_params=pltpu.CompilerParams(vmem_limit_bytes=20 << 20),
        cost_estimate=pl.CostEstimate(flops=1 << 32, bytes_accessed=moved, transcendentals=0),
    )(*operands)
    return result[0] if single else result


def shards(
    right_side,
    fine_inverse,
    fine_links,
    fine_faces,
    coarse_inverse,
    coarse_links,
    coarse_faces,
    face_operators,
    agglomerate,
):
    f32, bf16, i32 = jnp.float32, jnp.bfloat16, jnp.int32
    fine_rows, dofs = right_side.shape
    tele_size = lax.axis_size("tele")
    coarse_rows = coarse_inverse.shape[0] * tele_size
    types = face_operators.shape[0]
    spare = -dofs % LANES

    def across(block, bits):
        return lax.ppermute(block, "tele", [(i, i ^ bits) for i in range(tele_size)])

    table = face_table()
    pick, lift = jnp.asarray(table.T.copy(), bf16), jnp.asarray(table, bf16)
    target = agglomerate[None, :]
    operands = (
        right_side,
        fine_links.T,
        fine_faces.T,
        coarse_links,
        coarse_faces,
        face_operators,
        fine_inverse,
    )
    state, fine_index, lists, operators, inverse = run(
        functools.partial(first_kernel, count=len(operands)),
        [
            ((fine_rows, dofs), bf16),
            ((fine_rows, 12), i32),
            ((coarse_rows, spare), f32),
            ((types * LANES, LANES), bf16),
            (fine_inverse.shape, bf16),
        ],
        *operands,
        hbm=range(len(operands)),
        pinned=(3, 4),
        scratch=[pltpu.VMEM(o.shape, o.dtype) for o in operands[:-1]]
        + [pltpu.SemaphoreType.DMA((len(operands),)), pltpu.SemaphoreType.DMA((4,))],
    )
    shared = (operators, pick, lift)

    def halo(block, axis):
        inner, outer = swapped(block, axis)
        return inner, block, outer

    both = ("fine", "tele")
    for cycle in range(CYCLES):
        for sweep in range(SWEEPS):
            if cycle == 0 and sweep == 0:
                continue
            inner, own, outer = halo(state, both)
            if cycle == 0 and sweep == 1:
                sent, inner = lax.optimization_barrier((coarse_inverse, inner))
                near, other = across(sent, 1), across(sent, tele_size - 1)
            if cycle == 0 and sweep == 2:
                near, other, outer = lax.optimization_barrier((near, other, outer))
                far = across(other, 1)
                blocks = (coarse_inverse, near, far, other)
            turned = cycle > 0
            outs = [((fine_rows, dofs), bf16)]
            if sweep == SWEEPS - 1:
                outs += [((fine_rows, dofs), f32), ((fine_rows, dofs), bf16)]
            result = run(
                functools.partial(sweep_kernel, blocks=1, turned=turned),
                outs,
                inner,
                own,
                outer,
                fine_index,
                *shared,
                right_side,
                inverse,
                held=(5, 6, 8),
            )
            state = result[0]
            if cycle == 0 and sweep == SWEEPS - 1:
                inverse = run(turn_kernel, (inverse.shape, bf16), inverse, held=(0,), keep=(state,), pinned=(0,))
        solution, lowered = result[1], result[2]
        parts = run(
            restrict_kernel,
            ((tele_size, coarse_rows, dofs + spare), f32),
            *halo(state, both),
            fine_index,
            *shared,
            lowered,
            target,
            lists,
            held=(5, 6),
            keep=(far,) if cycle == 0 else (),
        )
        parts = lax.all_to_all(parts, "tele", 0, 0, tiled=True)
        restricted, coarse, coarse_index = run(
            functools.partial(coarse_first_kernel, blocks=len(blocks), turned=cycle > 0),
            [((coarse_rows, dofs), f32), ((coarse_rows, dofs), bf16), ((coarse_rows, spare), i32)],
            parts,
            *blocks,
            held=range(1, 1 + len(blocks)),
        )
        if cycle == 0:
            turned_shape = ((coarse_rows, dofs, dofs), bf16)
            held = range(len(blocks))
            blocks = (run(turn_kernel, turned_shape, *blocks, held=held, keep=(coarse,), pinned=(0,)),)
        for sweep in range(SWEEPS - 2):
            coarse = run(
                functools.partial(sweep_kernel, blocks=len(blocks), turned=True),
                [((coarse_rows, dofs), bf16)],
                *halo(coarse, "fine"),
                coarse_index,
                *shared,
                restricted,
                *blocks,
                held=(5, 6, *range(8, 8 + len(blocks))),
            )[0]
        last = cycle == CYCLES - 1
        state = run(
            functools.partial(correct_kernel, blocks=len(blocks)),
            ((fine_rows, dofs), f32 if last else bf16),
            *halo(coarse, "fine"),
            coarse_index,
            *shared,
            restricted,
            *blocks,
            target,
            solution,
            held=(5, 6, *range(8, 8 + len(blocks))),
        )
    return state


def solution(mesh):
    both = P(("fine", "tele"))
    return jax.shard_map(
        shards,
        mesh=mesh,
        in_specs=(both, both, both, both, both, both, both, P(), both),
        out_specs=both,
        check_vma=False,
    )
```

```python
import functools

import jax
import jax.numpy as jnp
import numpy as np
from jax import lax
from jax.experimental import pallas as pl
from jax.experimental.pallas import tpu as pltpu
from jax.sharding import PartitionSpec as P

FIELDS = 5
NODES = 4
SWEEPS = 3
CYCLES = 2
LANES = 128
OPPOSITE = (1, 0, 3, 2, 5, 4)


def swapped(block, axis):
    count = lax.axis_size(axis)
    inner = lax.ppermute(block, axis, [(i, i ^ 1) for i in range(count)])
    outer = lax.ppermute(block, axis, [(i, (i - 1 if i % 2 == 0 else i + 1) % count) for i in range(count)])
    return inner, outer


def face_table():
    cube = np.arange(FIELDS * NODES**3).reshape(FIELDS, NODES, NODES, NODES)
    far = NODES - 1
    faces = (cube[:, 0], cube[:, far], cube[:, :, 0], cube[:, :, far], cube[..., 0], cube[..., far])
    table = np.zeros((6 * LANES, cube.size), np.float32)
    for k, face in enumerate(faces):
        nodes = face.reshape(-1)
        table[k * LANES + np.arange(nodes.size), nodes] = 1.0
    return table


def halves(value):
    high = value.astype(jnp.bfloat16)
    low = (value - high.astype(jnp.float32)).astype(jnp.bfloat16)
    return high, low


def exact_dot(left, right):
    high, low = halves(right)
    return jnp.dot(left, high, preferred_element_type=jnp.float32) + jnp.dot(
        left, low, preferred_element_type=jnp.float32
    )


def coupling(states, index, operators, pick, lift):
    count = states[0].shape[0]
    pool = jnp.concatenate([state.astype(jnp.float32) for state in states], axis=0).astype(jnp.bfloat16)
    traces = jnp.dot(pool, pick, preferred_element_type=jnp.float32).astype(jnp.bfloat16)
    column = lax.broadcasted_iota(jnp.int32, (count, pool.shape[0]), 1)
    face_rows, kinds = [], []
    for k in range(6):
        chosen = jnp.where(index[:, k : k + 1] == column, 1.0, 0.0).astype(jnp.bfloat16)
        across = traces[:, OPPOSITE[k] * LANES : (OPPOSITE[k] + 1) * LANES]
        face_rows.append(jnp.dot(chosen, across, preferred_element_type=jnp.float32))
        kinds.append(jnp.broadcast_to(index[:, 6 + k : 7 + k], (count, LANES)))
    face_rows = jnp.concatenate(face_rows, axis=0)
    kinds = jnp.concatenate(kinds, axis=0)
    types = operators.shape[0] // LANES
    spread = jnp.concatenate(
        [jnp.where(kinds == q, face_rows, 0.0).astype(jnp.bfloat16) for q in range(types)], axis=1
    )
    coupled = jnp.dot(spread, operators, preferred_element_type=jnp.float32)
    side_by_side = jnp.concatenate([coupled[k * count : (k + 1) * count] for k in range(6)], axis=1)
    high = side_by_side.astype(jnp.bfloat16).astype(jnp.float32)
    terms = jnp.concatenate([high, side_by_side - high], axis=0).astype(jnp.bfloat16)
    lifted = jnp.dot(terms, lift, preferred_element_type=jnp.float32)
    return lifted[:count] + lifted[count:]


def apply_inverse(blocks, vector, turned=False):
    contracted = (((1,), (0 if turned else 1,)), ((), ()))
    row = lax.broadcasted_iota(jnp.int32, vector.shape, 0)
    result = jnp.zeros(vector.shape, jnp.float32)
    first = 0
    for block in blocks:
        for e in range(block.shape[0]):
            product = lax.dot_general(vector, block[e], contracted, preferred_element_type=jnp.float32)
            result = jnp.where(row == first + e, product, result)
        first += block.shape[0]
    return result


def pool_rows(links, count, position):
    shift = count.bit_length() - 1
    owner, within = links >> shift, links & (count - 1)
    place = jnp.where(owner == position, 1, jnp.where(owner == (position ^ 1), 0, 2))
    return jnp.where(links >= 0, place * count + within, -1)


def first_kernel(*refs, count):
    sources, (state_ref, index_ref, lists_ref, operators_ref, inverse_ref) = refs[:count], refs[count : count + 5]
    targets, (sems, block_sems) = refs[count + 5 : -2], refs[-2:]
    right_ref, links_ref, faces_ref, coarse_links_ref, coarse_faces_ref, operators_in_ref = targets
    whole = [pltpu.make_async_copy(sources[i], targets[i], sems.at[i]) for i in range(count - 1)]
    step = inverse_ref.shape[0] // block_sems.shape[0]
    blocks = [
        pltpu.make_async_copy(
            sources[-1].at[i * step : (i + 1) * step], inverse_ref.at[i * step : (i + 1) * step], block_sems.at[i]
        )
        for i in range(block_sems.shape[0])
    ]
    for copy in [whole[0], *blocks, *whole[1:]]:
        copy.start()

    tele, column = lax.axis_index("tele"), lax.axis_index("fine")
    tele_size = lax.axis_size("tele")
    whole[0].wait()
    lowered = right_ref[...].astype(jnp.bfloat16)
    row = lax.broadcasted_iota(jnp.int32, lowered.shape, 0)
    result = jnp.zeros(lowered.shape, jnp.float32)
    for e in range(inverse_ref.shape[0]):
        if e % step == 0:
            blocks[e // step].wait()
        product = lax.dot_general(
            lowered, inverse_ref[e], (((1,), (1,)), ((), ())), preferred_element_type=jnp.float32
        )
        result = jnp.where(row == e, product, result)
    state_ref[...] = result.astype(jnp.bfloat16)
    for copy in whole[1:]:
        copy.wait()

    fine_rows = right_ref.shape[0]
    rows = pool_rows(links_ref[...], fine_rows, column * tele_size + tele)
    index = jnp.concatenate([rows.astype(jnp.float32), faces_ref[...].astype(jnp.float32)], axis=0)
    index_ref[...] = index.T.astype(jnp.int32)

    own = coarse_links_ref.shape[0]
    count = own * tele_size
    rows = pool_rows(coarse_links_ref[...], count, column).astype(jnp.float32)
    kinds = coarse_faces_ref[...].astype(jnp.float32)
    lists_ref[...] = jnp.zeros(lists_ref.shape, jnp.float32)
    row = lax.broadcasted_iota(jnp.int32, (count, kinds.shape[1]), 0)
    for part, values in enumerate((rows, kinds)):
        placed = jnp.zeros(row.shape, jnp.float32)
        for c in range(own):
            placed = jnp.where(row == own * tele + c, values[c : c + 1], placed)
        lists_ref[:, part * 6 : part * 6 + 6] = placed

    types, size, _ = operators_in_ref.shape
    unit = lax.broadcasted_iota(jnp.int32, (LANES, size), 0) == lax.broadcasted_iota(jnp.int32, (LANES, size), 1)
    unit = jnp.where(unit, 1.0, 0.0).astype(jnp.bfloat16)
    operators_ref[...] = jnp.zeros(operators_ref.shape, jnp.bfloat16)
    for q in range(types):
        turned = lax.dot_general(
            unit, operators_in_ref[q], (((1,), (1,)), ((), ())), preferred_element_type=jnp.float32
        )
        operators_ref[q * LANES : (q + 1) * LANES, :size] = turned.astype(jnp.bfloat16)


def turn_kernel(*refs):
    out_ref = refs[-1]
    size = out_ref.shape[1]
    unit = lax.broadcasted_iota(jnp.int32, (size, size), 0) == lax.broadcasted_iota(jnp.int32, (size, size), 1)
    unit = jnp.where(unit, 1.0, 0.0).astype(jnp.bfloat16)
    blocks = [(ref, e) for ref in refs[:-1] for e in range(ref.shape[0])]
    for place, (ref, e) in enumerate(blocks):
        turned = lax.dot_general(unit, ref[e], (((1,), (1,)), ((), ())), preferred_element_type=jnp.float32)
        out_ref[place] = turned.astype(jnp.bfloat16)


def sweep(refs, blocks, turned=False):
    prev_ref, own_ref, next_ref, index_ref, operators_ref, pick_ref, lift_ref, right_ref = refs
    states = [prev_ref[...], own_ref[...], next_ref[...]]
    coupled = coupling(states, index_ref[...], operators_ref[...], pick_ref[...], lift_ref[...])
    lowered = (right_ref[...] - coupled).astype(jnp.bfloat16)
    return apply_inverse(blocks, lowered, turned), lowered


def sweep_kernel(*refs, blocks, turned=False):
    result, lowered = sweep(refs[:8], refs[8 : 8 + blocks], turned)
    outs = refs[8 + blocks :]
    outs[0][...] = result.astype(jnp.bfloat16)
    if len(outs) > 1:
        outs[1][...] = result
        outs[2][...] = lowered


def restrict_kernel(
    prev_ref, own_ref, next_ref, index_ref, operators_ref, pick_ref, lift_ref, lowered_ref, target_ref, lists_ref, out_ref
):
    states = [prev_ref[...], own_ref[...], next_ref[...]]
    coupled = coupling(states, index_ref[...], operators_ref[...], pick_ref[...], lift_ref[...])
    residual = lowered_ref[...].astype(jnp.float32) - coupled
    tele_size, rows, dofs = out_ref.shape[0], out_ref.shape[1], residual.shape[1]
    shape = (tele_size * rows, residual.shape[0])
    row = lax.broadcasted_iota(jnp.int32, shape, 0)
    element = (row & (rows - 1)) ^ ((row >> (rows.bit_length() - 1)) * (rows // tele_size))
    member = jnp.where((target_ref[...] & (rows - 1)) == element, 1.0, 0.0).astype(jnp.bfloat16)
    partial = exact_dot(member, residual)
    own = rows // tele_size
    for t in range(tele_size):
        out_ref[t, :, :dofs] = partial[t * rows : (t + 1) * rows]
        for s in range(tele_size):
            out_ref[t, s * own : (s + 1) * own, dofs:] = lists_ref[(s ^ t) * own : ((s ^ t) + 1) * own]


def coarse_first_kernel(*refs, blocks, turned):
    parts_ref, inverses, (restricted_ref, state_ref, index_ref) = refs[0], refs[1 : 1 + blocks], refs[1 + blocks :]
    total = parts_ref[0]
    for t in range(1, parts_ref.shape[0]):
        total = total + parts_ref[t]
    dofs = restricted_ref.shape[1]
    restricted = total[:, :dofs]
    restricted_ref[...] = restricted
    lists = total[:, dofs:].astype(jnp.int32)
    turn = lax.axis_index("tele") * (total.shape[0] // parts_ref.shape[0])
    moved = (lax.broadcasted_iota(jnp.int32, lists.shape, 1) < 6) & (lists >= 0)
    index_ref[...] = jnp.where(moved, lists ^ turn, lists)
    state_ref[...] = apply_inverse(inverses, restricted.astype(jnp.bfloat16), turned).astype(jnp.bfloat16)


def correct_kernel(*refs, blocks):
    coarse, _ = sweep(refs[:8], refs[8 : 8 + blocks], True)
    target_ref, solution_ref, out_ref = refs[8 + blocks :]
    rows, fine = coarse.shape[0], solution_ref.shape[0]
    turn = lax.axis_index("tele") * (rows // lax.axis_size("tele"))
    member = ((target_ref[...] & (rows - 1)) ^ turn) == lax.broadcasted_iota(jnp.int32, (rows, fine), 0)
    added = exact_dot(jnp.where(member, 1.0, 0.0).T.astype(jnp.bfloat16), coarse)
    out_ref[...] = (solution_ref[...] + added).astype(out_ref.dtype)


def run(kernel, outs, *operands, held=(), keep=(), hbm=(), pinned=(), scratch=()):
    count = len(operands)

    def body(*refs):
        kernel(*refs[:count], *refs[count + len(keep) :])

    single = not isinstance(outs, list)
    shapes = [outs] if single else outs
    vmem = pl.BlockSpec(memory_space=pltpu.VMEM)
    moved = sum(o.size * o.dtype.itemsize for o in operands)
    operands = [
        pltpu.with_memory_space_constraint(o, pltpu.HBM if i in hbm else pltpu.VMEM) if i in held or i in hbm else o
        for i, o in enumerate(operands)
    ]
    operands += [pltpu.with_memory_space_constraint(o, pltpu.VMEM) for o in keep]
    result = pl.pallas_call(
        body,
        out_shape=[pltpu.VMEM(s, d) if i in pinned else jax.ShapeDtypeStruct(s, d) for i, (s, d) in enumerate(shapes)],
        in_specs=[pl.BlockSpec(memory_space=pltpu.HBM) if i in hbm else vmem for i in range(len(operands))],
        out_specs=[vmem] * len(shapes),
        scratch_shapes=scratch,
        compiler_params=pltpu.CompilerParams(vmem_limit_bytes=20 << 20),
        cost_estimate=pl.CostEstimate(flops=1 << 32, bytes_accessed=moved, transcendentals=0),
    )(*operands)
    return result[0] if single else result


def shards(
    right_side,
    fine_inverse,
    fine_links,
    fine_faces,
    coarse_inverse,
    coarse_links,
    coarse_faces,
    face_operators,
    agglomerate,
):
    f32, bf16, i32 = jnp.float32, jnp.bfloat16, jnp.int32
    fine_rows, dofs = right_side.shape
    tele_size = lax.axis_size("tele")
    coarse_rows = coarse_inverse.shape[0] * tele_size
    types = face_operators.shape[0]
    spare = -dofs % LANES

    def across(block, bits):
        return lax.ppermute(block, "tele", [(i, i ^ bits) for i in range(tele_size)])

    table = face_table()
    pick, lift = jnp.asarray(table.T.copy(), bf16), jnp.asarray(table, bf16)
    target = agglomerate[None, :]
    operands = (
        right_side,
        fine_links.T,
        fine_faces.T,
        coarse_links,
        coarse_faces,
        face_operators,
        fine_inverse,
    )
    state, fine_index, lists, operators, inverse = run(
        functools.partial(first_kernel, count=len(operands)),
        [
            ((fine_rows, dofs), bf16),
            ((fine_rows, 12), i32),
            ((coarse_rows, spare), f32),
            ((types * LANES, LANES), bf16),
            (fine_inverse.shape, bf16),
        ],
        *operands,
        hbm=range(len(operands)),
        pinned=(3, 4),
        scratch=[pltpu.VMEM(o.shape, o.dtype) for o in operands[:-1]]
        + [pltpu.SemaphoreType.DMA((len(operands),)), pltpu.SemaphoreType.DMA((4,))],
    )
    shared = (operators, pick, lift)

    def halo(block, axis):
        inner, outer = swapped(block, axis)
        return inner, block, outer

    both = ("fine", "tele")
    for cycle in range(CYCLES):
        for sweep in range(SWEEPS):
            if cycle == 0 and sweep == 0:
                continue
            inner, own, outer = halo(state, both)
            if cycle == 0 and sweep == 1:
                sent, inner = lax.optimization_barrier((coarse_inverse, inner))
                near, other = across(sent, 1), across(sent, tele_size - 1)
            if cycle == 0 and sweep == 2:
                far = across(other, 1)
                blocks = (coarse_inverse, near, far, other)
            turned = cycle > 0
            outs = [((fine_rows, dofs), bf16)]
            if sweep == SWEEPS - 1:
                outs += [((fine_rows, dofs), f32), ((fine_rows, dofs), bf16)]
            result = run(
                functools.partial(sweep_kernel, blocks=1, turned=turned),
                outs,
                inner,
                own,
                outer,
                fine_index,
                *shared,
                right_side,
                inverse,
                held=(5, 6, 8),
            )
            state = result[0]
            if cycle == 0 and sweep == SWEEPS - 1:
                inverse = run(turn_kernel, (inverse.shape, bf16), inverse, held=(0,), keep=(state,), pinned=(0,))
        solution, lowered = result[1], result[2]
        parts = run(
            restrict_kernel,
            ((tele_size, coarse_rows, dofs + spare), f32),
            *halo(state, both),
            fine_index,
            *shared,
            lowered,
            target,
            lists,
            held=(5, 6),
            keep=(far,) if cycle == 0 else (),
        )
        parts = lax.all_to_all(parts, "tele", 0, 0, tiled=True)
        restricted, coarse, coarse_index = run(
            functools.partial(coarse_first_kernel, blocks=len(blocks), turned=cycle > 0),
            [((coarse_rows, dofs), f32), ((coarse_rows, dofs), bf16), ((coarse_rows, spare), i32)],
            parts,
            *blocks,
            held=range(1, 1 + len(blocks)),
        )
        if cycle == 0:
            turned_shape = ((coarse_rows, dofs, dofs), bf16)
            held = range(len(blocks))
            blocks = (run(turn_kernel, turned_shape, *blocks, held=held, keep=(coarse,), pinned=(0,)),)
        for sweep in range(SWEEPS - 2):
            coarse = run(
                functools.partial(sweep_kernel, blocks=len(blocks), turned=True),
                [((coarse_rows, dofs), bf16)],
                *halo(coarse, "fine"),
                coarse_index,
                *shared,
                restricted,
                *blocks,
                held=(5, 6, *range(8, 8 + len(blocks))),
            )[0]
        last = cycle == CYCLES - 1
        state = run(
            functools.partial(correct_kernel, blocks=len(blocks)),
            ((fine_rows, dofs), f32 if last else bf16),
            *halo(coarse, "fine"),
            coarse_index,
            *shared,
            restricted,
            *blocks,
            target,
            solution,
            held=(5, 6, *range(8, 8 + len(blocks))),
        )
    return state


def solution(mesh):
    both = P(("fine", "tele"))
    return jax.shard_map(
        shards,
        mesh=mesh,
        in_specs=(both, both, both, both, both, both, both, P(), both),
        out_specs=both,
        check_vma=False,
    )
```

```python
import functools

import jax
import jax.numpy as jnp
import numpy as np
from jax import lax
from jax.experimental import pallas as pl
from jax.experimental.pallas import tpu as pltpu
from jax.sharding import PartitionSpec as P

FIELDS = 5
NODES = 4
SWEEPS = 3
CYCLES = 2
LANES = 128
OPPOSITE = (1, 0, 3, 2, 5, 4)


def swapped(block, axis):
    count = lax.axis_size(axis)
    inner = lax.ppermute(block, axis, [(i, i ^ 1) for i in range(count)])
    outer = lax.ppermute(block, axis, [(i, (i - 1 if i % 2 == 0 else i + 1) % count) for i in range(count)])
    return inner, outer


def face_table():
    cube = np.arange(FIELDS * NODES**3).reshape(FIELDS, NODES, NODES, NODES)
    far = NODES - 1
    faces = (cube[:, 0], cube[:, far], cube[:, :, 0], cube[:, :, far], cube[..., 0], cube[..., far])
    table = np.zeros((6 * LANES, cube.size), np.float32)
    for k, face in enumerate(faces):
        nodes = face.reshape(-1)
        table[k * LANES + np.arange(nodes.size), nodes] = 1.0
    return table


def halves(value):
    high = value.astype(jnp.bfloat16)
    low = (value - high.astype(jnp.float32)).astype(jnp.bfloat16)
    return high, low


def exact_dot(left, right):
    high, low = halves(right)
    return jnp.dot(left, high, preferred_element_type=jnp.float32) + jnp.dot(
        left, low, preferred_element_type=jnp.float32
    )


def coupling(states, index, operators, pick, lift):
    count = states[0].shape[0]
    pool = jnp.concatenate([state.astype(jnp.float32) for state in states], axis=0).astype(jnp.bfloat16)
    traces = jnp.dot(pool, pick, preferred_element_type=jnp.float32).astype(jnp.bfloat16)
    column = lax.broadcasted_iota(jnp.int32, (count, pool.shape[0]), 1)
    face_rows, kinds = [], []
    for k in range(6):
        chosen = jnp.where(index[:, k : k + 1] == column, 1.0, 0.0).astype(jnp.bfloat16)
        across = traces[:, OPPOSITE[k] * LANES : (OPPOSITE[k] + 1) * LANES]
        face_rows.append(jnp.dot(chosen, across, preferred_element_type=jnp.float32))
        kinds.append(jnp.broadcast_to(index[:, 6 + k : 7 + k], (count, LANES)))
    face_rows = jnp.concatenate(face_rows, axis=0)
    kinds = jnp.concatenate(kinds, axis=0)
    types = operators.shape[0] // LANES
    spread = jnp.concatenate(
        [jnp.where(kinds == q, face_rows, 0.0).astype(jnp.bfloat16) for q in range(types)], axis=1
    )
    coupled = jnp.dot(spread, operators, preferred_element_type=jnp.float32)
    side_by_side = jnp.concatenate([coupled[k * count : (k + 1) * count] for k in range(6)], axis=1)
    high = side_by_side.astype(jnp.bfloat16).astype(jnp.float32)
    terms = jnp.concatenate([high, side_by_side - high], axis=0).astype(jnp.bfloat16)
    lifted = jnp.dot(terms, lift, preferred_element_type=jnp.float32)
    return lifted[:count] + lifted[count:]


def apply_inverse(blocks, vector, turned=False):
    contracted = (((1,), (0 if turned else 1,)), ((), ()))
    row = lax.broadcasted_iota(jnp.int32, vector.shape, 0)
    result = jnp.zeros(vector.shape, jnp.float32)
    first = 0
    for block in blocks:
        for e in range(block.shape[0]):
            product = lax.dot_general(vector, block[e], contracted, preferred_element_type=jnp.float32)
            result = jnp.where(row == first + e, product, result)
        first += block.shape[0]
    return result


def pool_rows(links, count, position):
    shift = count.bit_length() - 1
    owner, within = links >> shift, links & (count - 1)
    place = jnp.where(owner == position, 1, jnp.where(owner == (position ^ 1), 0, 2))
    return jnp.where(links >= 0, place * count + within, -1)


def first_kernel(*refs, count):
    sources, (state_ref, index_ref, lists_ref, operators_ref, inverse_ref) = refs[:count], refs[count : count + 5]
    targets, (sems, block_sems) = refs[count + 5 : -2], refs[-2:]
    right_ref, links_ref, faces_ref, coarse_links_ref, coarse_faces_ref, operators_in_ref = targets
    whole = [pltpu.make_async_copy(sources[i], targets[i], sems.at[i]) for i in range(count - 1)]
    step = inverse_ref.shape[0] // block_sems.shape[0]
    blocks = [
        pltpu.make_async_copy(
            sources[-1].at[i * step : (i + 1) * step], inverse_ref.at[i * step : (i + 1) * step], block_sems.at[i]
        )
        for i in range(block_sems.shape[0])
    ]
    for copy in [whole[0], *blocks[:2], *whole[1:], *blocks[2:]]:
        copy.start()

    tele, column = lax.axis_index("tele"), lax.axis_index("fine")
    tele_size = lax.axis_size("tele")
    def set_up():
        for copy in whole[1:]:
            copy.wait()

        fine_rows = right_ref.shape[0]
        rows = pool_rows(links_ref[...], fine_rows, column * tele_size + tele)
        index = jnp.concatenate([rows.astype(jnp.float32), faces_ref[...].astype(jnp.float32)], axis=0)
        index_ref[...] = index.T.astype(jnp.int32)

        own = coarse_links_ref.shape[0]
        count = own * tele_size
        rows = pool_rows(coarse_links_ref[...], count, column).astype(jnp.float32)
        kinds = coarse_faces_ref[...].astype(jnp.float32)
        lists_ref[...] = jnp.zeros(lists_ref.shape, jnp.float32)
        row = lax.broadcasted_iota(jnp.int32, (count, kinds.shape[1]), 0)
        for part, values in enumerate((rows, kinds)):
            placed = jnp.zeros(row.shape, jnp.float32)
            for c in range(own):
                placed = jnp.where(row == own * tele + c, values[c : c + 1], placed)
            lists_ref[:, part * 6 : part * 6 + 6] = placed

        types, size, _ = operators_in_ref.shape
        unit = lax.broadcasted_iota(jnp.int32, (LANES, size), 0) == lax.broadcasted_iota(jnp.int32, (LANES, size), 1)
        unit = jnp.where(unit, 1.0, 0.0).astype(jnp.bfloat16)
        operators_ref[...] = jnp.zeros(operators_ref.shape, jnp.bfloat16)
        for q in range(types):
            turned = lax.dot_general(
                unit, operators_in_ref[q], (((1,), (1,)), ((), ())), preferred_element_type=jnp.float32
            )
            operators_ref[q * LANES : (q + 1) * LANES, :size] = turned.astype(jnp.bfloat16)

    whole[0].wait()
    lowered = right_ref[...].astype(jnp.bfloat16)
    row = lax.broadcasted_iota(jnp.int32, lowered.shape, 0)
    result = jnp.zeros(lowered.shape, jnp.float32)
    for e in range(inverse_ref.shape[0]):
        if e == 2 * step:
            set_up()
        if e % step == 0:
            blocks[e // step].wait()
        product = lax.dot_general(
            lowered, inverse_ref[e], (((1,), (1,)), ((), ())), preferred_element_type=jnp.float32
        )
        result = jnp.where(row == e, product, result)
    state_ref[...] = result.astype(jnp.bfloat16)


def turn_kernel(*refs):
    out_ref = refs[-1]
    size = out_ref.shape[1]
    unit = lax.broadcasted_iota(jnp.int32, (size, size), 0) == lax.broadcasted_iota(jnp.int32, (size, size), 1)
    unit = jnp.where(unit, 1.0, 0.0).astype(jnp.bfloat16)
    blocks = [(ref, e) for ref in refs[:-1] for e in range(ref.shape[0])]
    for place, (ref, e) in enumerate(blocks):
        turned = lax.dot_general(unit, ref[e], (((1,), (1,)), ((), ())), preferred_element_type=jnp.float32)
        out_ref[place] = turned.astype(jnp.bfloat16)


def sweep(refs, blocks, turned=False):
    prev_ref, own_ref, next_ref, index_ref, operators_ref, pick_ref, lift_ref, right_ref = refs
    states = [prev_ref[...], own_ref[...], next_ref[...]]
    coupled = coupling(states, index_ref[...], operators_ref[...], pick_ref[...], lift_ref[...])
    lowered = (right_ref[...] - coupled).astype(jnp.bfloat16)
    return apply_inverse(blocks, lowered, turned), lowered


def sweep_kernel(*refs, blocks, turned=False):
    result, lowered = sweep(refs[:8], refs[8 : 8 + blocks], turned)
    outs = refs[8 + blocks :]
    outs[0][...] = result.astype(jnp.bfloat16)
    if len(outs) > 1:
        outs[1][...] = result
        outs[2][...] = lowered


def restrict_kernel(
    prev_ref, own_ref, next_ref, index_ref, operators_ref, pick_ref, lift_ref, lowered_ref, target_ref, lists_ref, out_ref
):
    states = [prev_ref[...], own_ref[...], next_ref[...]]
    coupled = coupling(states, index_ref[...], operators_ref[...], pick_ref[...], lift_ref[...])
    residual = lowered_ref[...].astype(jnp.float32) - coupled
    tele_size, rows, dofs = out_ref.shape[0], out_ref.shape[1], residual.shape[1]
    shape = (tele_size * rows, residual.shape[0])
    row = lax.broadcasted_iota(jnp.int32, shape, 0)
    element = (row & (rows - 1)) ^ ((row >> (rows.bit_length() - 1)) * (rows // tele_size))
    member = jnp.where((target_ref[...] & (rows - 1)) == element, 1.0, 0.0).astype(jnp.bfloat16)
    partial = exact_dot(member, residual)
    own = rows // tele_size
    for t in range(tele_size):
        out_ref[t, :, :dofs] = partial[t * rows : (t + 1) * rows]
        for s in range(tele_size):
            out_ref[t, s * own : (s + 1) * own, dofs:] = lists_ref[(s ^ t) * own : ((s ^ t) + 1) * own]


def coarse_first_kernel(*refs, blocks, turned):
    parts_ref, inverses, (restricted_ref, state_ref, index_ref) = refs[0], refs[1 : 1 + blocks], refs[1 + blocks :]
    total = parts_ref[0]
    for t in range(1, parts_ref.shape[0]):
        total = total + parts_ref[t]
    dofs = restricted_ref.shape[1]
    restricted = total[:, :dofs]
    restricted_ref[...] = restricted
    lists = total[:, dofs:].astype(jnp.int32)
    turn = lax.axis_index("tele") * (total.shape[0] // parts_ref.shape[0])
    moved = (lax.broadcasted_iota(jnp.int32, lists.shape, 1) < 6) & (lists >= 0)
    index_ref[...] = jnp.where(moved, lists ^ turn, lists)
    state_ref[...] = apply_inverse(inverses, restricted.astype(jnp.bfloat16), turned).astype(jnp.bfloat16)


def correct_kernel(*refs, blocks):
    coarse, _ = sweep(refs[:8], refs[8 : 8 + blocks], True)
    target_ref, solution_ref, out_ref = refs[8 + blocks :]
    rows, fine = coarse.shape[0], solution_ref.shape[0]
    turn = lax.axis_index("tele") * (rows // lax.axis_size("tele"))
    member = ((target_ref[...] & (rows - 1)) ^ turn) == lax.broadcasted_iota(jnp.int32, (rows, fine), 0)
    added = exact_dot(jnp.where(member, 1.0, 0.0).T.astype(jnp.bfloat16), coarse)
    out_ref[...] = (solution_ref[...] + added).astype(out_ref.dtype)


def run(kernel, outs, *operands, held=(), keep=(), hbm=(), pinned=(), scratch=()):
    count = len(operands)

    def body(*refs):
        kernel(*refs[:count], *refs[count + len(keep) :])

    single = not isinstance(outs, list)
    shapes = [outs] if single else outs
    vmem = pl.BlockSpec(memory_space=pltpu.VMEM)
    moved = sum(o.size * o.dtype.itemsize for o in operands)
    operands = [
        pltpu.with_memory_space_constraint(o, pltpu.HBM if i in hbm else pltpu.VMEM) if i in held or i in hbm else o
        for i, o in enumerate(operands)
    ]
    operands += [pltpu.with_memory_space_constraint(o, pltpu.VMEM) for o in keep]
    result = pl.pallas_call(
        body,
        out_shape=[pltpu.VMEM(s, d) if i in pinned else jax.ShapeDtypeStruct(s, d) for i, (s, d) in enumerate(shapes)],
        in_specs=[pl.BlockSpec(memory_space=pltpu.HBM) if i in hbm else vmem for i in range(len(operands))],
        out_specs=[vmem] * len(shapes),
        scratch_shapes=scratch,
        compiler_params=pltpu.CompilerParams(vmem_limit_bytes=20 << 20),
        cost_estimate=pl.CostEstimate(flops=1 << 32, bytes_accessed=moved, transcendentals=0),
    )(*operands)
    return result[0] if single else result


def shards(
    right_side,
    fine_inverse,
    fine_links,
    fine_faces,
    coarse_inverse,
    coarse_links,
    coarse_faces,
    face_operators,
    agglomerate,
):
    f32, bf16, i32 = jnp.float32, jnp.bfloat16, jnp.int32
    fine_rows, dofs = right_side.shape
    tele_size = lax.axis_size("tele")
    coarse_rows = coarse_inverse.shape[0] * tele_size
    types = face_operators.shape[0]
    spare = -dofs % LANES

    def across(block, bits):
        return lax.ppermute(block, "tele", [(i, i ^ bits) for i in range(tele_size)])

    table = face_table()
    pick, lift = jnp.asarray(table.T.copy(), bf16), jnp.asarray(table, bf16)
    target = agglomerate[None, :]
    operands = (
        right_side,
        fine_links.T,
        fine_faces.T,
        coarse_links,
        coarse_faces,
        face_operators,
        fine_inverse,
    )
    state, fine_index, lists, operators, inverse = run(
        functools.partial(first_kernel, count=len(operands)),
        [
            ((fine_rows, dofs), bf16),
            ((fine_rows, 12), i32),
            ((coarse_rows, spare), f32),
            ((types * LANES, LANES), bf16),
            (fine_inverse.shape, bf16),
        ],
        *operands,
        hbm=range(len(operands)),
        pinned=(3, 4),
        scratch=[pltpu.VMEM(o.shape, o.dtype) for o in operands[:-1]]
        + [pltpu.SemaphoreType.DMA((len(operands),)), pltpu.SemaphoreType.DMA((4,))],
    )
    shared = (operators, pick, lift)

    def halo(block, axis):
        inner, outer = swapped(block, axis)
        return inner, block, outer

    both = ("fine", "tele")
    for cycle in range(CYCLES):
        for sweep in range(SWEEPS):
            if cycle == 0 and sweep == 0:
                continue
            inner, own, outer = halo(state, both)
            if cycle == 0 and sweep == 1:
                sent, inner = lax.optimization_barrier((coarse_inverse, inner))
                near, other = across(sent, 1), across(sent, tele_size - 1)
            if cycle == 0 and sweep == 2:
                near, other, outer = lax.optimization_barrier((near, other, outer))
                far = across(other, 1)
                blocks = (coarse_inverse, near, far, other)
            turned = cycle > 0
            outs = [((fine_rows, dofs), bf16)]
            if sweep == SWEEPS - 1:
                outs += [((fine_rows, dofs), f32), ((fine_rows, dofs), bf16)]
            result = run(
                functools.partial(sweep_kernel, blocks=1, turned=turned),
                outs,
                inner,
                own,
                outer,
                fine_index,
                *shared,
                right_side,
                inverse,
                held=(5, 6, 8),
            )
            state = result[0]
            if cycle == 0 and sweep == SWEEPS - 1:
                inverse = run(turn_kernel, (inverse.shape, bf16), inverse, held=(0,), keep=(state,), pinned=(0,))
        solution, lowered = result[1], result[2]
        parts = run(
            restrict_kernel,
            ((tele_size, coarse_rows, dofs + spare), f32),
            *halo(state, both),
            fine_index,
            *shared,
            lowered,
            target,
            lists,
            held=(5, 6),
            keep=(far,) if cycle == 0 else (),
        )
        parts = lax.all_to_all(parts, "tele", 0, 0, tiled=True)
        restricted, coarse, coarse_index = run(
            functools.partial(coarse_first_kernel, blocks=len(blocks), turned=cycle > 0),
            [((coarse_rows, dofs), f32), ((coarse_rows, dofs), bf16), ((coarse_rows, spare), i32)],
            parts,
            *blocks,
            held=range(1, 1 + len(blocks)),
        )
        if cycle == 0:
            turned_shape = ((coarse_rows, dofs, dofs), bf16)
            held = range(len(blocks))
            blocks = (run(turn_kernel, turned_shape, *blocks, held=held, keep=(coarse,), pinned=(0,)),)
        for sweep in range(SWEEPS - 2):
            coarse = run(
                functools.partial(sweep_kernel, blocks=len(blocks), turned=True),
                [((coarse_rows, dofs), bf16)],
                *halo(coarse, "fine"),
                coarse_index,
                *shared,
                restricted,
                *blocks,
                held=(5, 6, *range(8, 8 + len(blocks))),
            )[0]
        last = cycle == CYCLES - 1
        state = run(
            functools.partial(correct_kernel, blocks=len(blocks)),
            ((fine_rows, dofs), f32 if last else bf16),
            *halo(coarse, "fine"),
            coarse_index,
            *shared,
            restricted,
            *blocks,
            target,
            solution,
            held=(5, 6, *range(8, 8 + len(blocks))),
        )
    return state


def solution(mesh):
    both = P(("fine", "tele"))
    return jax.shard_map(
        shards,
        mesh=mesh,
        in_specs=(both, both, both, both, both, both, both, P(), both),
        out_specs=both,
        check_vma=False,
    )
```
